256 devices in a mesh: det: 16 (over x, y), tm: 16 (over z, core).
Axes of the slice: x: 4, y: 4, z: 8, core: 2. Of those that a mesh axis runs over, the one named last changes fastest.
Arguments:
- tod: float32 [512, 32768], P('det', 'tm'), may hold values from -6 to 6
- pointing: int32 [512, 32768], P('det', 'tm'), may hold values from 0 to 12287
- noise_level: float32 [8, 512], P(None, 'det'), may hold values from 0.5 to 4
- modes: float32 [8, 512, 128], P(None, 'det'), may hold values from -0.75 to 0.75
Outputs:
- filtered: float32 [512, 32768], P('det', 'tm')
- binned: float32 [12288], P(('det', 'tm'))
The draws below stay inside these ranges and needn't reach their ends.
All inputs are finite; a program needn't handle non-finite values.
Results may differ from the reference program's by a relative error of at most 0.00026.
Values sent between devices are 32-bit elements; how exact they have to be, the bound alone decides.
No kernel may reach another device: no remote copies, remote signals or barrier semaphores. Data moves between devices by JAX's collectives and lax.ppermute only.
A program may use at most 64 MiB of HBM per device.

```python
import math
import jax
import jax.numpy as jnp
from jax import lax

MODES = 128
NS = 32768
ND = 512
NB = 8
NPIX = 12288


def draw_pointing(key, part):
    subkeys = jax.random.split(key, 6)
    half_width = jax.random.randint(subkeys[0], (ND, 1), NS // 32, NS // 8 + 1)
    scan_speed = jax.random.randint(subkeys[1], (ND, 1), 1, 4)
    sweep_phase = jax.random.randint(subkeys[2], (ND, 1), 0, 1 << 20) % (4 * half_width)
    drift_rate = jax.random.randint(subkeys[3], (ND, 1), 0, 1 << 20) % (half_width + 1)
    left_draw = jax.random.randint(subkeys[4], (ND, 1), 0, NPIX)
    right_draw = jax.random.randint(subkeys[5], (ND, 1), 0, NPIX)
    start_pixel = (left_draw + right_draw) // 2 - half_width
    detector_index = jnp.arange(ND, dtype=jnp.int32)[:, None]
    start_pixel = jnp.where(detector_index == 0, -half_width, start_pixel)
    start_pixel = jnp.where(detector_index == ND - 1, NPIX - 1 - half_width, start_pixel)
    sample_index = jnp.arange(NS, dtype=jnp.int32)[None, :]
    sweep_period = 4 * half_width
    sweep_offset = jnp.abs((sample_index * scan_speed + sweep_phase) % sweep_period - 2 * half_width)
    drift_offset = sample_index * drift_rate // NS
    return jnp.clip(start_pixel + sweep_offset + drift_offset, 0, NPIX - 1).astype(jnp.int32)


def block_scale(key, dims, cuts, low, high):
    gain, own = 1.0, jax.random.fold_in(key, 6)
    for position, blocks in cuts:
        heights = jnp.exp(jax.random.uniform(jax.random.fold_in(own, position), (blocks,), jnp.float32, low / len(cuts), high / len(cuts)))
        gain = gain * jnp.repeat(heights, dims[position] // blocks).reshape([-1 if axis == position else 1 for axis in range(len(dims))])
    return gain


def gaussian(stream_key, dims, deviation, bound, cuts=(), held_as=jnp.bfloat16):
    loudness = block_scale(stream_key, dims, cuts, -0.22, 0.18) if cuts else 1.0
    entries = jax.random.normal(stream_key, dims, jnp.float32) * deviation * loudness
    return jnp.minimum(jnp.maximum(entries, -bound), bound).astype(held_as)


def setup_inputs(seed: int = 0) -> dict:
    arg_keys = jax.random.split(jax.random.key(seed), 5)
    tod = gaussian(arg_keys[0], (ND, NS), 1.0, 6.0, ((0, 16), (1, 16)), jnp.float32)
    pointing = draw_pointing(jax.random.fold_in(arg_keys[4], 71), 0)
    noise_level = jnp.clip(jnp.exp(math.log(4.0) - 2.0794415 * jax.random.uniform(arg_keys[2], (NB, ND), jnp.float32) ** block_scale(arg_keys[2], (NB, ND), ((1, 16),), -0.2, 0.2)), 0.5, 4.0)
    modes = gaussian(arg_keys[3], (NB, ND, MODES), (ND // 8) ** -0.5, 0.75, ((1, 16),), jnp.float32)
    return dict(tod=tod, pointing=pointing, noise_level=noise_level, modes=modes)


def reference(tod, pointing, noise_level, modes):
    high = lax.Precision.HIGHEST
    width = NS // (2 * NB)
    spectrum = jnp.fft.rfft(tod, axis=1)
    spec_real = jnp.real(spectrum).astype(jnp.float32)
    spec_imag = jnp.imag(spectrum).astype(jnp.float32)
    eye = jnp.eye(MODES, dtype=jnp.float32)
    parts_real = []
    parts_imag = []
    for band in range(NB):
        low = band * width
        high_end = (band + 1) * width if band < NB - 1 else NS // 2 + 1
        count = high_end - low
        inverse = 1.0 / noise_level[band]
        basis = modes[band]
        gram = eye + jnp.dot(basis.T.astype(jnp.float32), (basis * inverse[:, None]).astype(jnp.float32), precision=high, preferred_element_type=jnp.float32)
        weighted = jnp.concatenate([spec_real[:, low:high_end], spec_imag[:, low:high_end]], axis=1) * inverse[:, None]
        proj = jnp.dot(basis.T.astype(jnp.float32), weighted.astype(jnp.float32), precision=high, preferred_element_type=jnp.float32)
        coef = jnp.linalg.solve(gram, proj)
        result = weighted - jnp.dot(basis.astype(jnp.float32), coef.astype(jnp.float32), precision=high, preferred_element_type=jnp.float32) * inverse[:, None]
        parts_real.append(result[:, :count])
        parts_imag.append(result[:, count:])
    full_real = jnp.concatenate(parts_real, axis=1)
    full_imag = jnp.concatenate(parts_imag, axis=1)
    filtered = jnp.fft.irfft(lax.complex(full_real, full_imag), n=NS, axis=1).astype(jnp.float32)
    sums = jax.ops.segment_sum(filtered.reshape(-1), pointing.reshape(-1), num_segments=NPIX)
    hits = jax.ops.segment_sum(jnp.ones((ND * NS,), jnp.float32), pointing.reshape(-1), num_segments=NPIX)
    binned = sums / jnp.sqrt(1.0 + hits)
    return (filtered, binned)
```

```python
import numpy as np
import jax
import jax.numpy as jnp
from jax import lax
from jax.experimental import pallas as pl
from jax.experimental.pallas import tpu as pltpu
from jax.sharding import PartitionSpec as P


HIGHEST = lax.Precision.HIGHEST
NS = 32768
N1 = 128
N2 = 256
BANDS = 8
TPIX = 48
F32 = jnp.float32
BF16 = jnp.bfloat16


def _slots():
    dev, step = np.meshgrid(np.arange(16), np.arange(8), indexing="ij")
    top = (16 * step + dev).reshape(-1)
    bottom = (16 * (step + 8) + dev).reshape(-1)
    return top, bottom


def _forward_tables():
    n1 = np.arange(N1)[:, None]
    k1 = np.arange(64)[None, :]
    angle = 2 * np.pi * (n1 * k1 % N1) / N1
    first = np.concatenate([np.cos(angle), -np.sin(angle)], axis=1)
    first[:, 64] = np.cos(np.pi * np.arange(N1))
    n2 = np.arange(N2)[:, None]
    turn = 2 * np.pi * (n2 * k1) / NS
    keep = np.concatenate([np.cos(turn), np.cos(turn)], axis=1)
    swap = np.concatenate([np.sin(turn), -np.sin(turn)], axis=1)
    edge = 2 * np.pi * 64 * np.arange(N2) / NS
    keep[:, 0] = 1.0
    swap[:, 0] = np.cos(edge)
    keep[:, 64] = -np.sin(edge)
    swap[:, 64] = 0.0
    last = []
    for rows in _slots():
        phase = 2 * np.pi * (rows[:, None] * np.arange(N2)[None, :] % N2) / N2
        last.append(np.concatenate([np.cos(phase), np.sin(phase)], axis=1))
    return [np.asarray(a, np.float32) for a in (first, keep, swap, last[0], last[1])]


def _inverse_tables():
    na = np.arange(N2)
    first = []
    for position, rows in enumerate(_slots()):
        phase = 2 * np.pi * (na[:, None] * rows[None, :] % N2) / N2
        sine = np.sin(phase)
        if position == 0:
            sine[:, 0] = np.where(na % 2 == 0, 1.0, -1.0)
        first.append(np.concatenate([np.cos(phase), sine], axis=1))
    k1 = np.arange(64)[None, :]
    turn = 2 * np.pi * (na[:, None] * k1) / NS
    keep = np.concatenate([2 * np.cos(turn), 2 * np.cos(turn)], axis=1)
    swap = np.concatenate([-2 * np.sin(turn), 2 * np.sin(turn)], axis=1)
    edge = 2 * np.pi * 64 * na / NS
    keep[:, 0] = 2.0
    swap[:, 0] = 0.0
    keep[:, 64] = -2 * np.sin(edge)
    swap[:, 64] = 2 * np.cos(edge)
    nb = np.arange(N1)[:, None]
    angle = 2 * np.pi * (nb * k1 % N1) / N1
    last = np.concatenate([np.cos(angle), -np.sin(angle)], axis=1) / NS
    last[:, 64] = np.cos(np.pi * np.arange(N1)) / NS
    return [np.asarray(a, np.float32) for a in (first[0], first[1], keep, swap, last)]


def _dot(a, b):
    return jnp.dot(a, b, precision=HIGHEST, preferred_element_type=F32)


def _dot_tn(a, b):
    return lax.dot_general(
        a, b, (((0,), (0,)), ((), ())), precision=HIGHEST, preferred_element_type=F32
    )


def _dot_nt(a, b):
    return lax.dot_general(
        a, b, (((1,), (1,)), ((), ())), precision=HIGHEST, preferred_element_type=F32
    )


def _lanes(shape):
    return lax.broadcasted_iota(jnp.int32, shape, 1)


def prep_kernel(where_ref, tod_ref, point_ref, modes_ref, noise_ref, tod_out, v_out, tod_tmp, point_tmp):
    for octet in range(4):
        for r in range(8):
            for h in range(2):
                cols = pl.ds(256 * r + 128 * h, 128)
                rows = pl.ds(256 * h + 64 * octet + r, 8, stride=8)
                tod_tmp[rows, :] = tod_ref[8 * octet : 8 * octet + 8, cols]
                point_tmp[rows, :] = point_ref[8 * octet : 8 * octet + 8, cols].astype(F32)
    for h in range(2):
        cols = slice(128 * h, 128 * h + 128)
        part = slice(256 * h, 256 * h + 256)
        tod_out[:, 0:16, cols] = tod_tmp[part, :].reshape(16, 16, 128)
        tod_out[:, 16:32, cols] = point_tmp[part, :].reshape(16, 16, 128)
    band = where_ref[0]
    root = lax.rsqrt(noise_ref[...])
    eye = lax.broadcasted_iota(jnp.int32, (32, 32), 0) == _lanes((32, 32))
    row_of = lax.broadcasted_iota(jnp.int32, (BANDS, 32), 0)
    for part, which in enumerate((band, BANDS - 1)):
        row = jnp.sum(jnp.where(row_of == which, root, 0.0), axis=0, keepdims=True)
        col = jnp.sum(jnp.where(eye, row, 0.0), axis=1, keepdims=True)
        vee = modes_ref[which] * col
        for dest in range(16):
            v_out[dest, 32 * part : 32 * part + 32, :] = vee


def scales_kernel(where_ref, noise_ref, scale_out):
    pos = where_ref[1]
    root = lax.rsqrt(noise_ref[...])
    noise_ref_lane = _lanes((BANDS, 32))
    flipped = jnp.concatenate([root[BANDS - 1 - j : BANDS - j] for j in range(BANDS)], axis=0)
    for e in range(2):
        mask = noise_ref_lane == 16 * e + pos
        lanes = pl.ds(128 * e, 128)
        up = jnp.sum(jnp.where(mask, root, 0.0), axis=1, keepdims=True)
        down = jnp.sum(jnp.where(mask, flipped, 0.0), axis=1, keepdims=True)
        scale_out[0:8, lanes] = jnp.broadcast_to(up, (8, 128))
        scale_out[8:16, lanes] = jnp.broadcast_to(down, (8, 128))
        scale_out[16:24, lanes] = jnp.broadcast_to(up[7:8], (8, 128))


def _first_scale(scale_ref):
    lane = _lanes((8, 256)) % 128
    row = lax.broadcasted_iota(jnp.int32, (8, 256), 0)
    return jnp.where((lane == 64) & (row == 0), scale_ref[16:24, :], scale_ref[0:8, :])


def forward_kernel(x_ref, scale_ref, first_ref, keep_ref, swap_ref, top_ref, bottom_ref, out_ref):
    lane = _lanes((N2, 128))
    sign = jnp.where(lane < 64, 1.0, -1.0)
    parity = lax.broadcasted_iota(jnp.int32, (N2, 128), 0) % 2
    alternate = jnp.where(lane == 64, jnp.where(parity == 0, -1.0, 1.0), 0.0)
    tops, bottoms, nyquist = [], [], []
    for e in range(2):
        x = x_ref[:, 8 * e : 8 * e + 8, :].reshape(N1, N2)
        s = _dot_tn(x, first_ref[...])
        a = keep_ref[...] * s
        b = swap_ref[...] * pltpu.roll(s, 64, 1)
        both = a + b
        top = jnp.where(lane == 0, a, jnp.where(lane == 64, 0.0, both))
        bottom = jnp.where(lane == 0, b, jnp.where(lane == 64, a, both))
        top_turn = pltpu.roll(top, 64, 1) * sign
        bottom_turn = pltpu.roll(bottom, 64, 1) * sign
        nyquist.append(jnp.sum(top_turn * alternate, axis=0, keepdims=True))
        tops.append(jnp.concatenate([top, top_turn], axis=0))
        bottoms.append(jnp.concatenate([bottom, bottom_turn], axis=0))
    out_top = _dot(top_ref[...], jnp.concatenate(tops, axis=1))
    out_bottom = _dot(bottom_ref[...], jnp.concatenate(bottoms, axis=1))
    nyq = jnp.concatenate(nyquist, axis=1)
    row0 = lax.broadcasted_iota(jnp.int32, (8, 256), 0) == 0
    for d in range(16):
        up = out_top[8 * d : 8 * d + 8]
        if d == 0:
            up = (up + jnp.where(row0, nyq, 0.0)) * _first_scale(scale_ref)
        else:
            up = up * scale_ref[0:8, :]
        down = out_bottom[8 * d : 8 * d + 8] * scale_ref[8:16, :]
        for e in range(2):
            cols = slice(128 * e, 128 * e + 128)
            out_ref[pl.ds(32 * d + e, 8, stride=2), :] = up[:, cols]
            out_ref[pl.ds(32 * d + 16 + e, 8, stride=2), :] = down[:, cols]


def gram_kernel(v_ref, trans_ref, gain_ref, mats_ref):
    parts = []
    for e in range(2):
        row = []
        for part in range(2):
            low = 32 * part + 0
            row.append(v_ref[:, low + 16 * e : low + 16 * e + 16, :].reshape(256, 128))
        parts.append(row)
    eye = lax.broadcasted_iota(jnp.int32, (128, 128), 0) == _lanes((128, 128))
    for part in range(2):
        mats_ref[part] = (
            jnp.where(eye, 1.0, 0.0)
            + _dot_tn(parts[0][part], parts[0][part])
            + _dot_tn(parts[1][part], parts[1][part])
        )
    lane = _lanes((1, 128))
    sub = lax.broadcasted_iota(jnp.int32, (128, 1), 0)

    def step(k, carry):
        here = lane == k
        there = sub == k
        for part in range(2):
            mat = mats_ref[part]
            row = mats_ref[part, pl.ds(k, 1), :]
            pivot = jnp.sum(jnp.where(here, row, 0.0), axis=1, keepdims=True)
            inverse = 1.0 / pivot
            col = jnp.sum(jnp.where(here, mat, 0.0), axis=1, keepdims=True)
            scaled = jnp.where(here, inverse, row * inverse)
            cleared = jnp.where(here, 0.0, mat)
            mats_ref[part] = jnp.where(there, scaled, cleared - col * scaled)
        return carry

    lax.fori_loop(0, 128, step, 0)
    for e in range(2):
        trans_ref[e] = jnp.concatenate([parts[e][0], parts[e][1]], axis=1).T
        gain_ref[e] = jnp.concatenate(
            [_dot(parts[e][0], mats_ref[0]), _dot(parts[e][1], mats_ref[1])], axis=1
        )


def apply_kernel(where_ref, x_ref, trans_ref, gain_ref, out_ref):
    xs = [x_ref[pl.ds(e, 256, stride=2), :] for e in range(2)]
    proj = _dot(trans_ref[0], xs[0]) + _dot(trans_ref[1], xs[1])
    special = (_lanes((256, 128)) == 64) & (where_ref[2] == 0)
    second = lax.broadcasted_iota(jnp.int32, (256, 128), 0) >= 128
    proj = jnp.where(special == second, proj, 0.0)
    for e in range(2):
        out_ref[pl.ds(e, 256, stride=2), :] = xs[e] - _dot(gain_ref[e], proj)


def inverse_kernel(y_ref, scale_ref, top_ref, bottom_ref, keep_ref, swap_ref, last_ref, out_ref):
    lane2 = _lanes((128, 256)) % 128
    sign2 = jnp.where(lane2 < 64, -1.0, 1.0)
    ups, downs = [], []
    for d in range(16):
        up, down = [
            jnp.concatenate(
                [y_ref[pl.ds(32 * d + 16 * half + e, 8, stride=2), :] for e in range(2)], axis=1
            )
            for half in range(2)
        ]
        ups.append(up * (_first_scale(scale_ref) if d == 0 else scale_ref[0:8, :]))
        downs.append(down * scale_ref[8:16, :])
    top = jnp.concatenate(ups, axis=0)
    bottom = jnp.concatenate(downs, axis=0)

    def turned(v):
        halves = [pltpu.roll(v[:, 128 * e : 128 * e + 128], 64, 1) for e in range(2)]
        return jnp.concatenate(halves, axis=1)

    first_row = lax.broadcasted_iota(jnp.int32, (128, 256), 0) == 0
    top_turn = turned(top)
    nyquist = jnp.where(lane2 == 0, 0.5 * top_turn, 0.0)
    top_turn = jnp.where(first_row, nyquist, top_turn * sign2)
    top = jnp.where(first_row & (lane2 == 0), 0.5 * top, top)
    bottom_turn = turned(bottom) * sign2
    a_top = _dot(top_ref[...], jnp.concatenate([top, top_turn], axis=0))
    a_bottom = _dot(bottom_ref[...], jnp.concatenate([bottom, bottom_turn], axis=0))
    lane = _lanes((N2, 128))
    for e in range(2):
        cols = slice(128 * e, 128 * e + 128)
        up, down = a_top[:, cols], a_bottom[:, cols]
        both = up + down
        direct = jnp.where(lane == 0, up, jnp.where(lane == 64, down, both))
        rolled = pltpu.roll(jnp.where(lane == 0, down, both), 64, 1)
        z = keep_ref[...] * direct + swap_ref[...] * rolled
        x = _dot_nt(last_ref[...], z)
        out_ref[:, 8 * e : 8 * e + 8, :] = x.reshape(16, 8, N2)


def split_pixel(point):
    owner = jnp.floor((point + 0.5) * (1.0 / TPIX))
    return owner, point - owner * TPIX


def _one_hot(row, count):
    index = lax.broadcasted_iota(jnp.int32, (count, 256), 0).astype(F32).astype(BF16)
    return index == jnp.broadcast_to(row, (count, 256)).astype(BF16)


def hits_kernel(point_ref, out_ref, owner_ref, inner_ref):
    owner, inner = split_pixel(point_ref[:, 16:32, :].reshape(256, 256))
    owner_ref[...] = owner
    inner_ref[...] = inner
    one = jnp.ones((), BF16)
    zero = jnp.zeros((), BF16)

    def step(r, acc):
        big = jnp.where(_one_hot(owner_ref[pl.ds(r, 1), :], 256), one, zero)
        small = jnp.where(_one_hot(inner_ref[pl.ds(r, 1), :], TPIX), one, zero)
        return acc + lax.dot_general(
            small, big, (((1,), (1,)), ((), ())), preferred_element_type=F32
        )

    out_ref[...] = lax.fori_loop(0, 256, step, jnp.zeros((TPIX, 256), F32), unroll=4)


def sums_kernel(value_ref, owner_ref, inner_ref, hits_ref, out_ref):
    zero = jnp.zeros((), BF16)

    def step(r, acc):
        value = value_ref[pl.ds(r, 1), :]
        high = value.astype(BF16)
        low = (value - high.astype(F32)).astype(BF16)
        big = jnp.where(_one_hot(owner_ref[pl.ds(r, 1), :], 256), jnp.ones((), BF16), zero)
        pick = _one_hot(inner_ref[pl.ds(r, 1), :], TPIX)
        small = jnp.concatenate(
            [
                jnp.where(pick, jnp.broadcast_to(high.astype(F32), (TPIX, 256)).astype(BF16), zero),
                jnp.where(pick, jnp.broadcast_to(low.astype(F32), (TPIX, 256)).astype(BF16), zero),
            ],
            axis=0,
        )
        return acc + lax.dot_general(
            small, big, (((1,), (1,)), ((), ())), preferred_element_type=F32
        )

    acc = lax.fori_loop(0, 256, step, jnp.zeros((2 * TPIX, 256), F32), unroll=4)
    sums = acc[:TPIX] + acc[TPIX:]
    full = jnp.concatenate([sums, hits_ref[...], jnp.zeros((32, 256), F32)], axis=0)
    out_ref[...] = full.T


def spread_kernel(x_ref, out_ref, tmp_ref):
    for h in range(2):
        tmp_ref[256 * h : 256 * h + 256, :] = x_ref[:, 128 * h : 128 * h + 128]
    for octet in range(4):
        for r in range(8):
            for h in range(2):
                rows = pl.ds(256 * h + 64 * octet + r, 8, stride=8)
                cols = pl.ds(256 * r + 128 * h, 128)
                out_ref[8 * octet : 8 * octet + 8, cols] = tmp_ref[rows, :]


def finish_kernel(x_ref, out_ref):
    total = jnp.sum(x_ref[...], axis=0, keepdims=True)
    hits = pltpu.roll(total, 128 - TPIX, 1)
    out_ref[...] = total / jnp.sqrt(1.0 + hits)


VMEM = pl.BlockSpec(memory_space=pltpu.VMEM)
SMEM = pl.BlockSpec(memory_space=pltpu.SMEM)


def call(kernel, outs, scratch=(), smem=0):
    many = isinstance(outs, list)
    shapes = [jax.ShapeDtypeStruct(s, d) for s, d in (outs if many else [outs])]

    def run(*args):
        return pl.pallas_call(
            kernel,
            out_shape=shapes if many else shapes[0],
            in_specs=[SMEM] * smem + [VMEM] * (len(args) - smem),
            out_specs=[VMEM] * len(shapes) if many else VMEM,
            scratch_shapes=list(scratch),
        )(*args)

    return run


def exchange(value, axes):
    return lax.all_to_all(value, axes, split_axis=0, concat_axis=0, tiled=True)


def steps(tod, pointing, noise_level, modes):
    d = lax.axis_index("det")
    t = lax.axis_index("tm")
    forward = [jnp.asarray(a) for a in _forward_tables()]
    inverse = [jnp.asarray(a) for a in _inverse_tables()]
    band = jnp.where(t < BANDS, t, 2 * BANDS - 1 - t)
    where = jnp.stack([band, t, d * 16 + t]).astype(jnp.int32)
    paired = modes.reshape(BANDS, 16, 2, 128).transpose(0, 2, 1, 3).reshape(BANDS, 32, 128)
    paired_noise = noise_level.reshape(BANDS, 16, 2).transpose(0, 2, 1).reshape(BANDS, 32)
    scale = call(scales_kernel, ((24, 256), F32), smem=1)(where, paired_noise)
    send_tod, send_v = call(
        prep_kernel,
        [((16, 32, 256), F32), ((16, 64, 128), F32)],
        scratch=[pltpu.VMEM((512, 128), F32), pltpu.VMEM((512, 128), F32)],
        smem=1,
    )(where, tod, pointing, paired, paired_noise)
    got_tod = exchange(send_tod, "tm")
    got_v = exchange(send_v, "det")
    spectra = call(forward_kernel, ((512, 128), F32))(got_tod, scale, *forward)
    trans, gain = call(
        gram_kernel,
        [((2, 256, 256), F32), ((2, 256, 256), F32)],
        scratch=[pltpu.VMEM((2, 128, 128), F32)],
    )(got_v)
    mixed = exchange(spectra.reshape(256, 2, 128), ("det", "tm")).reshape(512, 128)
    weighted = call(apply_kernel, ((512, 128), F32), smem=1)(where, mixed, trans, gain)
    hits, owner, inner = call(
        hits_kernel, [((TPIX, 256), F32), ((256, 256), F32), ((256, 256), F32)]
    )(got_tod)
    back = exchange(weighted.reshape(256, 2, 128), ("det", "tm")).reshape(512, 128)
    series = call(inverse_kernel, ((16, 16, 256), F32))(back, scale, *inverse)
    got_series = exchange(series, "tm").reshape(256, 256)
    bins = call(sums_kernel, ((256, 128), F32))(series.reshape(256, 256), owner, inner, hits)
    filtered = call(
        spread_kernel, ((32, 2048), F32), scratch=[pltpu.VMEM((512, 128), F32)]
    )(got_series)
    got_bins = exchange(bins, ("det", "tm"))
    binned = call(finish_kernel, ((1, 128), F32))(got_bins)
    return filtered, binned[0, :TPIX]


def solution(mesh):
    placed = (P("det", "tm"), P("det", "tm"), P(None, "det"), P(None, "det", None))
    return jax.shard_map(
        steps,
        mesh=mesh,
        in_specs=placed,
        out_specs=(P("det", "tm"), P(("det", "tm"))),
        check_vma=False,
    )
```

```python
import numpy as np
import jax
import jax.numpy as jnp
from jax import lax
from jax.experimental import pallas as pl
from jax.experimental.pallas import tpu as pltpu
from jax.sharding import PartitionSpec as P


HIGHEST = lax.Precision.HIGHEST
NS = 32768
N1 = 128
N2 = 256
BANDS = 8
TPIX = 48
F32 = jnp.float32
BF16 = jnp.bfloat16


def _slots():
    dev, step = np.meshgrid(np.arange(16), np.arange(8), indexing="ij")
    top = (16 * step + dev).reshape(-1)
    bottom = (16 * (step + 8) + dev).reshape(-1)
    return top, bottom


def _forward_tables():
    n1 = np.arange(N1)[:, None]
    k1 = np.arange(64)[None, :]
    angle = 2 * np.pi * (n1 * k1 % N1) / N1
    first = np.concatenate([np.cos(angle), -np.sin(angle)], axis=1)
    first[:, 64] = np.cos(np.pi * np.arange(N1))
    n2 = np.arange(N2)[:, None]
    turn = 2 * np.pi * (n2 * k1) / NS
    keep = np.concatenate([np.cos(turn), np.cos(turn)], axis=1)
    swap = np.concatenate([np.sin(turn), -np.sin(turn)], axis=1)
    edge = 2 * np.pi * 64 * np.arange(N2) / NS
    keep[:, 0] = 1.0
    swap[:, 0] = np.cos(edge)
    keep[:, 64] = -np.sin(edge)
    swap[:, 64] = 0.0
    last = []
    for rows in _slots():
        phase = 2 * np.pi * (rows[:, None] * np.arange(N2)[None, :] % N2) / N2
        last.append(np.concatenate([np.cos(phase), np.sin(phase)], axis=1))
    return [np.asarray(a, np.float32) for a in (first, keep, swap, last[0], last[1])]


def _inverse_tables():
    na = np.arange(N2)
    first = []
    for position, rows in enumerate(_slots()):
        phase = 2 * np.pi * (na[:, None] * rows[None, :] % N2) / N2
        sine = np.sin(phase)
        if position == 0:
            sine[:, 0] = np.where(na % 2 == 0, 1.0, -1.0)
        first.append(np.concatenate([np.cos(phase), sine], axis=1))
    k1 = np.arange(64)[None, :]
    turn = 2 * np.pi * (na[:, None] * k1) / NS
    keep = np.concatenate([2 * np.cos(turn), 2 * np.cos(turn)], axis=1)
    swap = np.concatenate([-2 * np.sin(turn), 2 * np.sin(turn)], axis=1)
    edge = 2 * np.pi * 64 * na / NS
    keep[:, 0] = 2.0
    swap[:, 0] = 0.0
    keep[:, 64] = -2 * np.sin(edge)
    swap[:, 64] = 2 * np.cos(edge)
    nb = np.arange(N1)[:, None]
    angle = 2 * np.pi * (nb * k1 % N1) / N1
    last = np.concatenate([np.cos(angle), -np.sin(angle)], axis=1) / NS
    last[:, 64] = np.cos(np.pi * np.arange(N1)) / NS
    return [np.asarray(a, np.float32) for a in (first[0], first[1], keep, swap, last)]


def _dot(a, b):
    return jnp.dot(a, b, precision=HIGHEST, preferred_element_type=F32)


def _dot_tn(a, b):
    return lax.dot_general(
        a, b, (((0,), (0,)), ((), ())), precision=HIGHEST, preferred_element_type=F32
    )


def _dot_nt(a, b):
    return lax.dot_general(
        a, b, (((1,), (1,)), ((), ())), precision=HIGHEST, preferred_element_type=F32
    )


def _lanes(shape):
    return lax.broadcasted_iota(jnp.int32, shape, 1)


def _position():
    return lax.axis_index("det"), lax.axis_index("tm")


def basis_kernel(modes_ref, noise_ref, v_out, scale_out, tmp_ref):
    _, pos = _position()
    band = jnp.where(pos < BANDS, pos, 2 * BANDS - 1 - pos)
    root = lax.rsqrt(noise_ref[...])
    eye = lax.broadcasted_iota(jnp.int32, (32, 32), 0) == _lanes((32, 32))
    row_of = lax.broadcasted_iota(jnp.int32, (BANDS, 32), 0)
    for part, which in enumerate((band, BANDS - 1)):
        row = jnp.sum(jnp.where(row_of == which, root, 0.0), axis=0, keepdims=True)
        col = jnp.sum(jnp.where(eye, row, 0.0), axis=1, keepdims=True)
        tmp_ref[part] = modes_ref[which] * col
        for e in range(2):
            vee = tmp_ref[part, pl.ds(e, 16, stride=2), :]
            low = 32 * part + 16 * e
            for dest in range(16):
                v_out[dest, low : low + 16, :] = vee
    flipped = jnp.concatenate([root[BANDS - 1 - j : BANDS - j] for j in range(BANDS)], axis=0)
    for e in range(2):
        mask = _lanes((BANDS, 32)) == 2 * pos + e
        lanes = pl.ds(128 * e, 128)
        up = jnp.sum(jnp.where(mask, root, 0.0), axis=1, keepdims=True)
        down = jnp.sum(jnp.where(mask, flipped, 0.0), axis=1, keepdims=True)
        scale_out[0:8, lanes] = jnp.broadcast_to(up, (8, 128))
        scale_out[8:16, lanes] = jnp.broadcast_to(down, (8, 128))
        scale_out[16:24, lanes] = jnp.broadcast_to(up[7:8], (8, 128))


def prep_kernel(tod_ref, point_ref, tod_out, tod_tmp, point_tmp):
    for octet in range(4):
        for r in range(8):
            for h in range(2):
                cols = pl.ds(256 * r + 128 * h, 128)
                rows = pl.ds(256 * h + 64 * octet + r, 8, stride=8)
                tod_tmp[rows, :] = tod_ref[8 * octet : 8 * octet + 8, cols]
                point_tmp[rows, :] = point_ref[8 * octet : 8 * octet + 8, cols].astype(F32)
    for h in range(2):
        cols = slice(128 * h, 128 * h + 128)
        part = slice(256 * h, 256 * h + 256)
        tod_out[:, 0:16, cols] = tod_tmp[part, :].reshape(16, 16, 128)
        tod_out[:, 16:32, cols] = point_tmp[part, :].reshape(16, 16, 128)


def _first_scale(scale_ref):
    lane = _lanes((8, 256)) % 128
    row = lax.broadcasted_iota(jnp.int32, (8, 256), 0)
    return jnp.where((lane == 64) & (row == 0), scale_ref[16:24, :], scale_ref[0:8, :])


def forward_kernel(x_ref, scale_ref, first_ref, keep_ref, swap_ref, top_ref, bottom_ref, out_ref):
    lane = _lanes((N2, 128))
    sign = jnp.where(lane < 64, 1.0, -1.0)
    parity = lax.broadcasted_iota(jnp.int32, (N2, 128), 0) % 2
    alternate = jnp.where(lane == 64, jnp.where(parity == 0, -1.0, 1.0), 0.0)
    tops, bottoms, nyquist = [], [], []
    for e in range(2):
        x = x_ref[:, 8 * e : 8 * e + 8, :].reshape(N1, N2)
        s = _dot_tn(x, first_ref[...])
        a = keep_ref[...] * s
        b = swap_ref[...] * pltpu.roll(s, 64, 1)
        both = a + b
        top = jnp.where(lane == 0, a, jnp.where(lane == 64, 0.0, both))
        bottom = jnp.where(lane == 0, b, jnp.where(lane == 64, a, both))
        top_turn = pltpu.roll(top, 64, 1) * sign
        bottom_turn = pltpu.roll(bottom, 64, 1) * sign
        nyquist.append(jnp.sum(top_turn * alternate, axis=0, keepdims=True))
        tops.append(jnp.concatenate([top, top_turn], axis=0))
        bottoms.append(jnp.concatenate([bottom, bottom_turn], axis=0))
    out_top = _dot(top_ref[...], jnp.concatenate(tops, axis=1))
    out_bottom = _dot(bottom_ref[...], jnp.concatenate(bottoms, axis=1))
    nyq = jnp.concatenate(nyquist, axis=1)
    row0 = lax.broadcasted_iota(jnp.int32, (8, 256), 0) == 0
    for d in range(16):
        up = out_top[8 * d : 8 * d + 8]
        if d == 0:
            up = (up + jnp.where(row0, nyq, 0.0)) * _first_scale(scale_ref)
        else:
            up = up * scale_ref[0:8, :]
        down = out_bottom[8 * d : 8 * d + 8] * scale_ref[8:16, :]
        for e in range(2):
            cols = slice(128 * e, 128 * e + 128)
            out_ref[pl.ds(32 * d + e, 8, stride=2), :] = up[:, cols]
            out_ref[pl.ds(32 * d + 16 + e, 8, stride=2), :] = down[:, cols]


def _pair_inverse(a, b, c):
    r = 1.0 / (a * c - b * b)
    return c * r, -b * r, a * r


def _quad_inverse(m):
    a0, a1, a2 = _pair_inverse(m[0][0], m[0][1], m[1][1])
    w00 = a0 * m[0][2] + a1 * m[1][2]
    w01 = a0 * m[0][3] + a1 * m[1][3]
    w10 = a1 * m[0][2] + a2 * m[1][2]
    w11 = a1 * m[0][3] + a2 * m[1][3]
    q0, q1, q2 = _pair_inverse(
        m[2][2] - (m[0][2] * w00 + m[1][2] * w10),
        m[2][3] - (m[0][2] * w01 + m[1][2] * w11),
        m[3][3] - (m[0][3] * w01 + m[1][3] * w11),
    )
    x00 = -(w00 * q0 + w01 * q1)
    x01 = -(w00 * q1 + w01 * q2)
    x10 = -(w10 * q0 + w11 * q1)
    x11 = -(w10 * q1 + w11 * q2)
    i00 = a0 - (x00 * w00 + x01 * w01)
    i01 = a1 - (x00 * w10 + x01 * w11)
    i11 = a2 - (x10 * w10 + x11 * w11)
    return [
        [i00, i01, x00, x01],
        [i01, i11, x10, x11],
        [x00, x10, q0, q1],
        [x01, x11, q1, q2],
    ]


def invert_in_place(mats_ref):
    lane = _lanes((128, 128))
    lane8 = _lanes((8, 128))

    def step(panel, carry):
        base = 4 * panel
        within = (lane >= base) & (lane < base + 4)
        index = [jnp.full((128, 128), base + j, jnp.int32) for j in range(4)]
        for part in range(2):
            mat = mats_ref[part]
            rows = [
                jnp.broadcast_to(mats_ref[part, pl.ds(base + j, 1), :], (8, 128)) for j in range(4)
            ]
            pivots = [
                [jnp.take_along_axis(rows[i], index[j][:8], axis=1) for j in range(4)]
                for i in range(4)
            ]
            inverse = _quad_inverse(pivots)
            new = jnp.where(within, 0.0, mat)
            scaled = []
            for i in range(4):
                row = sum(inverse[i][j] * rows[j] for j in range(4))
                for j in range(4):
                    row = jnp.where(lane8 == base + j, inverse[i][j], row)
                scaled.append(row)
                col = jnp.take_along_axis(mat, index[i], axis=1)
                new = new - col * jnp.concatenate([row] * 16, axis=0)
            mats_ref[part] = new
            for i in range(4):
                mats_ref[part, pl.ds(base + i, 1), :] = scaled[i][0:1]
        return carry

    lax.fori_loop(0, 32, step, 0)


def gram_kernel(v_ref, trans_ref, gain_ref, mats_ref):
    parts = []
    for e in range(2):
        row = []
        for part in range(2):
            low = 32 * part + 0
            row.append(v_ref[:, low + 16 * e : low + 16 * e + 16, :].reshape(256, 128))
        parts.append(row)
    eye = lax.broadcasted_iota(jnp.int32, (128, 128), 0) == _lanes((128, 128))
    for part in range(2):
        mats_ref[part] = (
            jnp.where(eye, 1.0, 0.0)
            + _dot_tn(parts[0][part], parts[0][part])
            + _dot_tn(parts[1][part], parts[1][part])
        )
    invert_in_place(mats_ref)
    for e in range(2):
        trans_ref[e] = jnp.concatenate([parts[e][0], parts[e][1]], axis=1).T
        gain_ref[e] = jnp.concatenate(
            [_dot(parts[e][0], mats_ref[0]), _dot(parts[e][1], mats_ref[1])], axis=1
        )


def apply_kernel(x_ref, trans_ref, gain_ref, out_ref):
    xs = [x_ref[pl.ds(e, 256, stride=2), :] for e in range(2)]
    proj = _dot(trans_ref[0], xs[0]) + _dot(trans_ref[1], xs[1])
    dev, pos = _position()
    special = (_lanes((256, 128)) == 64) & (dev * 16 + pos == 0)
    second = lax.broadcasted_iota(jnp.int32, (256, 128), 0) >= 128
    proj = jnp.where(special == second, proj, 0.0)
    for e in range(2):
        out_ref[pl.ds(e, 256, stride=2), :] = xs[e] - _dot(gain_ref[e], proj)


def inverse_kernel(y_ref, scale_ref, top_ref, bottom_ref, keep_ref, swap_ref, last_ref, out_ref):
    lane2 = _lanes((128, 256)) % 128
    sign2 = jnp.where(lane2 < 64, -1.0, 1.0)
    ups, downs = [], []
    for d in range(16):
        up, down = [
            jnp.concatenate(
                [y_ref[pl.ds(32 * d + 16 * half + e, 8, stride=2), :] for e in range(2)], axis=1
            )
            for half in range(2)
        ]
        ups.append(up * (_first_scale(scale_ref) if d == 0 else scale_ref[0:8, :]))
        downs.append(down * scale_ref[8:16, :])
    top = jnp.concatenate(ups, axis=0)
    bottom = jnp.concatenate(downs, axis=0)

    def turned(v):
        halves = [pltpu.roll(v[:, 128 * e : 128 * e + 128], 64, 1) for e in range(2)]
        return jnp.concatenate(halves, axis=1)

    first_row = lax.broadcasted_iota(jnp.int32, (128, 256), 0) == 0
    top_turn = turned(top)
    nyquist = jnp.where(lane2 == 0, 0.5 * top_turn, 0.0)
    top_turn = jnp.where(first_row, nyquist, top_turn * sign2)
    top = jnp.where(first_row & (lane2 == 0), 0.5 * top, top)
    bottom_turn = turned(bottom) * sign2
    a_top = _dot(top_ref[...], jnp.concatenate([top, top_turn], axis=0))
    a_bottom = _dot(bottom_ref[...], jnp.concatenate([bottom, bottom_turn], axis=0))
    lane = _lanes((N2, 128))
    for e in range(2):
        cols = slice(128 * e, 128 * e + 128)
        up, down = a_top[:, cols], a_bottom[:, cols]
        both = up + down
        direct = jnp.where(lane == 0, up, jnp.where(lane == 64, down, both))
        rolled = pltpu.roll(jnp.where(lane == 0, down, both), 64, 1)
        z = keep_ref[...] * direct + swap_ref[...] * rolled
        x = _dot_nt(last_ref[...], z)
        out_ref[:, 8 * e : 8 * e + 8, :] = x.reshape(16, 8, N2)


def _one_hot(row, count):
    index = lax.broadcasted_iota(jnp.int32, (count, 256), 0).astype(F32).astype(BF16)
    return index == jnp.broadcast_to(row, (count, 256)).astype(BF16)


def _pick(mask, row, count):
    return jnp.where(mask, jnp.broadcast_to(row, (count, 256)).astype(BF16), jnp.zeros((), BF16))


def _tally(small, big):
    return lax.dot_general(small, big, (((1,), (1,)), ((), ())), preferred_element_type=F32)


def _tiles(grid_ref, shift, out_fn):
    lane = _lanes((32, 128))
    rows = [grid_ref[pl.ds(r, 32, stride=3), :] for r in range(3)]

    def turned(value, amount):
        amount %= 128
        return pltpu.roll(value, amount, 1) if amount else value

    for j in range(8):
        first, offset = divmod(TPIX * j, 128)
        value = turned(rows[first], shift - offset)
        if offset + TPIX > 128:
            rest = turned(rows[first + 1], shift + 128 - offset)
            value = jnp.where(lane < shift + 128 - offset, value, rest)
        keep = (lane >= shift) & (lane < shift + TPIX)
        out_fn(pl.ds(j, 32, stride=8), jnp.where(keep, value, 0.0))


def hits_kernel(point_ref, out_ref, high_ref, low_ref, grid_ref):
    point = point_ref[:, 16:32, :].reshape(256, 256)
    high = jnp.floor(point * (1.0 / 128))
    high_ref[...] = high
    low_ref[...] = point - 128.0 * high
    one = jnp.ones((1, 256), F32)

    def step(r, acc):
        big = _pick(_one_hot(low_ref[pl.ds(r, 1), :], 128), one, 128)
        small = _pick(_one_hot(high_ref[pl.ds(r, 1), :], 96), one, 96)
        return acc + _tally(small, big)

    grid_ref[...] = lax.fori_loop(0, 256, step, jnp.zeros((96, 128), F32), unroll=32)

    def put(rows, value):
        out_ref[rows, :] = value

    _tiles(grid_ref, TPIX, put)


def sums_kernel(value_ref, high_ref, low_ref, hits_ref, out_ref, grid_ref):
    one = jnp.ones((1, 256), F32)

    def step(r, acc):
        value = value_ref[pl.ds(r, 1), :]
        upper = value.astype(BF16).astype(F32)
        big = _pick(_one_hot(low_ref[pl.ds(r, 1), :], 128), one, 128)
        mask = _one_hot(high_ref[pl.ds(r, 1), :], 96)
        small = jnp.concatenate([_pick(mask, upper, 96), _pick(mask, value - upper, 96)], axis=0)
        return acc + _tally(small, big)

    acc = lax.fori_loop(0, 256, step, jnp.zeros((192, 128), F32), unroll=32)
    grid_ref[...] = acc[:96] + acc[96:]

    def put(rows, value):
        out_ref[rows, :] = value + hits_ref[rows, :]

    _tiles(grid_ref, 0, put)


def spread_kernel(x_ref, out_ref, tmp_ref):
    for h in range(2):
        tmp_ref[256 * h : 256 * h + 256, :] = x_ref[:, 128 * h : 128 * h + 128]
    for octet in range(4):
        for r in range(8):
            for h in range(2):
                rows = pl.ds(256 * h + 64 * octet + r, 8, stride=8)
                cols = pl.ds(256 * r + 128 * h, 128)
                out_ref[8 * octet : 8 * octet + 8, cols] = tmp_ref[rows, :]


def finish_kernel(x_ref, out_ref):
    total = jnp.sum(x_ref[...], axis=0, keepdims=True)
    hits = pltpu.roll(total, 128 - TPIX, 1)
    out_ref[...] = (total / jnp.sqrt(1.0 + hits))[:, :TPIX]


VMEM = pl.BlockSpec(memory_space=pltpu.VMEM)


def call(kernel, outs, scratch=()):
    many = isinstance(outs, list)
    shapes = [jax.ShapeDtypeStruct(s, d) for s, d in (outs if many else [outs])]

    def run(*args):
        return pl.pallas_call(
            kernel,
            out_shape=shapes if many else shapes[0],
            in_specs=[VMEM] * len(args),
            out_specs=[VMEM] * len(shapes) if many else VMEM,
            scratch_shapes=list(scratch),
        )(*args)

    return run


def exchange(value, axes):
    return lax.all_to_all(value, axes, split_axis=0, concat_axis=0, tiled=True)


def steps(tod, pointing, noise_level, modes):
    forward = [jnp.asarray(a) for a in _forward_tables()]
    inverse = [jnp.asarray(a) for a in _inverse_tables()]
    send_v, scale = call(
        basis_kernel,
        [((16, 64, 128), F32), ((24, 256), F32)],
        scratch=[pltpu.VMEM((2, 32, 128), F32)],
    )(modes, noise_level)
    send_tod = call(
        prep_kernel,
        ((16, 32, 256), F32),
        scratch=[pltpu.VMEM((512, 128), F32), pltpu.VMEM((512, 128), F32)],
    )(tod, pointing)
    got_v = exchange(send_v, "det")
    got_tod = exchange(send_tod, "tm")
    spectra = call(forward_kernel, ((512, 128), F32))(got_tod, scale, *forward)
    trans, gain = call(
        gram_kernel,
        [((2, 256, 256), F32), ((2, 256, 256), F32)],
        scratch=[pltpu.VMEM((2, 128, 128), F32)],
    )(got_v)
    mixed = exchange(spectra.reshape(256, 2, 128), ("det", "tm")).reshape(512, 128)
    weighted = call(apply_kernel, ((512, 128), F32))(mixed, trans, gain)
    hits, high, low = call(
        hits_kernel,
        [((256, 128), F32), ((256, 256), F32), ((256, 256), F32)],
        scratch=[pltpu.VMEM((96, 128), F32)],
    )(got_tod)
    back = exchange(weighted.reshape(256, 2, 128), ("det", "tm")).reshape(512, 128)
    series = call(inverse_kernel, ((16, 16, 256), F32))(back, scale, *inverse)
    got_series = exchange(series, "tm").reshape(256, 256)
    bins = call(
        sums_kernel, ((256, 128), F32), scratch=[pltpu.VMEM((96, 128), F32)]
    )(series.reshape(256, 256), high, low, hits)
    filtered = call(
        spread_kernel, ((32, 2048), F32), scratch=[pltpu.VMEM((512, 128), F32)]
    )(got_series)
    got_bins = exchange(bins, ("det", "tm"))
    binned = call(finish_kernel, ((1, TPIX), F32))(got_bins)
    return filtered, binned.reshape(TPIX)


def solution(mesh):
    placed = (P("det", "tm"), P("det", "tm"), P(None, "det"), P(None, "det", None))
    return jax.shard_map(
        steps,
        mesh=mesh,
        in_specs=placed,
        out_specs=(P("det", "tm"), P(("det", "tm"))),
        check_vma=False,
    )
```

```python
import numpy as np
import jax
import jax.numpy as jnp
from jax import lax
from jax.experimental import pallas as pl
from jax.experimental.pallas import tpu as pltpu
from jax.sharding import PartitionSpec as P


HIGHEST = lax.Precision.HIGHEST
NS = 32768
N1 = 128
N2 = 256
BANDS = 8
TPIX = 48
GRANT = 12 << 20
F32 = jnp.float32
BF16 = jnp.bfloat16


def _slots():
    dev, step = np.meshgrid(np.arange(16), np.arange(8), indexing="ij")
    top = (16 * step + dev).reshape(-1)
    bottom = (16 * (step + 8) + dev).reshape(-1)
    return top, bottom


def _forward_tables():
    n1 = np.arange(N1)[:, None]
    k1 = np.arange(64)[None, :]
    angle = 2 * np.pi * (n1 * k1 % N1) / N1
    first = np.concatenate([np.cos(angle), -np.sin(angle)], axis=1)
    first[:, 64] = np.cos(np.pi * np.arange(N1))
    n2 = np.arange(N2)[:, None]
    turn = 2 * np.pi * (n2 * k1) / NS
    keep = np.concatenate([np.cos(turn), np.cos(turn)], axis=1)
    swap = np.concatenate([np.sin(turn), -np.sin(turn)], axis=1)
    edge = 2 * np.pi * 64 * np.arange(N2) / NS
    keep[:, 0] = 1.0
    swap[:, 0] = np.cos(edge)
    keep[:, 64] = -np.sin(edge)
    swap[:, 64] = 0.0
    last = []
    for rows in _slots():
        phase = 2 * np.pi * (rows[:, None] * np.arange(N2)[None, :] % N2) / N2
        last.append(np.concatenate([np.cos(phase), np.sin(phase)], axis=1))
    return [np.asarray(a, np.float32) for a in (first, keep, swap, last[0], last[1])]


def _inverse_tables():
    na = np.arange(N2)
    first = []
    for position, rows in enumerate(_slots()):
        phase = 2 * np.pi * (na[:, None] * rows[None, :] % N2) / N2
        sine = np.sin(phase)
        if position == 0:
            sine[:, 0] = np.where(na % 2 == 0, 1.0, -1.0)
        first.append(np.concatenate([np.cos(phase), sine], axis=1))
    k1 = np.arange(64)[None, :]
    turn = 2 * np.pi * (na[:, None] * k1) / NS
    keep = np.concatenate([2 * np.cos(turn), 2 * np.cos(turn)], axis=1)
    swap = np.concatenate([-2 * np.sin(turn), 2 * np.sin(turn)], axis=1)
    edge = 2 * np.pi * 64 * na / NS
    keep[:, 0] = 2.0
    swap[:, 0] = 0.0
    keep[:, 64] = -2 * np.sin(edge)
    swap[:, 64] = 2 * np.cos(edge)
    nb = np.arange(N1)[:, None]
    angle = 2 * np.pi * (nb * k1 % N1) / N1
    last = np.concatenate([np.cos(angle), -np.sin(angle)], axis=1) / NS
    last[:, 64] = np.cos(np.pi * np.arange(N1)) / NS
    tables = [np.asarray(a, np.float32) for a in (keep, swap)]
    for a in (first[0], first[1], last):
        upper = np.asarray(a, jnp.bfloat16)
        lower = np.asarray(a - upper.astype(np.float64), jnp.bfloat16)
        tables.append(np.stack([upper, lower]))
    return tables


def _dot(a, b):
    return jnp.dot(a, b, precision=HIGHEST, preferred_element_type=F32)


def _dot_tn(a, b):
    return lax.dot_general(
        a, b, (((0,), (0,)), ((), ())), precision=HIGHEST, preferred_element_type=F32
    )


def _parts(a):
    upper = a.astype(BF16)
    return upper, (a - upper.astype(F32)).astype(BF16)


def _dot3(table_ref, b, dims):
    upper, lower = _parts(b)

    def product(x, y):
        return lax.dot_general(x, y, (dims, ((), ())), preferred_element_type=F32)

    return product(table_ref[0], upper) + (
        product(table_ref[0], lower) + product(table_ref[1], upper)
    )


def _lanes(shape):
    return lax.broadcasted_iota(jnp.int32, shape, 1)


def _position():
    return lax.axis_index("det"), lax.axis_index("tm")


def basis_kernel(modes_ref, noise_ref, v_out, scale_out, tmp_ref):
    _, pos = _position()
    band = jnp.where(pos < BANDS, pos, 2 * BANDS - 1 - pos)
    root = lax.rsqrt(noise_ref[...])
    eye = lax.broadcasted_iota(jnp.int32, (32, 32), 0) == _lanes((32, 32))
    row_of = lax.broadcasted_iota(jnp.int32, (BANDS, 32), 0)
    for part, which in enumerate((band, BANDS - 1)):
        row = jnp.sum(jnp.where(row_of == which, root, 0.0), axis=0, keepdims=True)
        col = jnp.sum(jnp.where(eye, row, 0.0), axis=1, keepdims=True)
        tmp_ref[part] = modes_ref[which] * col
        for e in range(2):
            vee = tmp_ref[part, pl.ds(e, 16, stride=2), :]
            low = 32 * part + 16 * e
            for dest in range(16):
                v_out[dest, low : low + 16, :] = vee
    flipped = jnp.concatenate([root[BANDS - 1 - j : BANDS - j] for j in range(BANDS)], axis=0)
    for e in range(2):
        mask = _lanes((BANDS, 32)) == 2 * pos + e
        lanes = pl.ds(128 * e, 128)
        up = jnp.sum(jnp.where(mask, root, 0.0), axis=1, keepdims=True)
        down = jnp.sum(jnp.where(mask, flipped, 0.0), axis=1, keepdims=True)
        scale_out[0:8, lanes] = jnp.broadcast_to(up, (8, 128))
        scale_out[8:16, lanes] = jnp.broadcast_to(down, (8, 128))
        scale_out[16:24, lanes] = jnp.broadcast_to(up[7:8], (8, 128))


def prep_kernel(tod_ref, point_ref, tod_out, tod_tmp, point_tmp):
    for octet in range(4):
        for r in range(8):
            for h in range(2):
                cols = pl.ds(256 * r + 128 * h, 128)
                rows = pl.ds(256 * h + 64 * octet + r, 8, stride=8)
                tod_tmp[rows, :] = tod_ref[8 * octet : 8 * octet + 8, cols]
                point_tmp[rows, :] = point_ref[8 * octet : 8 * octet + 8, cols].astype(F32)
    for h in range(2):
        cols = slice(128 * h, 128 * h + 128)
        part = slice(256 * h, 256 * h + 256)
        tod_out[:, 0:16, cols] = tod_tmp[part, :].reshape(16, 16, 128)
        tod_out[:, 16:32, cols] = point_tmp[part, :].reshape(16, 16, 128)


def _first_scale(scale_ref):
    lane = _lanes((8, 256)) % 128
    row = lax.broadcasted_iota(jnp.int32, (8, 256), 0)
    return jnp.where((lane == 64) & (row == 0), scale_ref[16:24, :], scale_ref[0:8, :])


def forward_kernel(x_ref, scale_ref, first_ref, keep_ref, swap_ref, top_ref, bottom_ref, out_ref):
    lane = _lanes((N2, 128))
    sign = jnp.where(lane < 64, 1.0, -1.0)
    parity = lax.broadcasted_iota(jnp.int32, (N2, 128), 0) % 2
    alternate = jnp.where(lane == 64, jnp.where(parity == 0, -1.0, 1.0), 0.0)
    tops, bottoms, nyquist = [], [], []
    for e in range(2):
        x = x_ref[:, 8 * e : 8 * e + 8, :].reshape(N1, N2)
        s = _dot_tn(x, first_ref[...])
        a = keep_ref[...] * s
        b = swap_ref[...] * pltpu.roll(s, 64, 1)
        both = a + b
        top = jnp.where(lane == 0, a, jnp.where(lane == 64, 0.0, both))
        bottom = jnp.where(lane == 0, b, jnp.where(lane == 64, a, both))
        top_turn = pltpu.roll(top, 64, 1) * sign
        bottom_turn = pltpu.roll(bottom, 64, 1) * sign
        nyquist.append(jnp.sum(top_turn * alternate, axis=0, keepdims=True))
        tops.append(jnp.concatenate([top, top_turn], axis=0))
        bottoms.append(jnp.concatenate([bottom, bottom_turn], axis=0))
    out_top = _dot(top_ref[...], jnp.concatenate(tops, axis=1))
    out_bottom = _dot(bottom_ref[...], jnp.concatenate(bottoms, axis=1))
    nyq = jnp.concatenate(nyquist, axis=1)
    row0 = lax.broadcasted_iota(jnp.int32, (8, 256), 0) == 0
    for d in range(16):
        up = out_top[8 * d : 8 * d + 8]
        if d == 0:
            up = (up + jnp.where(row0, nyq, 0.0)) * _first_scale(scale_ref)
        else:
            up = up * scale_ref[0:8, :]
        down = out_bottom[8 * d : 8 * d + 8] * scale_ref[8:16, :]
        for e in range(2):
            cols = slice(128 * e, 128 * e + 128)
            out_ref[pl.ds(32 * d + e, 8, stride=2), :] = up[:, cols]
            out_ref[pl.ds(32 * d + 16 + e, 8, stride=2), :] = down[:, cols]


def _pair_inverse(a, b, c):
    r = 1.0 / (a * c - b * b)
    return c * r, -b * r, a * r


def _quad_inverse(m):
    a0, a1, a2 = _pair_inverse(m[0][0], m[0][1], m[1][1])
    w00 = a0 * m[0][2] + a1 * m[1][2]
    w01 = a0 * m[0][3] + a1 * m[1][3]
    w10 = a1 * m[0][2] + a2 * m[1][2]
    w11 = a1 * m[0][3] + a2 * m[1][3]
    q0, q1, q2 = _pair_inverse(
        m[2][2] - (m[0][2] * w00 + m[1][2] * w10),
        m[2][3] - (m[0][2] * w01 + m[1][2] * w11),
        m[3][3] - (m[0][3] * w01 + m[1][3] * w11),
    )
    x00 = -(w00 * q0 + w01 * q1)
    x01 = -(w00 * q1 + w01 * q2)
    x10 = -(w10 * q0 + w11 * q1)
    x11 = -(w10 * q1 + w11 * q2)
    i00 = a0 - (x00 * w00 + x01 * w01)
    i01 = a1 - (x00 * w10 + x01 * w11)
    i11 = a2 - (x10 * w10 + x11 * w11)
    return [
        [i00, i01, x00, x01],
        [i01, i11, x10, x11],
        [x00, x10, q0, q1],
        [x01, x11, q1, q2],
    ]


def invert_in_place(mat_refs):
    lane = _lanes((128, 128))
    lane8 = _lanes((8, 128))

    def step(panel, carry):
        base = 4 * panel
        within = (lane >= base) & (lane < base + 4)
        index = [jnp.full((128, 128), base + j, jnp.int32) for j in range(4)]
        mats = [ref[...] for ref in mat_refs]
        rows = [
            [jnp.broadcast_to(ref[pl.ds(base + j, 1), :], (8, 128)) for j in range(4)]
            for ref in mat_refs
        ]
        pivots = [
            [[jnp.take_along_axis(r[i], index[j][:8], axis=1) for j in range(4)] for i in range(4)]
            for r in rows
        ]
        inverses = [_quad_inverse(p) for p in pivots]
        results = []
        for mat, row, inverse in zip(mats, rows, inverses):
            new = jnp.where(within, 0.0, mat)
            scaled = []
            for i in range(4):
                line = sum(inverse[i][j] * row[j] for j in range(4))
                for j in range(4):
                    line = jnp.where(lane8 == base + j, inverse[i][j], line)
                scaled.append(line)
                col = jnp.take_along_axis(mat, index[i], axis=1)
                new = new - col * jnp.concatenate([line] * 16, axis=0)
            results.append((new, scaled))
        for ref, (new, scaled) in zip(mat_refs, results):
            ref[...] = new
            for i in range(4):
                ref[pl.ds(base + i, 1), :] = scaled[i][0:1]
        return carry

    lax.fori_loop(0, 32, step, 0)


def gram_kernel(v_ref, trans_ref, gain_ref, *mat_refs):
    parts = []
    for e in range(2):
        row = []
        for part in range(2):
            low = 32 * part + 0
            row.append(v_ref[:, low + 16 * e : low + 16 * e + 16, :].reshape(256, 128))
        parts.append(row)
    eye = lax.broadcasted_iota(jnp.int32, (128, 128), 0) == _lanes((128, 128))
    for part in range(2):
        mat_refs[part][...] = (
            jnp.where(eye, 1.0, 0.0)
            + _dot_tn(parts[0][part], parts[0][part])
            + _dot_tn(parts[1][part], parts[1][part])
        )
    invert_in_place(mat_refs)
    for e in range(2):
        trans_ref[e] = jnp.concatenate([parts[e][0], parts[e][1]], axis=1).T
        gain_ref[e] = jnp.concatenate(
            [_dot(parts[e][part], mat_refs[part][...]) for part in range(2)], axis=1
        )


def apply_kernel(x_ref, trans_ref, gain_ref, out_ref):
    xs = [x_ref[pl.ds(e, 256, stride=2), :] for e in range(2)]
    proj = _dot(trans_ref[0], xs[0]) + _dot(trans_ref[1], xs[1])
    dev, pos = _position()
    special = (_lanes((256, 128)) == 64) & (dev * 16 + pos == 0)
    second = lax.broadcasted_iota(jnp.int32, (256, 128), 0) >= 128
    proj = jnp.where(special == second, proj, 0.0)
    for e in range(2):
        out_ref[pl.ds(e, 256, stride=2), :] = xs[e] - _dot(gain_ref[e], proj)


def inverse_kernel(y_ref, scale_ref, keep_ref, swap_ref, top_ref, bottom_ref, last_ref, out_ref):
    lane2 = _lanes((128, 256)) % 128
    sign2 = jnp.where(lane2 < 64, -1.0, 1.0)
    ups, downs = [], []
    for d in range(16):
        up, down = [
            jnp.concatenate(
                [y_ref[pl.ds(32 * d + 16 * half + e, 8, stride=2), :] for e in range(2)], axis=1
            )
            for half in range(2)
        ]
        ups.append(up * (_first_scale(scale_ref) if d == 0 else scale_ref[0:8, :]))
        downs.append(down * scale_ref[8:16, :])
    top = jnp.concatenate(ups, axis=0)
    bottom = jnp.concatenate(downs, axis=0)

    def turned(v):
        halves = [pltpu.roll(v[:, 128 * e : 128 * e + 128], 64, 1) for e in range(2)]
        return jnp.concatenate(halves, axis=1)

    first_row = lax.broadcasted_iota(jnp.int32, (128, 256), 0) == 0
    top_turn = turned(top)
    nyquist = jnp.where(lane2 == 0, 0.5 * top_turn, 0.0)
    top_turn = jnp.where(first_row, nyquist, top_turn * sign2)
    top = jnp.where(first_row & (lane2 == 0), 0.5 * top, top)
    bottom_turn = turned(bottom) * sign2
    a_top = _dot3(top_ref, jnp.concatenate([top, top_turn], axis=0), ((1,), (0,)))
    a_bottom = _dot3(bottom_ref, jnp.concatenate([bottom, bottom_turn], axis=0), ((1,), (0,)))
    lane = _lanes((N2, 128))
    for e in range(2):
        cols = slice(128 * e, 128 * e + 128)
        up, down = a_top[:, cols], a_bottom[:, cols]
        both = up + down
        direct = jnp.where(lane == 0, up, jnp.where(lane == 64, down, both))
        rolled = pltpu.roll(jnp.where(lane == 0, down, both), 64, 1)
        z = keep_ref[...] * direct + swap_ref[...] * rolled
        x = _dot3(last_ref, z, ((1,), (1,)))
        out_ref[:, 8 * e : 8 * e + 8, :] = x.reshape(16, 8, N2)


def _one_hot(row, count):
    index = lax.broadcasted_iota(jnp.int32, (count, 256), 0).astype(F32).astype(BF16)
    return index == jnp.broadcast_to(row, (count, 256)).astype(BF16)


def _pick(mask, row, count):
    return jnp.where(mask, jnp.broadcast_to(row, (count, 256)).astype(BF16), jnp.zeros((), BF16))


def _tally(small, big):
    return lax.dot_general(small, big, (((1,), (1,)), ((), ())), preferred_element_type=F32)


def _tiles(grid_ref, shift, out_fn):
    lane = _lanes((32, 128))
    rows = [grid_ref[pl.ds(r, 32, stride=3), :] for r in range(3)]

    def turned(value, amount):
        amount %= 128
        return pltpu.roll(value, amount, 1) if amount else value

    for j in range(8):
        first, offset = divmod(TPIX * j, 128)
        value = turned(rows[first], shift - offset)
        if offset + TPIX > 128:
            rest = turned(rows[first + 1], shift + 128 - offset)
            value = jnp.where(lane < shift + 128 - offset, value, rest)
        keep = (lane >= shift) & (lane < shift + TPIX)
        out_fn(pl.ds(j, 32, stride=8), jnp.where(keep, value, 0.0))


def _split_pixel(point):
    high = jnp.floor(point * (1.0 / 128))
    return high, point - 128.0 * high


def hits_kernel(point_ref, out_ref, high_ref, low_ref, grid_ref):
    high_ref[...], low_ref[...] = _split_pixel(point_ref[...].astype(F32))
    one = jnp.ones((1, 256), F32)

    def step(r, acc):
        for c in range(8):
            cols = slice(256 * c, 256 * c + 256)
            big = _pick(_one_hot(low_ref[pl.ds(r, 1), cols], 128), one, 128)
            small = _pick(_one_hot(high_ref[pl.ds(r, 1), cols], 96), one, 96)
            acc = acc + _tally(small, big)
        return acc

    grid_ref[...] = lax.fori_loop(0, 32, step, jnp.zeros((96, 128), F32), unroll=4)

    def put(rows, value):
        out_ref[rows, :] = value

    _tiles(grid_ref, TPIX, put)


def sums_kernel(value_ref, point_ref, hits_ref, out_ref, high_ref, low_ref, grid_ref):
    high_ref[...], low_ref[...] = _split_pixel(point_ref[:, 16:32, :].reshape(256, 256))
    one = jnp.ones((1, 256), F32)

    def step(r, acc):
        value = value_ref[pl.ds(r, 1), :]
        upper = value.astype(BF16).astype(F32)
        big = _pick(_one_hot(low_ref[pl.ds(r, 1), :], 128), one, 128)
        mask = _one_hot(high_ref[pl.ds(r, 1), :], 96)
        small = jnp.concatenate([_pick(mask, upper, 96), _pick(mask, value - upper, 96)], axis=0)
        return acc + _tally(small, big)

    acc = lax.fori_loop(0, 256, step, jnp.zeros((192, 128), F32), unroll=32)
    grid_ref[...] = acc[:96] + acc[96:]

    def put(rows, value):
        out_ref[rows, :] = value + hits_ref[rows, :]

    _tiles(grid_ref, 0, put)


def spread_kernel(x_ref, out_ref, tmp_ref):
    for h in range(2):
        tmp_ref[256 * h : 256 * h + 256, :] = x_ref[:, 128 * h : 128 * h + 128]
    for octet in range(4):
        for r in range(8):
            for h in range(2):
                rows = pl.ds(256 * h + 64 * octet + r, 8, stride=8)
                cols = pl.ds(256 * r + 128 * h, 128)
                out_ref[8 * octet : 8 * octet + 8, cols] = tmp_ref[rows, :]


def finish_kernel(x_ref, out_ref):
    total = jnp.sum(x_ref[...], axis=0, keepdims=True)
    hits = pltpu.roll(total, 128 - TPIX, 1)
    out_ref[...] = (total / jnp.sqrt(1.0 + hits))[:, :TPIX]


VMEM = pl.BlockSpec(memory_space=pltpu.VMEM)


def call(kernel, outs, scratch=()):
    many = isinstance(outs, list)
    shapes = [jax.ShapeDtypeStruct(s, d) for s, d in (outs if many else [outs])]

    def run(*args):
        return pl.pallas_call(
            kernel,
            out_shape=shapes if many else shapes[0],
            in_specs=[VMEM] * len(args),
            out_specs=[VMEM] * len(shapes) if many else VMEM,
            scratch_shapes=list(scratch),
            compiler_params=pltpu.CompilerParams(vmem_limit_bytes=GRANT),
        )(*args)

    return run


def exchange(value, axes):
    return lax.all_to_all(value, axes, split_axis=0, concat_axis=0, tiled=True)


def steps(tod, pointing, noise_level, modes):
    forward = [jnp.asarray(a) for a in _forward_tables()]
    inverse = [jnp.asarray(a) for a in _inverse_tables()]
    send_v, scale = call(
        basis_kernel,
        [((16, 64, 128), F32), ((24, 256), F32)],
        scratch=[pltpu.VMEM((2, 32, 128), F32)],
    )(modes, noise_level)
    send_tod = call(
        prep_kernel,
        ((16, 32, 256), F32),
        scratch=[pltpu.VMEM((512, 128), F32), pltpu.VMEM((512, 128), F32)],
    )(tod, pointing)
    got_v = exchange(send_v, "det")
    got_tod = exchange(send_tod, "tm")
    spectra = call(forward_kernel, ((512, 128), F32))(got_tod, scale, *forward)
    trans, gain = call(
        gram_kernel,
        [((2, 256, 256), F32), ((2, 256, 256), F32)],
        scratch=[pltpu.VMEM((128, 128), F32), pltpu.VMEM((128, 128), F32)],
    )(got_v)
    mixed = exchange(spectra.reshape(256, 2, 128), ("det", "tm")).reshape(512, 128)
    weighted = call(apply_kernel, ((512, 128), F32))(mixed, trans, gain)
    hits = call(
        hits_kernel,
        ((256, 128), F32),
        scratch=[
            pltpu.VMEM((32, 2048), F32),
            pltpu.VMEM((32, 2048), F32),
            pltpu.VMEM((96, 128), F32),
        ],
    )(pointing)
    back = exchange(weighted.reshape(256, 2, 128), ("det", "tm")).reshape(512, 128)
    series = call(inverse_kernel, ((16, 16, 256), F32))(back, scale, *inverse)
    got_series = exchange(series, "tm").reshape(256, 256)
    bins = call(
        sums_kernel,
        ((256, 128), F32),
        scratch=[
            pltpu.VMEM((256, 256), F32),
            pltpu.VMEM((256, 256), F32),
            pltpu.VMEM((96, 128), F32),
        ],
    )(series.reshape(256, 256), got_tod, hits)
    filtered = call(
        spread_kernel, ((32, 2048), F32), scratch=[pltpu.VMEM((512, 128), F32)]
    )(got_series)
    got_bins = exchange(bins, ("det", "tm"))
    binned = call(finish_kernel, ((1, TPIX), F32))(got_bins)
    return filtered, binned.reshape(TPIX)


def solution(mesh):
    placed = (P("det", "tm"), P("det", "tm"), P(None, "det"), P(None, "det", None))
    return jax.shard_map(
        steps,
        mesh=mesh,
        in_specs=placed,
        out_specs=(P("det", "tm"), P(("det", "tm"))),
        check_vma=False,
    )
```

```python
import numpy as np
import jax
import jax.numpy as jnp
from jax import lax
from jax.experimental import pallas as pl
from jax.experimental.pallas import tpu as pltpu
from jax.sharding import PartitionSpec as P


HIGHEST = lax.Precision.HIGHEST
NS = 32768
N1 = 128
N2 = 256
BANDS = 8
TPIX = 48
GRANT = 12 << 20
F32 = jnp.float32
BF16 = jnp.bfloat16


def _slots():
    dev, step = np.meshgrid(np.arange(16), np.arange(8), indexing="ij")
    top = (16 * step + dev).reshape(-1)
    bottom = (16 * (step + 8) + dev).reshape(-1)
    return top, bottom


def _forward_tables():
    n1 = np.arange(N1)[:, None]
    k1 = np.arange(64)[None, :]
    angle = 2 * np.pi * (n1 * k1 % N1) / N1
    first = np.concatenate([np.cos(angle), -np.sin(angle)], axis=1)
    first[:, 64] = np.cos(np.pi * np.arange(N1))
    n2 = np.arange(N2)[:, None]
    turn = 2 * np.pi * (n2 * k1) / NS
    keep = np.concatenate([np.cos(turn), np.cos(turn)], axis=1)
    swap = np.concatenate([np.sin(turn), -np.sin(turn)], axis=1)
    edge = 2 * np.pi * 64 * np.arange(N2) / NS
    keep[:, 0] = 1.0
    swap[:, 0] = np.cos(edge)
    keep[:, 64] = -np.sin(edge)
    swap[:, 64] = 0.0
    last = []
    for rows in _slots():
        phase = 2 * np.pi * (rows[:, None] * np.arange(N2)[None, :] % N2) / N2
        last.append(np.concatenate([np.cos(phase), np.sin(phase)], axis=1))
    return [np.asarray(a, np.float32) for a in (first, keep, swap, last[0], last[1])]


def _inverse_tables():
    na = np.arange(N2)
    first = []
    for position, rows in enumerate(_slots()):
        phase = 2 * np.pi * (na[:, None] * rows[None, :] % N2) / N2
        sine = np.sin(phase)
        if position == 0:
            sine[:, 0] = np.where(na % 2 == 0, 1.0, -1.0)
        first.append(np.concatenate([np.cos(phase), sine], axis=1))
    k1 = np.arange(64)[None, :]
    turn = 2 * np.pi * (na[:, None] * k1) / NS
    keep = np.concatenate([2 * np.cos(turn), 2 * np.cos(turn)], axis=1)
    swap = np.concatenate([-2 * np.sin(turn), 2 * np.sin(turn)], axis=1)
    edge = 2 * np.pi * 64 * na / NS
    keep[:, 0] = 2.0
    swap[:, 0] = 0.0
    keep[:, 64] = -2 * np.sin(edge)
    swap[:, 64] = 2 * np.cos(edge)
    nb = np.arange(N1)[:, None]
    angle = 2 * np.pi * (nb * k1 % N1) / N1
    last = np.concatenate([np.cos(angle), -np.sin(angle)], axis=1) / NS
    last[:, 64] = np.cos(np.pi * np.arange(N1)) / NS
    tables = [np.asarray(a, np.float32) for a in (keep, swap)]
    for a in (first[0], first[1], last):
        upper = np.asarray(a, jnp.bfloat16)
        lower = np.asarray(a - upper.astype(np.float64), jnp.bfloat16)
        tables.append(np.stack([upper, lower]))
    return tables


def _dot(a, b):
    return jnp.dot(a, b, precision=HIGHEST, preferred_element_type=F32)


def _dot_tn(a, b):
    return lax.dot_general(
        a, b, (((0,), (0,)), ((), ())), precision=HIGHEST, preferred_element_type=F32
    )


def _parts(a):
    upper = a.astype(BF16)
    return upper, (a - upper.astype(F32)).astype(BF16)


def _dot3(table_ref, b, dims):
    upper, lower = _parts(b)

    def product(x, y):
        return lax.dot_general(x, y, (dims, ((), ())), preferred_element_type=F32)

    return product(table_ref[0], upper) + (
        product(table_ref[0], lower) + product(table_ref[1], upper)
    )


def _lanes(shape):
    return lax.broadcasted_iota(jnp.int32, shape, 1)


def _position():
    return lax.axis_index("det"), lax.axis_index("tm")


def basis_kernel(modes_ref, noise_ref, v_out, scale_out, tmp_ref):
    _, pos = _position()
    band = jnp.where(pos < BANDS, pos, 2 * BANDS - 1 - pos)
    root = lax.rsqrt(noise_ref[...])
    eye = lax.broadcasted_iota(jnp.int32, (32, 32), 0) == _lanes((32, 32))
    row_of = lax.broadcasted_iota(jnp.int32, (BANDS, 32), 0)
    for part, which in enumerate((band, BANDS - 1)):
        row = jnp.sum(jnp.where(row_of == which, root, 0.0), axis=0, keepdims=True)
        col = jnp.sum(jnp.where(eye, row, 0.0), axis=1, keepdims=True)
        tmp_ref[part] = modes_ref[which] * col
        for e in range(2):
            vee = tmp_ref[part, pl.ds(e, 16, stride=2), :]
            low = 32 * part + 16 * e
            for dest in range(16):
                v_out[dest, low : low + 16, :] = vee
    flipped = jnp.concatenate([root[BANDS - 1 - j : BANDS - j] for j in range(BANDS)], axis=0)
    for e in range(2):
        mask = _lanes((BANDS, 32)) == 2 * pos + e
        lanes = pl.ds(128 * e, 128)
        up = jnp.sum(jnp.where(mask, root, 0.0), axis=1, keepdims=True)
        down = jnp.sum(jnp.where(mask, flipped, 0.0), axis=1, keepdims=True)
        scale_out[0:8, lanes] = jnp.broadcast_to(up, (8, 128))
        scale_out[8:16, lanes] = jnp.broadcast_to(down, (8, 128))
        scale_out[16:24, lanes] = jnp.broadcast_to(up[7:8], (8, 128))


def prep_kernel(tod_ref, point_ref, tod_out, point_out, tod_in, point_in, tod_tmp, point_tmp, sems):
    copies = []
    for octet in range(4):
        rows = pl.ds(8 * octet, 8)
        pair = [
            pltpu.make_async_copy(src.at[rows], dst.at[rows], sems.at[octet, which])
            for which, (src, dst) in enumerate(((tod_ref, tod_in), (point_ref, point_in)))
        ]
        for copy in pair:
            copy.start()
        copies.append(pair)
    for octet in range(4):
        for copy in copies[octet]:
            copy.wait()
        for r in range(8):
            for h in range(2):
                cols = pl.ds(256 * r + 128 * h, 128)
                rows = pl.ds(256 * h + 64 * octet + r, 8, stride=8)
                tod_tmp[rows, :] = tod_in[8 * octet : 8 * octet + 8, cols]
                point_tmp[rows, :] = point_in[8 * octet : 8 * octet + 8, cols].astype(F32)
    for h in range(2):
        cols = slice(128 * h, 128 * h + 128)
        part = slice(256 * h, 256 * h + 256)
        points = point_tmp[part, :].reshape(16, 2, 8, 128)
        tod_out[:, 0:16, cols] = tod_tmp[part, :].reshape(16, 16, 128)
        tod_out[:, 16:24, cols] = points[:, 0]
        point_out[:, cols] = point_tmp[part, :]


def _first_scale(scale_ref):
    lane = _lanes((8, 256)) % 128
    row = lax.broadcasted_iota(jnp.int32, (8, 256), 0)
    return jnp.where((lane == 64) & (row == 0), scale_ref[16:24, :], scale_ref[0:8, :])


def forward_kernel(x_ref, scale_ref, first_ref, keep_ref, swap_ref, top_ref, bottom_ref, out_ref):
    lane = _lanes((N2, 128))
    sign = jnp.where(lane < 64, 1.0, -1.0)
    parity = lax.broadcasted_iota(jnp.int32, (N2, 128), 0) % 2
    alternate = jnp.where(lane == 64, jnp.where(parity == 0, -1.0, 1.0), 0.0)
    tops, bottoms, nyquist = [], [], []
    for e in range(2):
        x = x_ref[:, 8 * e : 8 * e + 8, :].reshape(N1, N2)
        s = _dot_tn(x, first_ref[...])
        a = keep_ref[...] * s
        b = swap_ref[...] * pltpu.roll(s, 64, 1)
        both = a + b
        top = jnp.where(lane == 0, a, jnp.where(lane == 64, 0.0, both))
        bottom = jnp.where(lane == 0, b, jnp.where(lane == 64, a, both))
        top_turn = pltpu.roll(top, 64, 1) * sign
        bottom_turn = pltpu.roll(bottom, 64, 1) * sign
        nyquist.append(jnp.sum(top_turn * alternate, axis=0, keepdims=True))
        tops.append(jnp.concatenate([top, top_turn], axis=0))
        bottoms.append(jnp.concatenate([bottom, bottom_turn], axis=0))
    out_top = _dot(top_ref[...], jnp.concatenate(tops, axis=1))
    out_bottom = _dot(bottom_ref[...], jnp.concatenate(bottoms, axis=1))
    nyq = jnp.concatenate(nyquist, axis=1)
    row0 = lax.broadcasted_iota(jnp.int32, (8, 256), 0) == 0
    for d in range(16):
        up = out_top[8 * d : 8 * d + 8]
        if d == 0:
            up = (up + jnp.where(row0, nyq, 0.0)) * _first_scale(scale_ref)
        else:
            up = up * scale_ref[0:8, :]
        down = out_bottom[8 * d : 8 * d + 8] * scale_ref[8:16, :]
        for e in range(2):
            cols = slice(128 * e, 128 * e + 128)
            out_ref[pl.ds(32 * d + e, 8, stride=2), :] = up[:, cols]
            out_ref[pl.ds(32 * d + 16 + e, 8, stride=2), :] = down[:, cols]


def _pair_inverse(a, b, c):
    r = 1.0 / (a * c - b * b)
    return c * r, -b * r, a * r


def _quad_inverse(m):
    a0, a1, a2 = _pair_inverse(m[0][0], m[0][1], m[1][1])
    w00 = a0 * m[0][2] + a1 * m[1][2]
    w01 = a0 * m[0][3] + a1 * m[1][3]
    w10 = a1 * m[0][2] + a2 * m[1][2]
    w11 = a1 * m[0][3] + a2 * m[1][3]
    q0, q1, q2 = _pair_inverse(
        m[2][2] - (m[0][2] * w00 + m[1][2] * w10),
        m[2][3] - (m[0][2] * w01 + m[1][2] * w11),
        m[3][3] - (m[0][3] * w01 + m[1][3] * w11),
    )
    x00 = -(w00 * q0 + w01 * q1)
    x01 = -(w00 * q1 + w01 * q2)
    x10 = -(w10 * q0 + w11 * q1)
    x11 = -(w10 * q1 + w11 * q2)
    i00 = a0 - (x00 * w00 + x01 * w01)
    i01 = a1 - (x00 * w10 + x01 * w11)
    i11 = a2 - (x10 * w10 + x11 * w11)
    return [
        [i00, i01, x00, x01],
        [i01, i11, x10, x11],
        [x00, x10, q0, q1],
        [x01, x11, q1, q2],
    ]


def invert_in_place(mat_refs):
    lane = _lanes((128, 128))
    lane8 = _lanes((8, 128))

    def step(panel, carry):
        base = 4 * panel
        within = (lane >= base) & (lane < base + 4)
        index = [jnp.full((128, 128), base + j, jnp.int32) for j in range(4)]
        mats = [ref[...] for ref in mat_refs]
        rows = [
            [jnp.broadcast_to(ref[pl.ds(base + j, 1), :], (8, 128)) for j in range(4)]
            for ref in mat_refs
        ]
        pivots = [
            [[jnp.take_along_axis(r[i], index[j][:8], axis=1) for j in range(4)] for i in range(4)]
            for r in rows
        ]
        inverses = [_quad_inverse(p) for p in pivots]
        results = []
        for mat, row, inverse in zip(mats, rows, inverses):
            new = jnp.where(within, 0.0, mat)
            scaled = []
            for i in range(4):
                line = sum(inverse[i][j] * row[j] for j in range(4))
                for j in range(4):
                    line = jnp.where(lane8 == base + j, inverse[i][j], line)
                scaled.append(line)
                col = jnp.take_along_axis(mat, index[i], axis=1)
                new = new - col * jnp.concatenate([line] * 16, axis=0)
            results.append((new, scaled))
        for ref, (new, scaled) in zip(mat_refs, results):
            ref[...] = new
            for i in range(4):
                ref[pl.ds(base + i, 1), :] = scaled[i][0:1]
        return carry

    lax.fori_loop(0, 32, step, 0)


def gram_kernel(v_ref, trans_ref, gain_ref, *mat_refs):
    parts = []
    for e in range(2):
        row = []
        for part in range(2):
            low = 32 * part + 0
            row.append(v_ref[:, low + 16 * e : low + 16 * e + 16, :].reshape(256, 128))
        parts.append(row)
    eye = lax.broadcasted_iota(jnp.int32, (128, 128), 0) == _lanes((128, 128))
    for part in range(2):
        mat_refs[part][...] = (
            jnp.where(eye, 1.0, 0.0)
            + _dot_tn(parts[0][part], parts[0][part])
            + _dot_tn(parts[1][part], parts[1][part])
        )
    invert_in_place(mat_refs)
    for e in range(2):
        trans_ref[e] = jnp.concatenate([parts[e][0], parts[e][1]], axis=1).T
        gain_ref[e] = jnp.concatenate(
            [_dot(parts[e][part], mat_refs[part][...]) for part in range(2)], axis=1
        )


def apply_kernel(x_ref, trans_ref, gain_ref, out_ref):
    xs = [x_ref[pl.ds(e, 256, stride=2), :] for e in range(2)]
    proj = _dot(trans_ref[0], xs[0]) + _dot(trans_ref[1], xs[1])
    dev, pos = _position()
    special = (_lanes((256, 128)) == 64) & (dev * 16 + pos == 0)
    second = lax.broadcasted_iota(jnp.int32, (256, 128), 0) >= 128
    proj = jnp.where(special == second, proj, 0.0)
    for e in range(2):
        out_ref[pl.ds(e, 256, stride=2), :] = xs[e] - _dot(gain_ref[e], proj)


def inverse_kernel(y_ref, scale_ref, keep_ref, swap_ref, top_ref, bottom_ref, last_ref, out_ref):
    lane2 = _lanes((128, 256)) % 128
    sign2 = jnp.where(lane2 < 64, -1.0, 1.0)
    ups, downs = [], []
    for d in range(16):
        up, down = [
            jnp.concatenate(
                [y_ref[pl.ds(32 * d + 16 * half + e, 8, stride=2), :] for e in range(2)], axis=1
            )
            for half in range(2)
        ]
        ups.append(up * (_first_scale(scale_ref) if d == 0 else scale_ref[0:8, :]))
        downs.append(down * scale_ref[8:16, :])
    top = jnp.concatenate(ups, axis=0)
    bottom = jnp.concatenate(downs, axis=0)

    def turned(v):
        halves = [pltpu.roll(v[:, 128 * e : 128 * e + 128], 64, 1) for e in range(2)]
        return jnp.concatenate(halves, axis=1)

    first_row = lax.broadcasted_iota(jnp.int32, (128, 256), 0) == 0
    top_turn = turned(top)
    nyquist = jnp.where(lane2 == 0, 0.5 * top_turn, 0.0)
    top_turn = jnp.where(first_row, nyquist, top_turn * sign2)
    top = jnp.where(first_row & (lane2 == 0), 0.5 * top, top)
    bottom_turn = turned(bottom) * sign2
    a_top = _dot3(top_ref, jnp.concatenate([top, top_turn], axis=0), ((1,), (0,)))
    a_bottom = _dot3(bottom_ref, jnp.concatenate([bottom, bottom_turn], axis=0), ((1,), (0,)))
    lane = _lanes((N2, 128))
    for e in range(2):
        cols = slice(128 * e, 128 * e + 128)
        up, down = a_top[:, cols], a_bottom[:, cols]
        both = up + down
        direct = jnp.where(lane == 0, up, jnp.where(lane == 64, down, both))
        rolled = pltpu.roll(jnp.where(lane == 0, down, both), 64, 1)
        z = keep_ref[...] * direct + swap_ref[...] * rolled
        x = _dot3(last_ref, z, ((1,), (1,)))
        out_ref[:, 8 * e : 8 * e + 8, :] = x.reshape(16, 8, N2)


def _one_hot(row, count):
    index = lax.broadcasted_iota(jnp.int32, (count, 256), 0).astype(F32).astype(BF16)
    return index == jnp.broadcast_to(row, (count, 256)).astype(BF16)


def _pick(mask, row, count):
    return jnp.where(mask, jnp.broadcast_to(row, (count, 256)).astype(BF16), jnp.zeros((), BF16))


def _tally(small, big):
    return lax.dot_general(small, big, (((1,), (1,)), ((), ())), preferred_element_type=F32)


def _tiles(grid_ref, shift, out_fn):
    lane = _lanes((32, 128))
    rows = [grid_ref[pl.ds(r, 32, stride=3), :] for r in range(3)]

    def turned(value, amount):
        amount %= 128
        return pltpu.roll(value, amount, 1) if amount else value

    for j in range(8):
        first, offset = divmod(TPIX * j, 128)
        value = turned(rows[first], shift - offset)
        if offset + TPIX > 128:
            rest = turned(rows[first + 1], shift + 128 - offset)
            value = jnp.where(lane < shift + 128 - offset, value, rest)
        keep = (lane >= shift) & (lane < shift + TPIX)
        out_fn(pl.ds(j, 32, stride=8), jnp.where(keep, value, 0.0))


def _split_pixel(point):
    high = jnp.floor(point * (1.0 / 128))
    return high, point - 128.0 * high


def hits_kernel(point_ref, out_ref, high_ref, low_ref, grid_ref):
    high_ref[...], low_ref[...] = _split_pixel(point_ref[...])
    one = jnp.ones((1, 256), F32)

    def step(r, acc):
        big = _pick(_one_hot(low_ref[pl.ds(r, 1), :], 128), one, 128)
        small = _pick(_one_hot(high_ref[pl.ds(r, 1), :], 96), one, 96)
        return acc + _tally(small, big)

    grid_ref[...] = lax.fori_loop(0, 256, step, jnp.zeros((96, 128), F32), unroll=32)

    def put(rows, value):
        out_ref[rows, :] = value

    _tiles(grid_ref, TPIX, put)


def _half_sums(value_ref, high_ref, low_ref):
    one = jnp.ones((1, 256), F32)

    def step(r, acc):
        value = value_ref[pl.ds(r, 1), :]
        upper = value.astype(BF16).astype(F32)
        big = _pick(_one_hot(low_ref[pl.ds(r, 1), :], 128), one, 128)
        mask = _one_hot(high_ref[pl.ds(r, 1), :], 96)
        small = jnp.concatenate([_pick(mask, upper, 96), _pick(mask, value - upper, 96)], axis=0)
        return acc + _tally(small, big)

    acc = lax.fori_loop(0, 128, step, jnp.zeros((192, 128), F32), unroll=32)
    return acc[:96] + acc[96:]


def early_kernel(series_ref, got_ref, point_ref, out_ref, high_out, low_out, value_ref, high_ref, low_ref):
    high_ref[...], low_ref[...] = _split_pixel(got_ref[:, 16:24, :].reshape(128, 256))
    value_ref[...] = series_ref[:, 0:8, :].reshape(128, 256)
    own = point_ref[...].reshape(16, 16, 256)[:, 8:16, :].reshape(128, 256)
    high_out[...], low_out[...] = _split_pixel(own)
    out_ref[...] = _half_sums(value_ref, high_ref, low_ref)


def late_kernel(series_ref, high_ref, low_ref, early_ref, hits_ref, out_ref, value_ref, grid_ref):
    value_ref[...] = series_ref[:, 8:16, :].reshape(128, 256)
    grid_ref[...] = early_ref[...] + _half_sums(value_ref, high_ref, low_ref)

    def put(rows, value):
        out_ref[rows, :] = value + hits_ref[rows, :]

    _tiles(grid_ref, 0, put)


def spread_kernel(x_ref, out_ref, tmp_ref):
    for h in range(2):
        tmp_ref[256 * h : 256 * h + 256, :] = x_ref[:, 128 * h : 128 * h + 128]
    for octet in range(4):
        for r in range(8):
            for h in range(2):
                rows = pl.ds(256 * h + 64 * octet + r, 8, stride=8)
                cols = pl.ds(256 * r + 128 * h, 128)
                out_ref[8 * octet : 8 * octet + 8, cols] = tmp_ref[rows, :]


def finish_kernel(x_ref, out_ref):
    total = jnp.sum(x_ref[...], axis=0, keepdims=True)
    hits = pltpu.roll(total, 128 - TPIX, 1)
    out_ref[...] = (total / jnp.sqrt(1.0 + hits))[:, :TPIX]


VMEM = pl.BlockSpec(memory_space=pltpu.VMEM)
HBM = pl.BlockSpec(memory_space=pl.ANY)


def call(kernel, outs, scratch=(), space=VMEM):
    many = isinstance(outs, list)
    shapes = [jax.ShapeDtypeStruct(s, d) for s, d in (outs if many else [outs])]

    def run(*args):
        return pl.pallas_call(
            kernel,
            out_shape=shapes if many else shapes[0],
            in_specs=[space] * len(args),
            out_specs=[VMEM] * len(shapes) if many else VMEM,
            scratch_shapes=list(scratch),
            compiler_params=pltpu.CompilerParams(vmem_limit_bytes=GRANT),
        )(*args)

    return run


def exchange(value, axes):
    return lax.all_to_all(value, axes, split_axis=0, concat_axis=0, tiled=True)


def steps(tod, pointing, noise_level, modes):
    forward = [jnp.asarray(a) for a in _forward_tables()]
    inverse = [jnp.asarray(a) for a in _inverse_tables()]
    send_v, scale = call(
        basis_kernel,
        [((16, 64, 128), F32), ((24, 256), F32)],
        scratch=[pltpu.VMEM((2, 32, 128), F32)],
    )(modes, noise_level)
    send_tod, local_point = call(
        prep_kernel,
        [((16, 24, 256), F32), ((256, 256), F32)],
        scratch=[
            pltpu.VMEM((32, 2048), F32),
            pltpu.VMEM((32, 2048), jnp.int32),
            pltpu.VMEM((512, 128), F32),
            pltpu.VMEM((512, 128), F32),
            pltpu.SemaphoreType.DMA((4, 2)),
        ],
        space=HBM,
    )(tod, pointing)
    got_v = exchange(send_v, "det")
    got_tod = exchange(send_tod, "tm")
    spectra = call(forward_kernel, ((512, 128), F32))(got_tod, scale, *forward)
    trans, gain = call(
        gram_kernel,
        [((2, 256, 256), F32), ((2, 256, 256), F32)],
        scratch=[pltpu.VMEM((128, 128), F32), pltpu.VMEM((128, 128), F32)],
    )(got_v)
    mixed = exchange(spectra.reshape(256, 2, 128), ("det", "tm")).reshape(512, 128)
    weighted = call(apply_kernel, ((512, 128), F32))(mixed, trans, gain)
    hits = call(
        hits_kernel,
        ((256, 128), F32),
        scratch=[
            pltpu.VMEM((256, 256), F32),
            pltpu.VMEM((256, 256), F32),
            pltpu.VMEM((96, 128), F32),
        ],
    )(local_point)
    back = exchange(weighted.reshape(256, 2, 128), ("det", "tm")).reshape(512, 128)
    series = call(inverse_kernel, ((16, 16, 256), F32))(back, scale, *inverse)
    got_series = exchange(series, "tm")
    half = pltpu.VMEM((128, 256), F32)
    early, high, low = call(
        early_kernel,
        [((96, 128), F32), ((128, 256), F32), ((128, 256), F32)],
        scratch=[half, half, half],
    )(series, got_tod, local_point)
    bins = call(
        late_kernel, ((256, 128), F32), scratch=[half, pltpu.VMEM((96, 128), F32)]
    )(got_series, high, low, early, hits)
    filtered = call(
        spread_kernel, ((32, 2048), F32), scratch=[pltpu.VMEM((512, 128), F32)]
    )(got_series.reshape(256, 256))
    got_bins = exchange(bins, ("det", "tm"))
    binned = call(finish_kernel, ((1, TPIX), F32))(got_bins)
    return filtered, binned.reshape(TPIX)


def solution(mesh):
    placed = (P("det", "tm"), P("det", "tm"), P(None, "det"), P(None, "det", None))
    return jax.shard_map(
        steps,
        mesh=mesh,
        in_specs=placed,
        out_specs=(P("det", "tm"), P(("det", "tm"))),
        check_vma=False,
    )
```

```python
import numpy as np
import jax
import jax.numpy as jnp
from jax import lax
from jax.experimental import pallas as pl
from jax.experimental.pallas import tpu as pltpu
from jax.sharding import PartitionSpec as P


HIGHEST = lax.Precision.HIGHEST
NS = 32768
N1 = 128
N2 = 256
BANDS = 8
TPIX = 48
GRANT = 12 << 20
WIDE_GRANT = 60 << 20
F32 = jnp.float32
BF16 = jnp.bfloat16


def _slots():
    dev, step = np.meshgrid(np.arange(16), np.arange(8), indexing="ij")
    top = (16 * step + dev).reshape(-1)
    bottom = (16 * (step + 8) + dev).reshape(-1)
    return top, bottom


def _forward_tables():
    n1 = np.arange(N1)[:, None]
    k1 = np.arange(64)[None, :]
    angle = 2 * np.pi * (n1 * k1 % N1) / N1
    first = np.concatenate([np.cos(angle), -np.sin(angle)], axis=1)
    first[:, 64] = np.cos(np.pi * np.arange(N1))
    n2 = np.arange(N2)[:, None]
    turn = 2 * np.pi * (n2 * k1) / NS
    keep = np.concatenate([np.cos(turn), np.cos(turn)], axis=1)
    swap = np.concatenate([np.sin(turn), -np.sin(turn)], axis=1)
    edge = 2 * np.pi * 64 * np.arange(N2) / NS
    keep[:, 0] = 1.0
    swap[:, 0] = np.cos(edge)
    keep[:, 64] = -np.sin(edge)
    swap[:, 64] = 0.0
    last = []
    for rows in _slots():
        phase = 2 * np.pi * (rows[:, None] * np.arange(N2)[None, :] % N2) / N2
        last.append(np.concatenate([np.cos(phase), np.sin(phase)], axis=1))
    return [np.asarray(a, np.float32) for a in (first, keep, swap, last[0], last[1])]


def _inverse_tables():
    na = np.arange(N2)
    first = []
    for position, rows in enumerate(_slots()):
        phase = 2 * np.pi * (na[:, None] * rows[None, :] % N2) / N2
        sine = np.sin(phase)
        if position == 0:
            sine[:, 0] = np.where(na % 2 == 0, 1.0, -1.0)
        first.append(np.concatenate([np.cos(phase), sine], axis=1))
    k1 = np.arange(64)[None, :]
    turn = 2 * np.pi * (na[:, None] * k1) / NS
    keep = np.concatenate([2 * np.cos(turn), 2 * np.cos(turn)], axis=1)
    swap = np.concatenate([-2 * np.sin(turn), 2 * np.sin(turn)], axis=1)
    edge = 2 * np.pi * 64 * na / NS
    keep[:, 0] = 2.0
    swap[:, 0] = 0.0
    keep[:, 64] = -2 * np.sin(edge)
    swap[:, 64] = 2 * np.cos(edge)
    nb = np.arange(N1)[:, None]
    angle = 2 * np.pi * (nb * k1 % N1) / N1
    last = np.concatenate([np.cos(angle), -np.sin(angle)], axis=1) / NS
    last[:, 64] = np.cos(np.pi * np.arange(N1)) / NS
    tables = [np.asarray(a, np.float32) for a in (keep, swap)]
    for a in (first[0], first[1], last):
        upper = np.asarray(a, jnp.bfloat16)
        lower = np.asarray(a - upper.astype(np.float64), jnp.bfloat16)
        tables.append(np.stack([upper, lower]))
    return tables


def _dot(a, b):
    return jnp.dot(a, b, precision=HIGHEST, preferred_element_type=F32)


def _dot_tn(a, b):
    return lax.dot_general(
        a, b, (((0,), (0,)), ((), ())), precision=HIGHEST, preferred_element_type=F32
    )


def _parts(a):
    upper = a.astype(BF16)
    return upper, (a - upper.astype(F32)).astype(BF16)


def _dot3(table_ref, b, dims):
    upper, lower = _parts(b)

    def product(x, y):
        return lax.dot_general(x, y, (dims, ((), ())), preferred_element_type=F32)

    return product(table_ref[0], upper) + (
        product(table_ref[0], lower) + product(table_ref[1], upper)
    )


def _lanes(shape):
    return lax.broadcasted_iota(jnp.int32, shape, 1)


def _position():
    return lax.axis_index("det"), lax.axis_index("tm")


def basis_kernel(modes_ref, noise_ref, v_out, scale_out, tmp_ref):
    _, pos = _position()
    band = jnp.where(pos < BANDS, pos, 2 * BANDS - 1 - pos)
    root = lax.rsqrt(noise_ref[...])
    eye = lax.broadcasted_iota(jnp.int32, (32, 32), 0) == _lanes((32, 32))
    row_of = lax.broadcasted_iota(jnp.int32, (BANDS, 32), 0)
    for part, which in enumerate((band, BANDS - 1)):
        row = jnp.sum(jnp.where(row_of == which, root, 0.0), axis=0, keepdims=True)
        col = jnp.sum(jnp.where(eye, row, 0.0), axis=1, keepdims=True)
        tmp_ref[part] = modes_ref[which] * col
        for e in range(2):
            vee = tmp_ref[part, pl.ds(e, 16, stride=2), :]
            low = 32 * part + 16 * e
            for dest in range(16):
                v_out[dest, low : low + 16, :] = vee
    flipped = jnp.concatenate([root[BANDS - 1 - j : BANDS - j] for j in range(BANDS)], axis=0)
    for e in range(2):
        mask = _lanes((BANDS, 32)) == 2 * pos + e
        lanes = pl.ds(128 * e, 128)
        up = jnp.sum(jnp.where(mask, root, 0.0), axis=1, keepdims=True)
        down = jnp.sum(jnp.where(mask, flipped, 0.0), axis=1, keepdims=True)
        scale_out[0:8, lanes] = jnp.broadcast_to(up, (8, 128))
        scale_out[8:16, lanes] = jnp.broadcast_to(down, (8, 128))
        scale_out[16:24, lanes] = jnp.broadcast_to(up[7:8], (8, 128))


def _spread_rows(source_ref, tmp_ref, octet):
    for r in range(8):
        for h in range(2):
            cols = pl.ds(256 * r + 128 * h, 128)
            rows = pl.ds(256 * h + 64 * octet + r, 8, stride=8)
            tmp_ref[rows, :] = source_ref[8 * octet : 8 * octet + 8, cols].astype(F32)


def prep_kernel(tod_ref, tod_out, tod_in, tod_tmp, sems):
    copies = []
    for octet in range(4):
        rows = pl.ds(8 * octet, 8)
        copy = pltpu.make_async_copy(tod_ref.at[rows], tod_in.at[rows], sems.at[octet])
        copy.start()
        copies.append(copy)
    for octet in range(4):
        copies[octet].wait()
        _spread_rows(tod_in, tod_tmp, octet)
        for h in range(2):
            cols = slice(128 * h, 128 * h + 128)
            low = 256 * h + 64 * octet
            tod_out[64 * octet : 64 * octet + 64, cols] = tod_tmp[low : low + 64, :]


def _first_scale(scale_ref):
    lane = _lanes((8, 256)) % 128
    row = lax.broadcasted_iota(jnp.int32, (8, 256), 0)
    return jnp.where((lane == 64) & (row == 0), scale_ref[16:24, :], scale_ref[0:8, :])


def forward_kernel(x_ref, scale_ref, first_ref, keep_ref, swap_ref, top_ref, bottom_ref, out_ref):
    lane = _lanes((N2, 128))
    sign = jnp.where(lane < 64, 1.0, -1.0)
    parity = lax.broadcasted_iota(jnp.int32, (N2, 128), 0) % 2
    alternate = jnp.where(lane == 64, jnp.where(parity == 0, -1.0, 1.0), 0.0)
    tops, bottoms, nyquist = [], [], []
    for e in range(2):
        x = x_ref[:, 8 * e : 8 * e + 8, :].reshape(N1, N2)
        s = _dot_tn(x, first_ref[...])
        a = keep_ref[...] * s
        b = swap_ref[...] * pltpu.roll(s, 64, 1)
        both = a + b
        top = jnp.where(lane == 0, a, jnp.where(lane == 64, 0.0, both))
        bottom = jnp.where(lane == 0, b, jnp.where(lane == 64, a, both))
        top_turn = pltpu.roll(top, 64, 1) * sign
        bottom_turn = pltpu.roll(bottom, 64, 1) * sign
        nyquist.append(jnp.sum(top_turn * alternate, axis=0, keepdims=True))
        tops.append(jnp.concatenate([top, top_turn], axis=0))
        bottoms.append(jnp.concatenate([bottom, bottom_turn], axis=0))
    out_top = _dot(top_ref[...], jnp.concatenate(tops, axis=1))
    out_bottom = _dot(bottom_ref[...], jnp.concatenate(bottoms, axis=1))
    nyq = jnp.concatenate(nyquist, axis=1)
    row0 = lax.broadcasted_iota(jnp.int32, (8, 256), 0) == 0
    for d in range(16):
        up = out_top[8 * d : 8 * d + 8]
        if d == 0:
            up = (up + jnp.where(row0, nyq, 0.0)) * _first_scale(scale_ref)
        else:
            up = up * scale_ref[0:8, :]
        down = out_bottom[8 * d : 8 * d + 8] * scale_ref[8:16, :]
        for e in range(2):
            cols = slice(128 * e, 128 * e + 128)
            out_ref[pl.ds(32 * d + e, 8, stride=2), :] = up[:, cols]
            out_ref[pl.ds(32 * d + 16 + e, 8, stride=2), :] = down[:, cols]


def _pair_inverse(a, b, c):
    r = 1.0 / (a * c - b * b)
    return c * r, -b * r, a * r


def _quad_inverse(m):
    a0, a1, a2 = _pair_inverse(m[0][0], m[0][1], m[1][1])
    w00 = a0 * m[0][2] + a1 * m[1][2]
    w01 = a0 * m[0][3] + a1 * m[1][3]
    w10 = a1 * m[0][2] + a2 * m[1][2]
    w11 = a1 * m[0][3] + a2 * m[1][3]
    q0, q1, q2 = _pair_inverse(
        m[2][2] - (m[0][2] * w00 + m[1][2] * w10),
        m[2][3] - (m[0][2] * w01 + m[1][2] * w11),
        m[3][3] - (m[0][3] * w01 + m[1][3] * w11),
    )
    x00 = -(w00 * q0 + w01 * q1)
    x01 = -(w00 * q1 + w01 * q2)
    x10 = -(w10 * q0 + w11 * q1)
    x11 = -(w10 * q1 + w11 * q2)
    i00 = a0 - (x00 * w00 + x01 * w01)
    i01 = a1 - (x00 * w10 + x01 * w11)
    i11 = a2 - (x10 * w10 + x11 * w11)
    return [
        [i00, i01, x00, x01],
        [i01, i11, x10, x11],
        [x00, x10, q0, q1],
        [x01, x11, q1, q2],
    ]


def invert_in_place(mat_refs):
    lane = _lanes((128, 128))
    lane8 = _lanes((8, 128))

    def step(panel, carry):
        base = 4 * panel
        within = (lane >= base) & (lane < base + 4)
        index = [jnp.full((128, 128), base + j, jnp.int32) for j in range(4)]
        mats = [ref[...] for ref in mat_refs]
        rows = [
            [jnp.broadcast_to(ref[pl.ds(base + j, 1), :], (8, 128)) for j in range(4)]
            for ref in mat_refs
        ]
        pivots = [
            [[jnp.take_along_axis(r[i], index[j][:8], axis=1) for j in range(4)] for i in range(4)]
            for r in rows
        ]
        inverses = [_quad_inverse(p) for p in pivots]
        results = []
        for mat, row, inverse in zip(mats, rows, inverses):
            new = jnp.where(within, 0.0, mat)
            scaled = []
            for i in range(4):
                line = sum(inverse[i][j] * row[j] for j in range(4))
                for j in range(4):
                    line = jnp.where(lane8 == base + j, inverse[i][j], line)
                scaled.append(line)
                col = jnp.take_along_axis(mat, index[i], axis=1)
                new = new - col * jnp.concatenate([line] * 16, axis=0)
            results.append((new, scaled))
        for ref, (new, scaled) in zip(mat_refs, results):
            ref[...] = new
            for i in range(4):
                ref[pl.ds(base + i, 1), :] = scaled[i][0:1]
        return carry

    lax.fori_loop(0, 32, step, 0)


def gram_kernel(v_ref, trans_ref, gain_ref, *mat_refs):
    parts = []
    for e in range(2):
        row = []
        for part in range(2):
            low = 32 * part + 0
            row.append(v_ref[:, low + 16 * e : low + 16 * e + 16, :].reshape(256, 128))
        parts.append(row)
    eye = lax.broadcasted_iota(jnp.int32, (128, 128), 0) == _lanes((128, 128))
    for part in range(2):
        mat_refs[part][...] = (
            jnp.where(eye, 1.0, 0.0)
            + _dot_tn(parts[0][part], parts[0][part])
            + _dot_tn(parts[1][part], parts[1][part])
        )
    invert_in_place(mat_refs)
    for e in range(2):
        trans_ref[e] = jnp.concatenate([parts[e][0], parts[e][1]], axis=1).T
        gain_ref[e] = jnp.concatenate(
            [_dot(parts[e][part], mat_refs[part][...]) for part in range(2)], axis=1
        )


def apply_kernel(x_ref, trans_ref, gain_ref, out_ref):
    xs = [x_ref[pl.ds(e, 256, stride=2), :] for e in range(2)]
    proj = _dot(trans_ref[0], xs[0]) + _dot(trans_ref[1], xs[1])
    dev, pos = _position()
    special = (_lanes((256, 128)) == 64) & (dev * 16 + pos == 0)
    second = lax.broadcasted_iota(jnp.int32, (256, 128), 0) >= 128
    proj = jnp.where(special == second, proj, 0.0)
    for e in range(2):
        out_ref[pl.ds(e, 256, stride=2), :] = xs[e] - _dot(gain_ref[e], proj)


def inverse_kernel(y_ref, scale_ref, keep_ref, swap_ref, top_ref, bottom_ref, last_ref, out_ref):
    lane2 = _lanes((128, 256)) % 128
    sign2 = jnp.where(lane2 < 64, -1.0, 1.0)
    ups, downs = [], []
    for d in range(16):
        up, down = [
            jnp.concatenate(
                [y_ref[pl.ds(32 * d + 16 * half + e, 8, stride=2), :] for e in range(2)], axis=1
            )
            for half in range(2)
        ]
        ups.append(up * (_first_scale(scale_ref) if d == 0 else scale_ref[0:8, :]))
        downs.append(down * scale_ref[8:16, :])
    top = jnp.concatenate(ups, axis=0)
    bottom = jnp.concatenate(downs, axis=0)

    def turned(v):
        halves = [pltpu.roll(v[:, 128 * e : 128 * e + 128], 64, 1) for e in range(2)]
        return jnp.concatenate(halves, axis=1)

    first_row = lax.broadcasted_iota(jnp.int32, (128, 256), 0) == 0
    top_turn = turned(top)
    nyquist = jnp.where(lane2 == 0, 0.5 * top_turn, 0.0)
    top_turn = jnp.where(first_row, nyquist, top_turn * sign2)
    top = jnp.where(first_row & (lane2 == 0), 0.5 * top, top)
    bottom_turn = turned(bottom) * sign2
    a_top = _dot3(top_ref, jnp.concatenate([top, top_turn], axis=0), ((1,), (0,)))
    a_bottom = _dot3(bottom_ref, jnp.concatenate([bottom, bottom_turn], axis=0), ((1,), (0,)))
    lane = _lanes((N2, 128))
    for e in range(2):
        cols = slice(128 * e, 128 * e + 128)
        up, down = a_top[:, cols], a_bottom[:, cols]
        both = up + down
        direct = jnp.where(lane == 0, up, jnp.where(lane == 64, down, both))
        rolled = pltpu.roll(jnp.where(lane == 0, down, both), 64, 1)
        z = keep_ref[...] * direct + swap_ref[...] * rolled
        x = _dot3(last_ref, z, ((1,), (1,)))
        out_ref[:, 8 * e : 8 * e + 8, :] = x.reshape(16, 8, N2)


def _one_hot(row, count):
    index = lax.broadcasted_iota(jnp.int32, (count, 256), 0).astype(F32).astype(BF16)
    return index == jnp.broadcast_to(row, (count, 256)).astype(BF16)


def _pick(mask, row, count):
    return jnp.where(mask, jnp.broadcast_to(row, (count, 256)).astype(BF16), jnp.zeros((), BF16))


def _tally(small, big):
    return lax.dot_general(small, big, (((1,), (1,)), ((), ())), preferred_element_type=F32)


def _tiles(grid_ref, shift, out_fn):
    lane = _lanes((32, 128))
    rows = [grid_ref[pl.ds(r, 32, stride=3), :] for r in range(3)]

    def turned(value, amount):
        amount %= 128
        return pltpu.roll(value, amount, 1) if amount else value

    for j in range(8):
        first, offset = divmod(TPIX * j, 128)
        value = turned(rows[first], shift - offset)
        if offset + TPIX > 128:
            rest = turned(rows[first + 1], shift + 128 - offset)
            value = jnp.where(lane < shift + 128 - offset, value, rest)
        keep = (lane >= shift) & (lane < shift + TPIX)
        out_fn(pl.ds(j, 32, stride=8), jnp.where(keep, value, 0.0))


def _split_pixel(point):
    high = jnp.floor(point * (1.0 / 128))
    return high, point - 128.0 * high


def hits_kernel(point_ref, out_ref, high_ref, low_ref, tmp_ref, grid_ref):
    for octet in range(4):
        _spread_rows(point_ref, tmp_ref, octet)
    for h in range(2):
        cols = slice(128 * h, 128 * h + 128)
        high, low = _split_pixel(tmp_ref[256 * h : 256 * h + 256, :])
        high_ref[:, cols] = high
        low_ref[:, cols] = low
    one = jnp.ones((1, 256), F32)

    def step(r, acc):
        big = _pick(_one_hot(low_ref[pl.ds(r, 1), :], 128), one, 128)
        small = _pick(_one_hot(high_ref[pl.ds(r, 1), :], 96), one, 96)
        return acc + _tally(small, big)

    grid_ref[...] = lax.fori_loop(0, 256, step, jnp.zeros((96, 128), F32), unroll=32)

    def put(rows, value):
        out_ref[rows, :] = value

    _tiles(grid_ref, TPIX, put)


def sums_kernel(value_ref, high_ref, low_ref, hits_ref, out_ref, grid_ref):
    one = jnp.ones((1, 256), F32)

    def step(r, acc):
        value = value_ref[pl.ds(r, 1), :]
        upper = value.astype(BF16).astype(F32)
        big = _pick(_one_hot(low_ref[pl.ds(r, 1), :], 128), one, 128)
        mask = _one_hot(high_ref[pl.ds(r, 1), :], 96)
        small = jnp.concatenate([_pick(mask, upper, 96), _pick(mask, value - upper, 96)], axis=0)
        return acc + _tally(small, big)

    acc = lax.fori_loop(0, 256, step, jnp.zeros((192, 128), F32), unroll=64)
    grid_ref[...] = acc[:96] + acc[96:]

    def put(rows, value):
        out_ref[rows, :] = value + hits_ref[rows, :]

    _tiles(grid_ref, 0, put)


def spread_kernel(x_ref, out_ref, tmp_ref):
    for h in range(2):
        tmp_ref[256 * h : 256 * h + 256, :] = x_ref[:, 128 * h : 128 * h + 128]
    for octet in range(4):
        for r in range(8):
            for h in range(2):
                rows = pl.ds(256 * h + 64 * octet + r, 8, stride=8)
                cols = pl.ds(256 * r + 128 * h, 128)
                out_ref[8 * octet : 8 * octet + 8, cols] = tmp_ref[rows, :]


def finish_kernel(x_ref, out_ref):
    total = jnp.sum(x_ref[...], axis=0, keepdims=True)
    hits = pltpu.roll(total, 128 - TPIX, 1)
    out_ref[...] = (total / jnp.sqrt(1.0 + hits))[:, :TPIX]


VMEM = pl.BlockSpec(memory_space=pltpu.VMEM)
HBM = pl.BlockSpec(memory_space=pltpu.HBM)


def call(kernel, outs, scratch=(), space=VMEM, grant=GRANT):
    many = isinstance(outs, list)
    shapes = [jax.ShapeDtypeStruct(s, d) for s, d in (outs if many else [outs])]

    def run(*args):
        return pl.pallas_call(
            kernel,
            out_shape=shapes if many else shapes[0],
            in_specs=[space] * len(args),
            out_specs=[VMEM] * len(shapes) if many else VMEM,
            scratch_shapes=list(scratch),
            compiler_params=pltpu.CompilerParams(vmem_limit_bytes=grant),
        )(*args)

    return run


def exchange(value, axes):
    return lax.all_to_all(value, axes, split_axis=0, concat_axis=0, tiled=True)


def steps(tod, pointing, noise_level, modes):
    forward = [jnp.asarray(a) for a in _forward_tables()]
    inverse = [jnp.asarray(a) for a in _inverse_tables()]
    send_v, scale = call(
        basis_kernel,
        [((16, 64, 128), F32), ((24, 256), F32)],
        scratch=[pltpu.VMEM((2, 32, 128), F32)],
    )(modes, noise_level)
    send_tod = call(
        prep_kernel,
        ((256, 256), F32),
        scratch=[
            pltpu.VMEM((32, 2048), F32),
            pltpu.VMEM((512, 128), F32),
            pltpu.SemaphoreType.DMA((4,)),
        ],
        space=HBM,
        grant=WIDE_GRANT,
    )(tod).reshape(16, 16, 256)
    got_v = exchange(send_v, "det")
    got_tod = exchange(send_tod, "tm")
    spectra = call(forward_kernel, ((512, 128), F32))(got_tod, scale, *forward)
    trans, gain = call(
        gram_kernel,
        [((2, 256, 256), F32), ((2, 256, 256), F32)],
        scratch=[pltpu.VMEM((128, 128), F32), pltpu.VMEM((128, 128), F32)],
    )(got_v)
    mixed = exchange(spectra.reshape(256, 2, 128), ("det", "tm")).reshape(512, 128)
    weighted = call(apply_kernel, ((512, 128), F32))(mixed, trans, gain)
    hits, high, low = call(
        hits_kernel,
        [((256, 128), F32), ((256, 256), F32), ((256, 256), F32)],
        scratch=[pltpu.VMEM((512, 128), F32), pltpu.VMEM((96, 128), F32)],
    )(pointing)
    back = exchange(weighted.reshape(256, 2, 128), ("det", "tm")).reshape(512, 128)
    series = call(inverse_kernel, ((16, 16, 256), F32))(back, scale, *inverse)
    got_series = exchange(series, "tm").reshape(256, 256)
    bins = call(
        sums_kernel, ((256, 128), F32), scratch=[pltpu.VMEM((96, 128), F32)]
    )(got_series, high, low, hits)
    filtered = call(
        spread_kernel, ((32, 2048), F32), scratch=[pltpu.VMEM((512, 128), F32)]
    )(got_series)
    got_bins = exchange(bins, ("det", "tm"))
    binned = call(finish_kernel, ((1, TPIX), F32))(got_bins)
    return filtered, binned.reshape(TPIX)


def solution(mesh):
    placed = (P("det", "tm"), P("det", "tm"), P(None, "det"), P(None, "det", None))
    return jax.shard_map(
        steps,
        mesh=mesh,
        in_specs=placed,
        out_specs=(P("det", "tm"), P(("det", "tm"))),
        check_vma=False,
    )
```

```python
import functools

import numpy as np
import jax
import jax.numpy as jnp
from jax import lax
from jax.experimental import pallas as pl
from jax.experimental.pallas import tpu as pltpu
from jax.sharding import PartitionSpec as P


HIGHEST = lax.Precision.HIGHEST
NS = 32768
N1 = 128
N2 = 256
BANDS = 8
TPIX = 48
GRANT = 12 << 20
WIDE_GRANT = 60 << 20
F32 = jnp.float32
BF16 = jnp.bfloat16


def _slots():
    dev, step = np.meshgrid(np.arange(16), np.arange(8), indexing="ij")
    top = (16 * step + dev).reshape(-1)
    bottom = (16 * (step + 8) + dev).reshape(-1)
    return top, bottom


def _forward_tables():
    n1 = np.arange(N1)[:, None]
    k1 = np.arange(64)[None, :]
    angle = 2 * np.pi * (n1 * k1 % N1) / N1
    first = np.concatenate([np.cos(angle), -np.sin(angle)], axis=1)
    first[:, 64] = np.cos(np.pi * np.arange(N1))
    n2 = np.arange(N2)[:, None]
    turn = 2 * np.pi * (n2 * k1) / NS
    keep = np.concatenate([np.cos(turn), np.cos(turn)], axis=1)
    swap = np.concatenate([np.sin(turn), -np.sin(turn)], axis=1)
    edge = 2 * np.pi * 64 * np.arange(N2) / NS
    keep[:, 0] = 1.0
    swap[:, 0] = np.cos(edge)
    keep[:, 64] = -np.sin(edge)
    swap[:, 64] = 0.0
    last = []
    for rows in _slots():
        phase = 2 * np.pi * (rows[:, None] * np.arange(N2)[None, :] % N2) / N2
        last.append(np.concatenate([np.cos(phase), np.sin(phase)], axis=1))
    return [np.asarray(a, np.float32) for a in (first, keep, swap, last[0], last[1])]


def _inverse_tables():
    na = np.arange(N2)
    first = []
    for position, rows in enumerate(_slots()):
        phase = 2 * np.pi * (na[:, None] * rows[None, :] % N2) / N2
        sine = np.sin(phase)
        if position == 0:
            sine[:, 0] = np.where(na % 2 == 0, 1.0, -1.0)
        first.append(np.concatenate([np.cos(phase), sine], axis=1))
    k1 = np.arange(64)[None, :]
    turn = 2 * np.pi * (na[:, None] * k1) / NS
    keep = np.concatenate([2 * np.cos(turn), 2 * np.cos(turn)], axis=1)
    swap = np.concatenate([-2 * np.sin(turn), 2 * np.sin(turn)], axis=1)
    edge = 2 * np.pi * 64 * na / NS
    keep[:, 0] = 2.0
    swap[:, 0] = 0.0
    keep[:, 64] = -2 * np.sin(edge)
    swap[:, 64] = 2 * np.cos(edge)
    nb = np.arange(N1)[:, None]
    angle = 2 * np.pi * (nb * k1 % N1) / N1
    last = np.concatenate([np.cos(angle), -np.sin(angle)], axis=1) / NS
    last[:, 64] = np.cos(np.pi * np.arange(N1)) / NS
    tables = [np.asarray(a, np.float32) for a in (keep, swap)]
    for a in (first[0], first[1], last):
        upper = np.asarray(a, jnp.bfloat16)
        lower = np.asarray(a - upper.astype(np.float64), jnp.bfloat16)
        tables.append(np.stack([upper, lower]))
    return tables


def _dot(a, b):
    return jnp.dot(a, b, precision=HIGHEST, preferred_element_type=F32)


def _dot_tn(a, b):
    return lax.dot_general(
        a, b, (((0,), (0,)), ((), ())), precision=HIGHEST, preferred_element_type=F32
    )


def _parts(a):
    upper = a.astype(BF16)
    return upper, (a - upper.astype(F32)).astype(BF16)


def _dot3(table_ref, b, dims):
    upper, lower = _parts(b)

    def product(x, y):
        return lax.dot_general(x, y, (dims, ((), ())), preferred_element_type=F32)

    return product(table_ref[0], upper) + (
        product(table_ref[0], lower) + product(table_ref[1], upper)
    )


def _lanes(shape):
    return lax.broadcasted_iota(jnp.int32, shape, 1)


def _position():
    return lax.axis_index("det"), lax.axis_index("tm")


def basis_kernel(modes_ref, noise_ref, v_out, scale_out, tmp_ref):
    _, pos = _position()
    band = jnp.where(pos < BANDS, pos, 2 * BANDS - 1 - pos)
    root = lax.rsqrt(noise_ref[...])
    eye = lax.broadcasted_iota(jnp.int32, (32, 32), 0) == _lanes((32, 32))
    row_of = lax.broadcasted_iota(jnp.int32, (BANDS, 32), 0)
    for part, which in enumerate((band, BANDS - 1)):
        row = jnp.sum(jnp.where(row_of == which, root, 0.0), axis=0, keepdims=True)
        col = jnp.sum(jnp.where(eye, row, 0.0), axis=1, keepdims=True)
        tmp_ref[part] = modes_ref[which] * col
        for e in range(2):
            low = 32 * part + 16 * e
            v_out[0, low : low + 16, :] = tmp_ref[part, pl.ds(e, 16, stride=2), :]
    flipped = jnp.concatenate([root[BANDS - 1 - j : BANDS - j] for j in range(BANDS)], axis=0)
    for e in range(2):
        mask = _lanes((BANDS, 32)) == 2 * pos + e
        lanes = pl.ds(128 * e, 128)
        up = jnp.sum(jnp.where(mask, root, 0.0), axis=1, keepdims=True)
        down = jnp.sum(jnp.where(mask, flipped, 0.0), axis=1, keepdims=True)
        scale_out[0:8, lanes] = jnp.broadcast_to(up, (8, 128))
        scale_out[8:16, lanes] = jnp.broadcast_to(down, (8, 128))
        scale_out[16:24, lanes] = jnp.broadcast_to(up[7:8], (8, 128))


def _spread_rows(source_ref, tmp_ref, octet):
    for r in range(8):
        for h in range(2):
            cols = pl.ds(256 * r + 128 * h, 128)
            rows = pl.ds(256 * h + 64 * octet + r, 8, stride=8)
            tmp_ref[rows, :] = source_ref[8 * octet : 8 * octet + 8, cols].astype(F32)


def prep_kernel(tod_ref, tod_out, tod_in, tod_tmp, sems):
    copies = []
    for octet in range(4):
        rows = pl.ds(8 * octet, 8)
        copy = pltpu.make_async_copy(tod_ref.at[rows], tod_in.at[rows], sems.at[octet])
        copy.start()
        copies.append(copy)
    for octet in range(4):
        copies[octet].wait()
        _spread_rows(tod_in, tod_tmp, octet)
        for h in range(2):
            cols = slice(128 * h, 128 * h + 128)
            low = 256 * h + 64 * octet
            tod_out[64 * octet : 64 * octet + 64, cols] = tod_tmp[low : low + 64, :]


def _first_scale(scale_ref):
    lane = _lanes((8, 256)) % 128
    row = lax.broadcasted_iota(jnp.int32, (8, 256), 0)
    return jnp.where((lane == 64) & (row == 0), scale_ref[16:24, :], scale_ref[0:8, :])


def forward_kernel(x_ref, scale_ref, first_ref, keep_ref, swap_ref, top_ref, bottom_ref, out_ref):
    lane = _lanes((N2, 128))
    sign = jnp.where(lane < 64, 1.0, -1.0)
    parity = lax.broadcasted_iota(jnp.int32, (N2, 128), 0) % 2
    alternate = jnp.where(lane == 64, jnp.where(parity == 0, -1.0, 1.0), 0.0)
    tops, bottoms, nyquist = [], [], []
    for e in range(2):
        x = x_ref[:, 8 * e : 8 * e + 8, :].reshape(N1, N2)
        s = _dot_tn(x, first_ref[...])
        a = keep_ref[...] * s
        b = swap_ref[...] * pltpu.roll(s, 64, 1)
        both = a + b
        top = jnp.where(lane == 0, a, jnp.where(lane == 64, 0.0, both))
        bottom = jnp.where(lane == 0, b, jnp.where(lane == 64, a, both))
        top_turn = pltpu.roll(top, 64, 1) * sign
        bottom_turn = pltpu.roll(bottom, 64, 1) * sign
        nyquist.append(jnp.sum(top_turn * alternate, axis=0, keepdims=True))
        tops.append(jnp.concatenate([top, top_turn], axis=0))
        bottoms.append(jnp.concatenate([bottom, bottom_turn], axis=0))
    out_top = _dot(top_ref[...], jnp.concatenate(tops, axis=1))
    out_bottom = _dot(bottom_ref[...], jnp.concatenate(bottoms, axis=1))
    nyq = jnp.concatenate(nyquist, axis=1)
    row0 = lax.broadcasted_iota(jnp.int32, (8, 256), 0) == 0
    for d in range(16):
        up = out_top[8 * d : 8 * d + 8]
        if d == 0:
            up = (up + jnp.where(row0, nyq, 0.0)) * _first_scale(scale_ref)
        else:
            up = up * scale_ref[0:8, :]
        down = out_bottom[8 * d : 8 * d + 8] * scale_ref[8:16, :]
        for e in range(2):
            cols = slice(128 * e, 128 * e + 128)
            out_ref[pl.ds(32 * d + e, 8, stride=2), :] = up[:, cols]
            out_ref[pl.ds(32 * d + 16 + e, 8, stride=2), :] = down[:, cols]


def _pair_inverse(a, b, c):
    r = 1.0 / (a * c - b * b)
    return c * r, -b * r, a * r


def _quad_inverse(m):
    a0, a1, a2 = _pair_inverse(m[0][0], m[0][1], m[1][1])
    w00 = a0 * m[0][2] + a1 * m[1][2]
    w01 = a0 * m[0][3] + a1 * m[1][3]
    w10 = a1 * m[0][2] + a2 * m[1][2]
    w11 = a1 * m[0][3] + a2 * m[1][3]
    q0, q1, q2 = _pair_inverse(
        m[2][2] - (m[0][2] * w00 + m[1][2] * w10),
        m[2][3] - (m[0][2] * w01 + m[1][2] * w11),
        m[3][3] - (m[0][3] * w01 + m[1][3] * w11),
    )
    x00 = -(w00 * q0 + w01 * q1)
    x01 = -(w00 * q1 + w01 * q2)
    x10 = -(w10 * q0 + w11 * q1)
    x11 = -(w10 * q1 + w11 * q2)
    i00 = a0 - (x00 * w00 + x01 * w01)
    i01 = a1 - (x00 * w10 + x01 * w11)
    i11 = a2 - (x10 * w10 + x11 * w11)
    return [
        [i00, i01, x00, x01],
        [i01, i11, x10, x11],
        [x00, x10, q0, q1],
        [x01, x11, q1, q2],
    ]


def invert_in_place(mat_refs):
    lane = _lanes((128, 128))
    lane8 = _lanes((8, 128))

    def step(panel, carry):
        base = 4 * panel
        within = (lane >= base) & (lane < base + 4)
        index = [jnp.full((128, 128), base + j, jnp.int32) for j in range(4)]
        mats = [ref[...] for ref in mat_refs]
        rows = [
            [jnp.broadcast_to(ref[pl.ds(base + j, 1), :], (8, 128)) for j in range(4)]
            for ref in mat_refs
        ]
        pivots = [
            [[jnp.take_along_axis(r[i], index[j][:8], axis=1) for j in range(4)] for i in range(4)]
            for r in rows
        ]
        inverses = [_quad_inverse(p) for p in pivots]
        results = []
        for mat, row, inverse in zip(mats, rows, inverses):
            new = jnp.where(within, 0.0, mat)
            scaled = []
            for i in range(4):
                line = sum(inverse[i][j] * row[j] for j in range(4))
                for j in range(4):
                    line = jnp.where(lane8 == base + j, inverse[i][j], line)
                scaled.append(line)
                col = jnp.take_along_axis(mat, index[i], axis=1)
                new = new - col * jnp.concatenate([line] * 16, axis=0)
            results.append((new, scaled))
        for ref, (new, scaled) in zip(mat_refs, results):
            ref[...] = new
            for i in range(4):
                ref[pl.ds(base + i, 1), :] = scaled[i][0:1]
        return carry

    lax.fori_loop(0, 32, step, 0)


def gram_kernel(near_ref, far_ref, trans_ref, gain_ref, vees_ref, *mat_refs):
    dev, _ = _position()
    for j in range(16):
        source = near_ref if j < 8 else far_ref
        rows = pl.ds(pl.multiple_of((dev ^ j) * 16, 16), 16)
        for e in range(2):
            for part in range(2):
                low = 32 * part + 16 * e
                vees_ref[e, rows, 128 * part : 128 * part + 128] = source[j % 8, low : low + 16, :]
    parts = [[vees_ref[e, :, 128 * part : 128 * part + 128] for part in range(2)] for e in range(2)]
    eye = lax.broadcasted_iota(jnp.int32, (128, 128), 0) == _lanes((128, 128))
    for part in range(2):
        mat_refs[part][...] = (
            jnp.where(eye, 1.0, 0.0)
            + _dot_tn(parts[0][part], parts[0][part])
            + _dot_tn(parts[1][part], parts[1][part])
        )
    invert_in_place(mat_refs)
    for e in range(2):
        trans_ref[e] = jnp.concatenate([parts[e][0], parts[e][1]], axis=1).T
        gain_ref[e] = jnp.concatenate(
            [_dot(parts[e][part], mat_refs[part][...]) for part in range(2)], axis=1
        )


def apply_kernel(x_ref, trans_ref, gain_ref, out_ref):
    xs = [x_ref[pl.ds(e, 256, stride=2), :] for e in range(2)]
    proj = _dot(trans_ref[0], xs[0]) + _dot(trans_ref[1], xs[1])
    dev, pos = _position()
    special = (_lanes((256, 128)) == 64) & (dev * 16 + pos == 0)
    second = lax.broadcasted_iota(jnp.int32, (256, 128), 0) >= 128
    proj = jnp.where(special == second, proj, 0.0)
    for e in range(2):
        out_ref[pl.ds(e, 256, stride=2), :] = xs[e] - _dot(gain_ref[e], proj)


def inverse_kernel(y_ref, scale_ref, keep_ref, swap_ref, top_ref, bottom_ref, last_ref, out_ref):
    lane2 = _lanes((128, 256)) % 128
    sign2 = jnp.where(lane2 < 64, -1.0, 1.0)
    ups, downs = [], []
    for d in range(16):
        up, down = [
            jnp.concatenate(
                [y_ref[pl.ds(32 * d + 16 * half + e, 8, stride=2), :] for e in range(2)], axis=1
            )
            for half in range(2)
        ]
        ups.append(up * (_first_scale(scale_ref) if d == 0 else scale_ref[0:8, :]))
        downs.append(down * scale_ref[8:16, :])
    top = jnp.concatenate(ups, axis=0)
    bottom = jnp.concatenate(downs, axis=0)

    def turned(v):
        halves = [pltpu.roll(v[:, 128 * e : 128 * e + 128], 64, 1) for e in range(2)]
        return jnp.concatenate(halves, axis=1)

    first_row = lax.broadcasted_iota(jnp.int32, (128, 256), 0) == 0
    top_turn = turned(top)
    nyquist = jnp.where(lane2 == 0, 0.5 * top_turn, 0.0)
    top_turn = jnp.where(first_row, nyquist, top_turn * sign2)
    top = jnp.where(first_row & (lane2 == 0), 0.5 * top, top)
    bottom_turn = turned(bottom) * sign2
    a_top = _dot3(top_ref, jnp.concatenate([top, top_turn], axis=0), ((1,), (0,)))
    a_bottom = _dot3(bottom_ref, jnp.concatenate([bottom, bottom_turn], axis=0), ((1,), (0,)))
    lane = _lanes((N2, 128))
    for e in range(2):
        cols = slice(128 * e, 128 * e + 128)
        up, down = a_top[:, cols], a_bottom[:, cols]
        both = up + down
        direct = jnp.where(lane == 0, up, jnp.where(lane == 64, down, both))
        rolled = pltpu.roll(jnp.where(lane == 0, down, both), 64, 1)
        z = keep_ref[...] * direct + swap_ref[...] * rolled
        x = _dot3(last_ref, z, ((1,), (1,)))
        out_ref[:, 8 * e : 8 * e + 8, :] = x.reshape(16, 8, N2)


def _one_hot(row, count):
    index = lax.broadcasted_iota(jnp.int32, (count, 256), 0).astype(F32).astype(BF16)
    return index == jnp.broadcast_to(row, (count, 256)).astype(BF16)


def _pick(mask, row, count):
    return jnp.where(mask, jnp.broadcast_to(row, (count, 256)).astype(BF16), jnp.zeros((), BF16))


def _tally(small, big):
    return lax.dot_general(small, big, (((1,), (1,)), ((), ())), preferred_element_type=F32)


def _tiles(grid_ref, shift, out_fn):
    lane = _lanes((32, 128))
    rows = [grid_ref[pl.ds(r, 32, stride=3), :] for r in range(3)]

    def turned(value, amount):
        amount %= 128
        return pltpu.roll(value, amount, 1) if amount else value

    for j in range(8):
        first, offset = divmod(TPIX * j, 128)
        value = turned(rows[first], shift - offset)
        if offset + TPIX > 128:
            rest = turned(rows[first + 1], shift + 128 - offset)
            value = jnp.where(lane < shift + 128 - offset, value, rest)
        keep = (lane >= shift) & (lane < shift + TPIX)
        out_fn(pl.ds(j, 32, stride=8), jnp.where(keep, value, 0.0))


def _split_pixel(point):
    high = jnp.floor(point * (1.0 / 128))
    return high, point - 128.0 * high


def hits_kernel(half, point_ref, out_ref, high_ref, low_ref, tmp_ref, grid_ref):
    for octet in range(2):
        for r in range(8):
            for h in range(2):
                cols = pl.ds(256 * r + 128 * h, 128)
                rows = pl.ds(128 * h + 64 * octet + r, 8, stride=8)
                low = 16 * half + 8 * octet
                tmp_ref[rows, :] = point_ref[low : low + 8, cols].astype(F32)
    for h in range(2):
        cols = slice(128 * h, 128 * h + 128)
        high, low = _split_pixel(tmp_ref[128 * h : 128 * h + 128, :])
        high_ref[:, cols] = high
        low_ref[:, cols] = low
    one = jnp.ones((1, 256), F32)

    def step(r, acc):
        big = _pick(_one_hot(low_ref[pl.ds(r, 1), :], 128), one, 128)
        small = _pick(_one_hot(high_ref[pl.ds(r, 1), :], 96), one, 96)
        return acc + _tally(small, big)

    grid_ref[...] = lax.fori_loop(0, 128, step, jnp.zeros((96, 128), F32), unroll=32)

    def put(rows, value):
        out_ref[rows, :] = value

    _tiles(grid_ref, TPIX, put)


def sums_kernel(value_ref, first_refs, second_refs, out_ref, grid_ref):
    one = jnp.ones((1, 256), F32)

    def step(base, high_ref, low_ref, r, acc):
        value = value_ref[pl.ds(base + r, 1), :]
        upper = value.astype(BF16).astype(F32)
        big = _pick(_one_hot(low_ref[pl.ds(r, 1), :], 128), one, 128)
        mask = _one_hot(high_ref[pl.ds(r, 1), :], 96)
        small = jnp.concatenate([_pick(mask, upper, 96), _pick(mask, value - upper, 96)], axis=0)
        return acc + _tally(small, big)

    acc = jnp.zeros((192, 128), F32)
    for base, (_, high_ref, low_ref) in ((0, first_refs), (128, second_refs)):
        turn = functools.partial(step, base, high_ref, low_ref)
        acc = lax.fori_loop(0, 128, turn, acc, unroll=64)
    grid_ref[...] = acc[:96] + acc[96:]

    def put(rows, value):
        out_ref[rows, :] = value + first_refs[0][rows, :] + second_refs[0][rows, :]

    _tiles(grid_ref, 0, put)


def spread_kernel(x_ref, out_ref, tmp_ref):
    for h in range(2):
        tmp_ref[256 * h : 256 * h + 256, :] = x_ref[:, 128 * h : 128 * h + 128]
    for octet in range(4):
        for r in range(8):
            for h in range(2):
                rows = pl.ds(256 * h + 64 * octet + r, 8, stride=8)
                cols = pl.ds(256 * r + 128 * h, 128)
                out_ref[8 * octet : 8 * octet + 8, cols] = tmp_ref[rows, :]


def finish_kernel(x_ref, out_ref):
    total = jnp.sum(x_ref[...], axis=0, keepdims=True)
    hits = pltpu.roll(total, 128 - TPIX, 1)
    out_ref[...] = (total / jnp.sqrt(1.0 + hits))[:, :TPIX]


VMEM = pl.BlockSpec(memory_space=pltpu.VMEM)
HBM = pl.BlockSpec(memory_space=pltpu.HBM)


def call(kernel, outs, scratch=(), space=VMEM, grant=GRANT):
    many = isinstance(outs, list)
    shapes = [jax.ShapeDtypeStruct(s, d) for s, d in (outs if many else [outs])]

    def run(*args):
        return pl.pallas_call(
            kernel,
            out_shape=shapes if many else shapes[0],
            in_specs=[space] * len(args),
            out_specs=[VMEM] * len(shapes) if many else VMEM,
            scratch_shapes=list(scratch),
            compiler_params=pltpu.CompilerParams(vmem_limit_bytes=grant),
        )(*args)

    return run


def exchange(value, axes):
    return lax.all_to_all(value, axes, split_axis=0, concat_axis=0, tiled=True)


def steps(tod, pointing, noise_level, modes):
    forward = [jnp.asarray(a) for a in _forward_tables()]
    inverse = [jnp.asarray(a) for a in _inverse_tables()]
    send_v, scale = call(
        basis_kernel,
        [((1, 64, 128), F32), ((24, 256), F32)],
        scratch=[pltpu.VMEM((2, 32, 128), F32)],
    )(modes, noise_level)
    send_tod = call(
        prep_kernel,
        ((256, 256), F32),
        scratch=[
            pltpu.VMEM((32, 2048), F32),
            pltpu.VMEM((512, 128), F32),
            pltpu.SemaphoreType.DMA((4,)),
        ],
        space=HBM,
        grant=WIDE_GRANT,
    )(tod).reshape(16, 16, 256)
    near = send_v
    for bit in range(4):
        pairs = [(i, i ^ (1 << bit)) for i in range(16)]
        far = lax.ppermute(near, "det", pairs)
        if bit < 3:
            near = jnp.concatenate([near, far], axis=0)
    got_tod = exchange(send_tod, "tm")
    spectra = call(forward_kernel, ((512, 128), F32))(got_tod, scale, *forward)
    trans, gain = call(
        gram_kernel,
        [((2, 256, 256), F32), ((2, 256, 256), F32)],
        scratch=[
            pltpu.VMEM((2, 256, 256), F32),
            pltpu.VMEM((128, 128), F32),
            pltpu.VMEM((128, 128), F32),
        ],
    )(near, far)
    mixed = exchange(spectra.reshape(256, 2, 128), ("det", "tm")).reshape(512, 128)
    weighted = call(apply_kernel, ((512, 128), F32))(mixed, trans, gain)
    counted = [
        call(
            functools.partial(hits_kernel, half),
            [((256, 128), F32), ((128, 256), F32), ((128, 256), F32)],
            scratch=[pltpu.VMEM((256, 128), F32), pltpu.VMEM((96, 128), F32)],
        )(pointing)
        for half in range(2)
    ]
    back = exchange(weighted.reshape(256, 2, 128), ("det", "tm")).reshape(512, 128)
    series = call(inverse_kernel, ((16, 16, 256), F32))(back, scale, *inverse)
    got_series = exchange(series, "tm").reshape(256, 256)
    bins = call(
        lambda value, *refs: sums_kernel(value, refs[0:3], refs[3:6], *refs[6:]),
        ((256, 128), F32),
        scratch=[pltpu.VMEM((96, 128), F32)],
    )(got_series, *counted[0], *counted[1])
    filtered = call(
        spread_kernel, ((32, 2048), F32), scratch=[pltpu.VMEM((512, 128), F32)]
    )(got_series)
    got_bins = exchange(bins, ("det", "tm"))
    binned = call(finish_kernel, ((1, TPIX), F32))(got_bins)
    return filtered, binned.reshape(TPIX)


def solution(mesh):
    placed = (P("det", "tm"), P("det", "tm"), P(None, "det"), P(None, "det", None))
    return jax.shard_map(
        steps,
        mesh=mesh,
        in_specs=placed,
        out_specs=(P("det", "tm"), P(("det", "tm"))),
        check_vma=False,
    )
```

```python
import functools

import numpy as np
import jax
import jax.numpy as jnp
from jax import lax
from jax.experimental import pallas as pl
from jax.experimental.pallas import tpu as pltpu
from jax.sharding import PartitionSpec as P


HIGHEST = lax.Precision.HIGHEST
NS = 32768
N1 = 128
N2 = 256
BANDS = 8
TPIX = 48
GRANT = 12 << 20
WIDE_GRANT = 60 << 20
F32 = jnp.float32
BF16 = jnp.bfloat16


def _slots():
    dev, step = np.meshgrid(np.arange(16), np.arange(8), indexing="ij")
    top = (16 * step + dev).reshape(-1)
    bottom = (16 * (15 - step) + dev).reshape(-1)
    return top, bottom


def _forward_tables():
    n1 = np.arange(N1)[:, None]
    k1 = np.arange(64)[None, :]
    angle = 2 * np.pi * (n1 * k1 % N1) / N1
    first = np.concatenate([np.cos(angle), -np.sin(angle)], axis=1)
    first[:, 64] = np.cos(np.pi * np.arange(N1))
    n2 = np.arange(N2)[:, None]
    turn = 2 * np.pi * (n2 * k1) / NS
    keep = np.concatenate([np.cos(turn), np.cos(turn)], axis=1)
    swap = np.concatenate([np.sin(turn), -np.sin(turn)], axis=1)
    edge = 2 * np.pi * 64 * np.arange(N2) / NS
    keep[:, 0] = 1.0
    swap[:, 0] = np.cos(edge)
    keep[:, 64] = -np.sin(edge)
    swap[:, 64] = 0.0
    last = []
    for rows in _slots():
        phase = 2 * np.pi * (rows[:, None] * np.arange(N2)[None, :] % N2) / N2
        last.append(np.concatenate([np.cos(phase), np.sin(phase)], axis=1))
    return [np.asarray(a, np.float32) for a in (first, keep, swap, last[0], last[1])]


def _inverse_tables():
    na = np.arange(N2)
    first = []
    for position, rows in enumerate(_slots()):
        phase = 2 * np.pi * (na[:, None] * rows[None, :] % N2) / N2
        sine = np.sin(phase)
        if position == 0:
            sine[:, 0] = np.where(na % 2 == 0, 1.0, -1.0)
        first.append(np.concatenate([np.cos(phase), sine], axis=1))
    k1 = np.arange(64)[None, :]
    turn = 2 * np.pi * (na[:, None] * k1) / NS
    keep = np.concatenate([2 * np.cos(turn), 2 * np.cos(turn)], axis=1)
    swap = np.concatenate([-2 * np.sin(turn), 2 * np.sin(turn)], axis=1)
    edge = 2 * np.pi * 64 * na / NS
    keep[:, 0] = 2.0
    swap[:, 0] = 0.0
    keep[:, 64] = -2 * np.sin(edge)
    swap[:, 64] = 2 * np.cos(edge)
    nb = np.arange(N1)[:, None]
    angle = 2 * np.pi * (nb * k1 % N1) / N1
    last = np.concatenate([np.cos(angle), -np.sin(angle)], axis=1) / NS
    last[:, 64] = np.cos(np.pi * np.arange(N1)) / NS
    tables = [np.asarray(a, np.float32) for a in (keep, swap)]
    for a in (first[0], first[1], last):
        upper = np.asarray(a, jnp.bfloat16)
        lower = np.asarray(a - upper.astype(np.float64), jnp.bfloat16)
        tables.append(np.stack([upper, lower]))
    return tables


def _dot(a, b):
    return jnp.dot(a, b, precision=HIGHEST, preferred_element_type=F32)


def _dot_tn(a, b):
    return lax.dot_general(
        a, b, (((0,), (0,)), ((), ())), precision=HIGHEST, preferred_element_type=F32
    )


def _parts(a):
    upper = a.astype(BF16)
    return upper, (a - upper.astype(F32)).astype(BF16)


def _dot3(table_ref, b, dims):
    upper, lower = _parts(b)

    def product(x, y):
        return lax.dot_general(x, y, (dims, ((), ())), preferred_element_type=F32)

    return product(table_ref[0], upper) + (
        product(table_ref[0], lower) + product(table_ref[1], upper)
    )


def _lanes(shape):
    return lax.broadcasted_iota(jnp.int32, shape, 1)


def _position():
    return lax.axis_index("det"), lax.axis_index("tm")


def basis_kernel(modes_ref, noise_ref, v_out, scale_out, tmp_ref):
    _, pos = _position()
    band = pos // 2
    root = lax.rsqrt(noise_ref[...])
    eye = lax.broadcasted_iota(jnp.int32, (32, 32), 0) == _lanes((32, 32))
    row_of = lax.broadcasted_iota(jnp.int32, (BANDS, 32), 0)
    for part, which in enumerate((band, BANDS - 1)):
        row = jnp.sum(jnp.where(row_of == which, root, 0.0), axis=0, keepdims=True)
        col = jnp.sum(jnp.where(eye, row, 0.0), axis=1, keepdims=True)
        tmp_ref[part] = modes_ref[which] * col
        even, odd = [tmp_ref[part, pl.ds(e, 16, stride=2), :] for e in range(2)]
        v_out[0, 16 * part : 16 * part + 16, :] = jnp.where(pos % 2 == 0, even, odd)
    for e in range(2):
        mask = _lanes((BANDS, 32)) == 2 * pos + e
        lanes = pl.ds(128 * e, 128)
        up = jnp.sum(jnp.where(mask, root, 0.0), axis=1, keepdims=True)
        scale_out[0:8, lanes] = jnp.broadcast_to(up, (8, 128))
        scale_out[8:16, lanes] = jnp.broadcast_to(up[7:8], (8, 128))


def _spread_rows(source_ref, tmp_ref, octet):
    for r in range(8):
        for h in range(2):
            cols = pl.ds(256 * r + 128 * h, 128)
            rows = pl.ds(256 * h + 64 * octet + r, 8, stride=8)
            tmp_ref[rows, :] = source_ref[8 * octet : 8 * octet + 8, cols].astype(F32)


def prep_kernel(tod_ref, tod_out, tod_in, tod_tmp, sems):
    copies = []
    for octet in range(4):
        rows = pl.ds(8 * octet, 8)
        copy = pltpu.make_async_copy(tod_ref.at[rows], tod_in.at[rows], sems.at[octet])
        copy.start()
        copies.append(copy)
    for octet in range(4):
        copies[octet].wait()
        _spread_rows(tod_in, tod_tmp, octet)
        for h in range(2):
            cols = slice(128 * h, 128 * h + 128)
            low = 256 * h + 64 * octet
            tod_out[64 * octet : 64 * octet + 64, cols] = tod_tmp[low : low + 64, :]


def _first_scale(scale_ref):
    lane = _lanes((8, 256)) % 128
    row = lax.broadcasted_iota(jnp.int32, (8, 256), 0)
    return jnp.where((lane == 64) & (row == 0), scale_ref[8:16, :], scale_ref[0:8, :])


def forward_kernel(x_ref, scale_ref, first_ref, keep_ref, swap_ref, top_ref, bottom_ref, out_ref):
    lane = _lanes((N2, 128))
    sign = jnp.where(lane < 64, 1.0, -1.0)
    parity = lax.broadcasted_iota(jnp.int32, (N2, 128), 0) % 2
    alternate = jnp.where(lane == 64, jnp.where(parity == 0, -1.0, 1.0), 0.0)
    tops, bottoms, nyquist = [], [], []
    for e in range(2):
        x = x_ref[:, 8 * e : 8 * e + 8, :].reshape(N1, N2)
        s = _dot_tn(x, first_ref[...])
        a = keep_ref[...] * s
        b = swap_ref[...] * pltpu.roll(s, 64, 1)
        both = a + b
        top = jnp.where(lane == 0, a, jnp.where(lane == 64, 0.0, both))
        bottom = jnp.where(lane == 0, b, jnp.where(lane == 64, a, both))
        top_turn = pltpu.roll(top, 64, 1) * sign
        bottom_turn = pltpu.roll(bottom, 64, 1) * sign
        nyquist.append(jnp.sum(top_turn * alternate, axis=0, keepdims=True))
        tops.append(jnp.concatenate([top, top_turn], axis=0))
        bottoms.append(jnp.concatenate([bottom, bottom_turn], axis=0))
    out_top = _dot(top_ref[...], jnp.concatenate(tops, axis=1))
    out_bottom = _dot(bottom_ref[...], jnp.concatenate(bottoms, axis=1))
    nyq = jnp.concatenate(nyquist, axis=1)
    row0 = lax.broadcasted_iota(jnp.int32, (8, 256), 0) == 0
    for d in range(16):
        up = out_top[8 * d : 8 * d + 8]
        if d == 0:
            up = (up + jnp.where(row0, nyq, 0.0)) * _first_scale(scale_ref)
        else:
            up = up * scale_ref[0:8, :]
        down = out_bottom[8 * d : 8 * d + 8] * scale_ref[0:8, :]
        for e in range(2):
            cols = slice(128 * e, 128 * e + 128)
            out_ref[pl.ds(32 * d + e, 8, stride=4), :] = up[:, cols]
            out_ref[pl.ds(32 * d + 2 + e, 8, stride=4), :] = down[:, cols]


def _pair_inverse(a, b, c):
    r = 1.0 / (a * c - b * b)
    return c * r, -b * r, a * r


def _quad_inverse(m):
    a0, a1, a2 = _pair_inverse(m[0][0], m[0][1], m[1][1])
    w00 = a0 * m[0][2] + a1 * m[1][2]
    w01 = a0 * m[0][3] + a1 * m[1][3]
    w10 = a1 * m[0][2] + a2 * m[1][2]
    w11 = a1 * m[0][3] + a2 * m[1][3]
    q0, q1, q2 = _pair_inverse(
        m[2][2] - (m[0][2] * w00 + m[1][2] * w10),
        m[2][3] - (m[0][2] * w01 + m[1][2] * w11),
        m[3][3] - (m[0][3] * w01 + m[1][3] * w11),
    )
    x00 = -(w00 * q0 + w01 * q1)
    x01 = -(w00 * q1 + w01 * q2)
    x10 = -(w10 * q0 + w11 * q1)
    x11 = -(w10 * q1 + w11 * q2)
    i00 = a0 - (x00 * w00 + x01 * w01)
    i01 = a1 - (x00 * w10 + x01 * w11)
    i11 = a2 - (x10 * w10 + x11 * w11)
    return [
        [i00, i01, x00, x01],
        [i01, i11, x10, x11],
        [x00, x10, q0, q1],
        [x01, x11, q1, q2],
    ]


def invert_in_place(mat_refs):
    lane = _lanes((128, 128))
    lane8 = _lanes((8, 128))

    def step(panel, carry):
        base = 4 * panel
        within = (lane >= base) & (lane < base + 4)
        index = [jnp.full((128, 128), base + j, jnp.int32) for j in range(4)]
        mats = [ref[...] for ref in mat_refs]
        rows = [
            [jnp.broadcast_to(ref[pl.ds(base + j, 1), :], (8, 128)) for j in range(4)]
            for ref in mat_refs
        ]
        pivots = [
            [[jnp.take_along_axis(r[i], index[j][:8], axis=1) for j in range(4)] for i in range(4)]
            for r in rows
        ]
        inverses = [_quad_inverse(p) for p in pivots]
        results = []
        for mat, row, inverse in zip(mats, rows, inverses):
            new = jnp.where(within, 0.0, mat)
            scaled = []
            for i in range(4):
                line = sum(inverse[i][j] * row[j] for j in range(4))
                for j in range(4):
                    line = jnp.where(lane8 == base + j, inverse[i][j], line)
                scaled.append(line)
                col = jnp.take_along_axis(mat, index[i], axis=1)
                new = new - col * jnp.concatenate([line] * 16, axis=0)
            results.append((new, scaled))
        for ref, (new, scaled) in zip(mat_refs, results):
            ref[...] = new
            for i in range(4):
                ref[pl.ds(base + i, 1), :] = scaled[i][0:1]
        return carry

    lax.fori_loop(0, 32, step, 0)


def gram_kernel(near_ref, far_ref, other_ref, trans_ref, gain_ref, vees_ref, *mat_refs):
    dev, pos = _position()
    parity = pos % 2
    for j in range(16):
        own = near_ref if j < 8 else far_ref
        rows = pl.ds(pl.multiple_of((dev ^ j) * 16, 16), 16)
        for part in range(2):
            cols = slice(128 * part, 128 * part + 128)
            low = slice(16 * part, 16 * part + 16)
            vees_ref[parity, rows, cols] = own[j % 8, low, :]
            vees_ref[1 - parity, rows, cols] = other_ref[j, low, :]
    parts = [[vees_ref[e, :, 128 * part : 128 * part + 128] for part in range(2)] for e in range(2)]
    eye = lax.broadcasted_iota(jnp.int32, (128, 128), 0) == _lanes((128, 128))
    for part in range(2):
        mat_refs[part][...] = (
            jnp.where(eye, 1.0, 0.0)
            + _dot_tn(parts[0][part], parts[0][part])
            + _dot_tn(parts[1][part], parts[1][part])
        )
    invert_in_place(mat_refs)
    for e in range(2):
        trans_ref[e] = jnp.concatenate([parts[e][0], parts[e][1]], axis=1).T
        gain_ref[e] = jnp.concatenate(
            [_dot(parts[e][part], mat_refs[part][...]) for part in range(2)], axis=1
        )


def apply_kernel(x_ref, trans_ref, gain_ref, out_ref):
    xs = [x_ref[pl.ds(e, 256, stride=2), :] for e in range(2)]
    proj = _dot(trans_ref[0], xs[0]) + _dot(trans_ref[1], xs[1])
    dev, pos = _position()
    special = (_lanes((256, 128)) == 64) & (dev * 16 + pos == 0)
    second = lax.broadcasted_iota(jnp.int32, (256, 128), 0) >= 128
    proj = jnp.where(special == second, proj, 0.0)
    for e in range(2):
        out_ref[pl.ds(e, 256, stride=2), :] = xs[e] - _dot(gain_ref[e], proj)


def inverse_kernel(y_ref, scale_ref, keep_ref, swap_ref, top_ref, bottom_ref, last_ref, out_ref):
    lane2 = _lanes((128, 256)) % 128
    sign2 = jnp.where(lane2 < 64, -1.0, 1.0)
    ups, downs = [], []
    for d in range(16):
        up, down = [
            jnp.concatenate(
                [y_ref[pl.ds(32 * d + 2 * half + e, 8, stride=4), :] for e in range(2)], axis=1
            )
            for half in range(2)
        ]
        ups.append(up * (_first_scale(scale_ref) if d == 0 else scale_ref[0:8, :]))
        downs.append(down * scale_ref[0:8, :])
    top = jnp.concatenate(ups, axis=0)
    bottom = jnp.concatenate(downs, axis=0)

    def turned(v):
        halves = [pltpu.roll(v[:, 128 * e : 128 * e + 128], 64, 1) for e in range(2)]
        return jnp.concatenate(halves, axis=1)

    first_row = lax.broadcasted_iota(jnp.int32, (128, 256), 0) == 0
    top_turn = turned(top)
    nyquist = jnp.where(lane2 == 0, 0.5 * top_turn, 0.0)
    top_turn = jnp.where(first_row, nyquist, top_turn * sign2)
    top = jnp.where(first_row & (lane2 == 0), 0.5 * top, top)
    bottom_turn = turned(bottom) * sign2
    a_top = _dot3(top_ref, jnp.concatenate([top, top_turn], axis=0), ((1,), (0,)))
    a_bottom = _dot3(bottom_ref, jnp.concatenate([bottom, bottom_turn], axis=0), ((1,), (0,)))
    lane = _lanes((N2, 128))
    for e in range(2):
        cols = slice(128 * e, 128 * e + 128)
        up, down = a_top[:, cols], a_bottom[:, cols]
        both = up + down
        direct = jnp.where(lane == 0, up, jnp.where(lane == 64, down, both))
        rolled = pltpu.roll(jnp.where(lane == 0, down, both), 64, 1)
        z = keep_ref[...] * direct + swap_ref[...] * rolled
        x = _dot3(last_ref, z, ((1,), (1,)))
        out_ref[:, 8 * e : 8 * e + 8, :] = x.reshape(16, 8, N2)


def _one_hot(row, count):
    index = lax.broadcasted_iota(jnp.int32, (count, 256), 0).astype(F32).astype(BF16)
    return index == jnp.broadcast_to(row, (count, 256)).astype(BF16)


def _pick(mask, row, count):
    return jnp.where(mask, jnp.broadcast_to(row, (count, 256)).astype(BF16), jnp.zeros((), BF16))


def _tally(small, big):
    return lax.dot_general(small, big, (((1,), (1,)), ((), ())), preferred_element_type=F32)


def _tiles(grid_ref, shift, out_fn):
    lane = _lanes((32, 128))
    rows = [grid_ref[pl.ds(r, 32, stride=3), :] for r in range(3)]

    def turned(value, amount):
        amount %= 128
        return pltpu.roll(value, amount, 1) if amount else value

    for j in range(8):
        first, offset = divmod(TPIX * j, 128)
        value = turned(rows[first], shift - offset)
        if offset + TPIX > 128:
            rest = turned(rows[first + 1], shift + 128 - offset)
            value = jnp.where(lane < shift + 128 - offset, value, rest)
        keep = (lane >= shift) & (lane < shift + TPIX)
        out_fn(pl.ds(j, 32, stride=8), jnp.where(keep, value, 0.0))


def _split_pixel(point):
    high = jnp.floor(point * (1.0 / 128))
    return high, point - 128.0 * high


def hits_kernel(half, point_ref, out_ref, high_ref, low_ref, tmp_ref, grid_ref):
    for octet in range(2):
        for r in range(8):
            for h in range(2):
                cols = pl.ds(256 * r + 128 * h, 128)
                rows = pl.ds(128 * h + 64 * octet + r, 8, stride=8)
                low = 16 * half + 8 * octet
                tmp_ref[rows, :] = point_ref[low : low + 8, cols].astype(F32)
    for h in range(2):
        cols = slice(128 * h, 128 * h + 128)
        high, low = _split_pixel(tmp_ref[128 * h : 128 * h + 128, :])
        high_ref[:, cols] = high
        low_ref[:, cols] = low
    one = jnp.ones((1, 256), F32)

    def step(r, acc):
        big = _pick(_one_hot(low_ref[pl.ds(r, 1), :], 128), one, 128)
        small = _pick(_one_hot(high_ref[pl.ds(r, 1), :], 96), one, 96)
        return acc + _tally(small, big)

    grid_ref[...] = lax.fori_loop(0, 128, step, jnp.zeros((96, 128), F32), unroll=32)

    def put(rows, value):
        out_ref[rows, :] = value

    _tiles(grid_ref, TPIX, put)


def sums_kernel(value_ref, first_refs, second_refs, out_ref, grid_ref):
    one = jnp.ones((1, 256), F32)

    def step(base, high_ref, low_ref, r, acc):
        value = value_ref[pl.ds(base + r, 1), :]
        upper = value.astype(BF16).astype(F32)
        big = _pick(_one_hot(low_ref[pl.ds(r, 1), :], 128), one, 128)
        mask = _one_hot(high_ref[pl.ds(r, 1), :], 96)
        small = jnp.concatenate([_pick(mask, upper, 96), _pick(mask, value - upper, 96)], axis=0)
        return acc + _tally(small, big)

    acc = jnp.zeros((192, 128), F32)
    for base, (_, high_ref, low_ref) in ((0, first_refs), (128, second_refs)):
        turn = functools.partial(step, base, high_ref, low_ref)
        acc = lax.fori_loop(0, 128, turn, acc, unroll=64)
    grid_ref[...] = acc[:96] + acc[96:]

    def put(rows, value):
        out_ref[rows, :] = value + first_refs[0][rows, :] + second_refs[0][rows, :]

    _tiles(grid_ref, 0, put)


def spread_kernel(x_ref, out_ref, tmp_ref):
    for h in range(2):
        tmp_ref[256 * h : 256 * h + 256, :] = x_ref[:, 128 * h : 128 * h + 128]
    for octet in range(4):
        for r in range(8):
            for h in range(2):
                rows = pl.ds(256 * h + 64 * octet + r, 8, stride=8)
                cols = pl.ds(256 * r + 128 * h, 128)
                out_ref[8 * octet : 8 * octet + 8, cols] = tmp_ref[rows, :]


def finish_kernel(x_ref, out_ref):
    total = jnp.sum(x_ref[...], axis=0, keepdims=True)
    hits = pltpu.roll(total, 128 - TPIX, 1)
    out_ref[...] = (total / jnp.sqrt(1.0 + hits))[:, :TPIX]


VMEM = pl.BlockSpec(memory_space=pltpu.VMEM)
HBM = pl.BlockSpec(memory_space=pltpu.HBM)


def call(kernel, outs, scratch=(), space=VMEM, grant=GRANT):
    many = isinstance(outs, list)
    shapes = [jax.ShapeDtypeStruct(s, d) for s, d in (outs if many else [outs])]

    def run(*args):
        return pl.pallas_call(
            kernel,
            out_shape=shapes if many else shapes[0],
            in_specs=[space] * len(args),
            out_specs=[VMEM] * len(shapes) if many else VMEM,
            scratch_shapes=list(scratch),
            compiler_params=pltpu.CompilerParams(vmem_limit_bytes=grant),
        )(*args)

    return run


def exchange(value, axes):
    return lax.all_to_all(value, axes, split_axis=0, concat_axis=0, tiled=True)


def steps(tod, pointing, noise_level, modes):
    forward = [jnp.asarray(a) for a in _forward_tables()]
    inverse = [jnp.asarray(a) for a in _inverse_tables()]
    send_v, scale = call(
        basis_kernel,
        [((1, 32, 128), F32), ((16, 256), F32)],
        scratch=[pltpu.VMEM((2, 32, 128), F32)],
    )(modes, noise_level)
    send_tod = call(
        prep_kernel,
        ((256, 256), F32),
        scratch=[
            pltpu.VMEM((32, 2048), F32),
            pltpu.VMEM((512, 128), F32),
            pltpu.SemaphoreType.DMA((4,)),
        ],
        space=HBM,
        grant=WIDE_GRANT,
    )(tod).reshape(16, 16, 256)
    near = send_v
    for bit in range(4):
        pairs = [(i, i ^ (1 << bit)) for i in range(16)]
        far = lax.ppermute(near, "det", pairs)
        if bit < 3:
            near = jnp.concatenate([near, far], axis=0)
    gathered = jnp.concatenate([near, far], axis=0)
    other = lax.ppermute(gathered, "tm", [(i, i ^ 1) for i in range(16)])
    got_tod = exchange(send_tod, "tm")
    spectra = call(forward_kernel, ((512, 128), F32))(got_tod, scale, *forward)
    trans, gain = call(
        gram_kernel,
        [((2, 256, 256), F32), ((2, 256, 256), F32)],
        scratch=[
            pltpu.VMEM((2, 256, 256), F32),
            pltpu.VMEM((128, 128), F32),
            pltpu.VMEM((128, 128), F32),
        ],
    )(near, far, other)
    mixed = exchange(spectra.reshape(256, 2, 128), ("det", "tm")).reshape(512, 128)
    weighted = call(apply_kernel, ((512, 128), F32))(mixed, trans, gain)
    counted = [
        call(
            functools.partial(hits_kernel, half),
            [((256, 128), F32), ((128, 256), F32), ((128, 256), F32)],
            scratch=[pltpu.VMEM((256, 128), F32), pltpu.VMEM((96, 128), F32)],
        )(pointing)
        for half in range(2)
    ]
    back = exchange(weighted.reshape(256, 2, 128), ("det", "tm")).reshape(512, 128)
    series = call(inverse_kernel, ((16, 16, 256), F32))(back, scale, *inverse)
    got_series = exchange(series, "tm").reshape(256, 256)
    bins = call(
        lambda value, *refs: sums_kernel(value, refs[0:3], refs[3:6], *refs[6:]),
        ((256, 128), F32),
        scratch=[pltpu.VMEM((96, 128), F32)],
    )(got_series, *counted[0], *counted[1])
    filtered = call(
        spread_kernel, ((32, 2048), F32), scratch=[pltpu.VMEM((512, 128), F32)]
    )(got_series)
    got_bins = exchange(bins, ("det", "tm"))
    binned = call(finish_kernel, ((1, TPIX), F32))(got_bins)
    return filtered, binned.reshape(TPIX)


def solution(mesh):
    placed = (P("det", "tm"), P("det", "tm"), P(None, "det"), P(None, "det", None))
    return jax.shard_map(
        steps,
        mesh=mesh,
        in_specs=placed,
        out_specs=(P("det", "tm"), P(("det", "tm"))),
        check_vma=False,
    )
```

```python
import functools

import numpy as np
import jax
import jax.numpy as jnp
from jax import lax
from jax.experimental import pallas as pl
from jax.experimental.pallas import tpu as pltpu
from jax.sharding import PartitionSpec as P


HIGHEST = lax.Precision.HIGHEST
NS = 32768
N1 = 128
N2 = 256
BANDS = 8
TPIX = 48
GRANT = 12 << 20
WIDE_GRANT = 60 << 20
F32 = jnp.float32
BF16 = jnp.bfloat16


def _slots():
    dev, step = np.meshgrid(np.arange(16), np.arange(8), indexing="ij")
    top = (16 * step + dev).reshape(-1)
    bottom = (16 * (step + 8) + dev).reshape(-1)
    return top, bottom


def _forward_tables():
    n1 = np.arange(N1)[:, None]
    k1 = np.arange(64)[None, :]
    angle = 2 * np.pi * (n1 * k1 % N1) / N1
    first = np.concatenate([np.cos(angle), -np.sin(angle)], axis=1)
    first[:, 64] = np.cos(np.pi * np.arange(N1))
    n2 = np.arange(N2)[:, None]
    turn = 2 * np.pi * (n2 * k1) / NS
    keep = np.concatenate([np.cos(turn), np.cos(turn)], axis=1)
    swap = np.concatenate([np.sin(turn), -np.sin(turn)], axis=1)
    edge = 2 * np.pi * 64 * np.arange(N2) / NS
    keep[:, 0] = 1.0
    swap[:, 0] = np.cos(edge)
    keep[:, 64] = -np.sin(edge)
    swap[:, 64] = 0.0
    last = []
    for rows in _slots():
        phase = 2 * np.pi * (rows[:, None] * np.arange(N2)[None, :] % N2) / N2
        last.append(np.concatenate([np.cos(phase), np.sin(phase)], axis=1))
    return [np.asarray(a, np.float32) for a in (first, keep, swap, last[0], last[1])]


def _inverse_tables():
    na = np.arange(N2)
    first = []
    for position, rows in enumerate(_slots()):
        phase = 2 * np.pi * (na[:, None] * rows[None, :] % N2) / N2
        sine = np.sin(phase)
        if position == 0:
            sine[:, 0] = np.where(na % 2 == 0, 1.0, -1.0)
        first.append(np.concatenate([np.cos(phase), sine], axis=1))
    k1 = np.arange(64)[None, :]
    turn = 2 * np.pi * (na[:, None] * k1) / NS
    keep = np.concatenate([2 * np.cos(turn), 2 * np.cos(turn)], axis=1)
    swap = np.concatenate([-2 * np.sin(turn), 2 * np.sin(turn)], axis=1)
    edge = 2 * np.pi * 64 * na / NS
    keep[:, 0] = 2.0
    swap[:, 0] = 0.0
    keep[:, 64] = -2 * np.sin(edge)
    swap[:, 64] = 2 * np.cos(edge)
    nb = np.arange(N1)[:, None]
    angle = 2 * np.pi * (nb * k1 % N1) / N1
    last = np.concatenate([np.cos(angle), -np.sin(angle)], axis=1) / NS
    last[:, 64] = np.cos(np.pi * np.arange(N1)) / NS
    tables = [np.asarray(a, np.float32) for a in (keep, swap)]
    for a in (first[0], first[1], last):
        upper = np.asarray(a, jnp.bfloat16)
        lower = np.asarray(a - upper.astype(np.float64), jnp.bfloat16)
        tables.append(np.stack([upper, lower]))
    return tables


def _dot(a, b):
    return jnp.dot(a, b, precision=HIGHEST, preferred_element_type=F32)


def _dot_tn(a, b):
    return lax.dot_general(
        a, b, (((0,), (0,)), ((), ())), precision=HIGHEST, preferred_element_type=F32
    )


def _parts(a):
    upper = a.astype(BF16)
    return upper, (a - upper.astype(F32)).astype(BF16)


def _dot3(table_ref, b, dims):
    upper, lower = _parts(b)

    def product(x, y):
        return lax.dot_general(x, y, (dims, ((), ())), preferred_element_type=F32)

    return product(table_ref[0], upper) + (
        product(table_ref[0], lower) + product(table_ref[1], upper)
    )


def _lanes(shape):
    return lax.broadcasted_iota(jnp.int32, shape, 1)


def _position():
    return lax.axis_index("det"), lax.axis_index("tm")


def basis_kernel(modes_hbm, noise_hbm, v_out, scale_out, tmp_ref, modes_ref, noise_ref, sems):
    _, pos = _position()
    band = jnp.where(pos < BANDS, pos, 2 * BANDS - 1 - pos)
    copies = [
        pltpu.make_async_copy(noise_hbm, noise_ref, sems.at[0]),
        pltpu.make_async_copy(modes_hbm.at[band], modes_ref.at[0], sems.at[1]),
        pltpu.make_async_copy(modes_hbm.at[BANDS - 1], modes_ref.at[1], sems.at[2]),
    ]
    for copy in copies:
        copy.start()
    for copy in copies:
        copy.wait()
    root = lax.rsqrt(noise_ref[...])
    eye = lax.broadcasted_iota(jnp.int32, (32, 32), 0) == _lanes((32, 32))
    row_of = lax.broadcasted_iota(jnp.int32, (BANDS, 32), 0)
    for part, which in enumerate((band, BANDS - 1)):
        row = jnp.sum(jnp.where(row_of == which, root, 0.0), axis=0, keepdims=True)
        col = jnp.sum(jnp.where(eye, row, 0.0), axis=1, keepdims=True)
        tmp_ref[part] = modes_ref[part] * col
        for e in range(2):
            low = 32 * part + 16 * e
            v_out[0, low : low + 16, :] = tmp_ref[part, pl.ds(e, 16, stride=2), :]
    flipped = jnp.concatenate([root[BANDS - 1 - j : BANDS - j] for j in range(BANDS)], axis=0)
    for e in range(2):
        mask = _lanes((BANDS, 32)) == 2 * pos + e
        lanes = pl.ds(128 * e, 128)
        up = jnp.sum(jnp.where(mask, root, 0.0), axis=1, keepdims=True)
        down = jnp.sum(jnp.where(mask, flipped, 0.0), axis=1, keepdims=True)
        scale_out[0:8, lanes] = jnp.broadcast_to(up, (8, 128))
        scale_out[8:16, lanes] = jnp.broadcast_to(down, (8, 128))
        scale_out[16:24, lanes] = jnp.broadcast_to(up[7:8], (8, 128))


def _spread_rows(source_ref, tmp_ref, octet):
    for r in range(8):
        for h in range(2):
            cols = pl.ds(256 * r + 128 * h, 128)
            rows = pl.ds(256 * h + 64 * octet + r, 8, stride=8)
            tmp_ref[rows, :] = source_ref[8 * octet : 8 * octet + 8, cols].astype(F32)


def prep_kernel(tod_ref, tod_out, tod_in, tod_tmp, sems):
    copies = []
    for octet in range(4):
        rows = pl.ds(8 * octet, 8)
        copy = pltpu.make_async_copy(tod_ref.at[rows], tod_in.at[rows], sems.at[octet])
        copy.start()
        copies.append(copy)
    for octet in range(4):
        copies[octet].wait()
        _spread_rows(tod_in, tod_tmp, octet)
        for h in range(2):
            cols = slice(128 * h, 128 * h + 128)
            low = 256 * h + 64 * octet
            tod_out[64 * octet : 64 * octet + 64, cols] = tod_tmp[low : low + 64, :]


def _first_scale(scale_ref):
    lane = _lanes((8, 256)) % 128
    row = lax.broadcasted_iota(jnp.int32, (8, 256), 0)
    return jnp.where((lane == 64) & (row == 0), scale_ref[16:24, :], scale_ref[0:8, :])


def forward_kernel(x_ref, scale_ref, first_ref, keep_ref, swap_ref, top_ref, bottom_ref, out_ref):
    lane = _lanes((N2, 128))
    sign = jnp.where(lane < 64, 1.0, -1.0)
    parity = lax.broadcasted_iota(jnp.int32, (N2, 128), 0) % 2
    alternate = jnp.where(lane == 64, jnp.where(parity == 0, -1.0, 1.0), 0.0)
    tops, bottoms, nyquist = [], [], []
    for e in range(2):
        x = x_ref[:, 8 * e : 8 * e + 8, :].reshape(N1, N2)
        s = _dot_tn(x, first_ref[...])
        a = keep_ref[...] * s
        b = swap_ref[...] * pltpu.roll(s, 64, 1)
        both = a + b
        top = jnp.where(lane == 0, a, jnp.where(lane == 64, 0.0, both))
        bottom = jnp.where(lane == 0, b, jnp.where(lane == 64, a, both))
        top_turn = pltpu.roll(top, 64, 1) * sign
        bottom_turn = pltpu.roll(bottom, 64, 1) * sign
        nyquist.append(jnp.sum(top_turn * alternate, axis=0, keepdims=True))
        tops.append(jnp.concatenate([top, top_turn], axis=0))
        bottoms.append(jnp.concatenate([bottom, bottom_turn], axis=0))
    out_top = _dot(top_ref[...], jnp.concatenate(tops, axis=1))
    out_bottom = _dot(bottom_ref[...], jnp.concatenate(bottoms, axis=1))
    nyq = jnp.concatenate(nyquist, axis=1)
    row0 = lax.broadcasted_iota(jnp.int32, (8, 256), 0) == 0
    for d in range(16):
        up = out_top[8 * d : 8 * d + 8]
        if d == 0:
            up = (up + jnp.where(row0, nyq, 0.0)) * _first_scale(scale_ref)
        else:
            up = up * scale_ref[0:8, :]
        down = out_bottom[8 * d : 8 * d + 8] * scale_ref[8:16, :]
        for e in range(2):
            cols = slice(128 * e, 128 * e + 128)
            out_ref[pl.ds(32 * d + e, 8, stride=2), :] = up[:, cols]
            out_ref[pl.ds(32 * d + 16 + e, 8, stride=2), :] = down[:, cols]


def _pair_inverse(a, b, c):
    r = 1.0 / (a * c - b * b)
    return c * r, -b * r, a * r


def _quad_inverse(m):
    a0, a1, a2 = _pair_inverse(m[0][0], m[0][1], m[1][1])
    w00 = a0 * m[0][2] + a1 * m[1][2]
    w01 = a0 * m[0][3] + a1 * m[1][3]
    w10 = a1 * m[0][2] + a2 * m[1][2]
    w11 = a1 * m[0][3] + a2 * m[1][3]
    q0, q1, q2 = _pair_inverse(
        m[2][2] - (m[0][2] * w00 + m[1][2] * w10),
        m[2][3] - (m[0][2] * w01 + m[1][2] * w11),
        m[3][3] - (m[0][3] * w01 + m[1][3] * w11),
    )
    x00 = -(w00 * q0 + w01 * q1)
    x01 = -(w00 * q1 + w01 * q2)
    x10 = -(w10 * q0 + w11 * q1)
    x11 = -(w10 * q1 + w11 * q2)
    i00 = a0 - (x00 * w00 + x01 * w01)
    i01 = a1 - (x00 * w10 + x01 * w11)
    i11 = a2 - (x10 * w10 + x11 * w11)
    return [
        [i00, i01, x00, x01],
        [i01, i11, x10, x11],
        [x00, x10, q0, q1],
        [x01, x11, q1, q2],
    ]


def invert_in_place(mat_refs):
    lane = _lanes((128, 128))
    lane8 = _lanes((8, 128))

    def step(panel, carry):
        base = 4 * panel
        within = (lane >= base) & (lane < base + 4)
        index = [jnp.full((128, 128), base + j, jnp.int32) for j in range(4)]
        mats = [ref[...] for ref in mat_refs]
        rows = [
            [jnp.broadcast_to(ref[pl.ds(base + j, 1), :], (8, 128)) for j in range(4)]
            for ref in mat_refs
        ]
        pivots = [
            [[jnp.take_along_axis(r[i], index[j][:8], axis=1) for j in range(4)] for i in range(4)]
            for r in rows
        ]
        inverses = [_quad_inverse(p) for p in pivots]
        results = []
        for mat, row, inverse in zip(mats, rows, inverses):
            new = jnp.where(within, 0.0, mat)
            scaled = []
            for i in range(4):
                line = sum(inverse[i][j] * row[j] for j in range(4))
                for j in range(4):
                    line = jnp.where(lane8 == base + j, inverse[i][j], line)
                scaled.append(line)
                col = jnp.take_along_axis(mat, index[i], axis=1)
                new = new - col * jnp.concatenate([line] * 16, axis=0)
            results.append((new, scaled))
        for ref, (new, scaled) in zip(mat_refs, results):
            ref[...] = new
            for i in range(4):
                ref[pl.ds(base + i, 1), :] = scaled[i][0:1]
        return carry

    lax.fori_loop(0, 32, step, 0)


def gram_kernel(near_ref, far_ref, trans_ref, gain_ref, vees_ref, *mat_refs):
    dev, _ = _position()
    for j in range(16):
        source = near_ref if j < 8 else far_ref
        rows = pl.ds(pl.multiple_of((dev ^ j) * 16, 16), 16)
        for e in range(2):
            for part in range(2):
                low = 32 * part + 16 * e
                vees_ref[e, rows, 128 * part : 128 * part + 128] = source[j % 8, low : low + 16, :]
    parts = [[vees_ref[e, :, 128 * part : 128 * part + 128] for part in range(2)] for e in range(2)]
    eye = lax.broadcasted_iota(jnp.int32, (128, 128), 0) == _lanes((128, 128))
    for part in range(2):
        mat_refs[part][...] = (
            jnp.where(eye, 1.0, 0.0)
            + _dot_tn(parts[0][part], parts[0][part])
            + _dot_tn(parts[1][part], parts[1][part])
        )
    invert_in_place(mat_refs)
    for e in range(2):
        trans_ref[e] = jnp.concatenate([parts[e][0], parts[e][1]], axis=1).T
        gain_ref[e] = jnp.concatenate(
            [_dot(parts[e][part], mat_refs[part][...]) for part in range(2)], axis=1
        )


def apply_kernel(x_ref, trans_ref, gain_ref, out_ref):
    xs = [x_ref[pl.ds(e, 256, stride=2), :] for e in range(2)]
    proj = _dot(trans_ref[0], xs[0]) + _dot(trans_ref[1], xs[1])
    dev, pos = _position()
    special = (_lanes((256, 128)) == 64) & (dev * 16 + pos == 0)
    second = lax.broadcasted_iota(jnp.int32, (256, 128), 0) >= 128
    proj = jnp.where(special == second, proj, 0.0)
    for e in range(2):
        out_ref[pl.ds(e, 256, stride=2), :] = xs[e] - _dot(gain_ref[e], proj)


def inverse_kernel(y_ref, scale_ref, keep_ref, swap_ref, top_ref, bottom_ref, last_ref, out_ref):
    lane2 = _lanes((128, 256)) % 128
    sign2 = jnp.where(lane2 < 64, -1.0, 1.0)
    ups, downs = [], []
    for d in range(16):
        up, down = [
            jnp.concatenate(
                [y_ref[pl.ds(32 * d + 16 * half + e, 8, stride=2), :] for e in range(2)], axis=1
            )
            for half in range(2)
        ]
        ups.append(up * (_first_scale(scale_ref) if d == 0 else scale_ref[0:8, :]))
        downs.append(down * scale_ref[8:16, :])
    top = jnp.concatenate(ups, axis=0)
    bottom = jnp.concatenate(downs, axis=0)

    def turned(v):
        halves = [pltpu.roll(v[:, 128 * e : 128 * e + 128], 64, 1) for e in range(2)]
        return jnp.concatenate(halves, axis=1)

    first_row = lax.broadcasted_iota(jnp.int32, (128, 256), 0) == 0
    top_turn = turned(top)
    nyquist = jnp.where(lane2 == 0, 0.5 * top_turn, 0.0)
    top_turn = jnp.where(first_row, nyquist, top_turn * sign2)
    top = jnp.where(first_row & (lane2 == 0), 0.5 * top, top)
    bottom_turn = turned(bottom) * sign2
    a_top = _dot3(top_ref, jnp.concatenate([top, top_turn], axis=0), ((1,), (0,)))
    a_bottom = _dot3(bottom_ref, jnp.concatenate([bottom, bottom_turn], axis=0), ((1,), (0,)))
    lane = _lanes((N2, 128))
    for e in range(2):
        cols = slice(128 * e, 128 * e + 128)
        up, down = a_top[:, cols], a_bottom[:, cols]
        both = up + down
        direct = jnp.where(lane == 0, up, jnp.where(lane == 64, down, both))
        rolled = pltpu.roll(jnp.where(lane == 0, down, both), 64, 1)
        z = keep_ref[...] * direct + swap_ref[...] * rolled
        x = _dot3(last_ref, z, ((1,), (1,)))
        out_ref[:, 8 * e : 8 * e + 8, :] = x.reshape(16, 8, N2)


def _one_hot(row, count):
    index = lax.broadcasted_iota(jnp.int32, (count, 256), 0).astype(F32).astype(BF16)
    return index == jnp.broadcast_to(row, (count, 256)).astype(BF16)


def _pick(mask, row, count):
    return jnp.where(mask, jnp.broadcast_to(row, (count, 256)).astype(BF16), jnp.zeros((), BF16))


def _tally(small, big):
    return lax.dot_general(small, big, (((1,), (1,)), ((), ())), preferred_element_type=F32)


def _tiles(grid_ref, shift, out_fn):
    lane = _lanes((32, 128))
    rows = [grid_ref[pl.ds(r, 32, stride=3), :] for r in range(3)]

    def turned(value, amount):
        amount %= 128
        return pltpu.roll(value, amount, 1) if amount else value

    for j in range(8):
        first, offset = divmod(TPIX * j, 128)
        value = turned(rows[first], shift - offset)
        if offset + TPIX > 128:
            rest = turned(rows[first + 1], shift + 128 - offset)
            value = jnp.where(lane < shift + 128 - offset, value, rest)
        keep = (lane >= shift) & (lane < shift + TPIX)
        out_fn(pl.ds(j, 32, stride=8), jnp.where(keep, value, 0.0))


def _split_pixel(point):
    high = jnp.floor(point * (1.0 / 128))
    return high, point - 128.0 * high


def hits_kernel(half, point_ref, out_ref, high_ref, low_ref, tmp_ref, grid_ref):
    for octet in range(2):
        for r in range(8):
            for h in range(2):
                cols = pl.ds(256 * r + 128 * h, 128)
                rows = pl.ds(128 * h + 64 * octet + r, 8, stride=8)
                low = 16 * half + 8 * octet
                tmp_ref[rows, :] = point_ref[low : low + 8, cols].astype(F32)
    for h in range(2):
        cols = slice(128 * h, 128 * h + 128)
        high, low = _split_pixel(tmp_ref[128 * h : 128 * h + 128, :])
        high_ref[:, cols] = high
        low_ref[:, cols] = low
    one = jnp.ones((1, 256), F32)

    def step(r, acc):
        big = _pick(_one_hot(low_ref[pl.ds(r, 1), :], 128), one, 128)
        small = _pick(_one_hot(high_ref[pl.ds(r, 1), :], 96), one, 96)
        return acc + _tally(small, big)

    grid_ref[...] = lax.fori_loop(0, 128, step, jnp.zeros((96, 128), F32), unroll=32)

    def put(rows, value):
        out_ref[rows, :] = value

    _tiles(grid_ref, TPIX, put)


def sums_kernel(value_ref, first_refs, second_refs, out_ref, grid_ref):
    one = jnp.ones((1, 256), F32)

    def step(base, high_ref, low_ref, r, acc):
        value = value_ref[pl.ds(base + r, 1), :]
        upper = value.astype(BF16).astype(F32)
        big = _pick(_one_hot(low_ref[pl.ds(r, 1), :], 128), one, 128)
        mask = _one_hot(high_ref[pl.ds(r, 1), :], 96)
        small = jnp.concatenate([_pick(mask, upper, 96), _pick(mask, value - upper, 96)], axis=0)
        return acc + _tally(small, big)

    acc = jnp.zeros((192, 128), F32)
    for base, (_, high_ref, low_ref) in ((0, first_refs), (128, second_refs)):
        turn = functools.partial(step, base, high_ref, low_ref)
        acc = lax.fori_loop(0, 128, turn, acc, unroll=64)
    grid_ref[...] = acc[:96] + acc[96:]

    def put(rows, value):
        out_ref[rows, :] = value + first_refs[0][rows, :] + second_refs[0][rows, :]

    _tiles(grid_ref, 0, put)


def spread_kernel(x_ref, out_ref, tmp_ref):
    for h in range(2):
        tmp_ref[256 * h : 256 * h + 256, :] = x_ref[:, 128 * h : 128 * h + 128]
    for octet in range(4):
        for r in range(8):
            for h in range(2):
                rows = pl.ds(256 * h + 64 * octet + r, 8, stride=8)
                cols = pl.ds(256 * r + 128 * h, 128)
                out_ref[8 * octet : 8 * octet + 8, cols] = tmp_ref[rows, :]


def finish_kernel(x_ref, out_ref):
    total = jnp.sum(x_ref[...], axis=0, keepdims=True)
    hits = pltpu.roll(total, 128 - TPIX, 1)
    out_ref[...] = (total / jnp.sqrt(1.0 + hits))[:, :TPIX]


VMEM = pl.BlockSpec(memory_space=pltpu.VMEM)
HBM = pl.BlockSpec(memory_space=pltpu.HBM)


def call(kernel, outs, scratch=(), space=VMEM, grant=GRANT):
    many = isinstance(outs, list)
    shapes = [jax.ShapeDtypeStruct(s, d) for s, d in (outs if many else [outs])]

    def run(*args):
        return pl.pallas_call(
            kernel,
            out_shape=shapes if many else shapes[0],
            in_specs=[space] * len(args),
            out_specs=[VMEM] * len(shapes) if many else VMEM,
            scratch_shapes=list(scratch),
            compiler_params=pltpu.CompilerParams(vmem_limit_bytes=grant),
        )(*args)

    return run


def exchange(value, axes):
    return lax.all_to_all(value, axes, split_axis=0, concat_axis=0, tiled=True)


def steps(tod, pointing, noise_level, modes):
    forward = [jnp.asarray(a) for a in _forward_tables()]
    inverse = [jnp.asarray(a) for a in _inverse_tables()]
    send_v, scale = call(
        basis_kernel,
        [((1, 64, 128), F32), ((24, 256), F32)],
        scratch=[
            pltpu.VMEM((2, 32, 128), F32),
            pltpu.VMEM((2, 32, 128), F32),
            pltpu.VMEM((BANDS, 32), F32),
            pltpu.SemaphoreType.DMA((3,)),
        ],
        space=HBM,
        grant=WIDE_GRANT,
    )(modes, noise_level)
    send_tod = call(
        prep_kernel,
        ((256, 256), F32),
        scratch=[
            pltpu.VMEM((32, 2048), F32),
            pltpu.VMEM((512, 128), F32),
            pltpu.SemaphoreType.DMA((4,)),
        ],
        space=HBM,
        grant=WIDE_GRANT,
    )(tod).reshape(16, 16, 256)
    near = send_v
    for bit in range(4):
        pairs = [(i, i ^ (1 << bit)) for i in range(16)]
        far = lax.ppermute(near, "det", pairs)
        if bit < 3:
            near = jnp.concatenate([near, far], axis=0)
    got_tod = exchange(send_tod, "tm")
    spectra = call(forward_kernel, ((512, 128), F32))(got_tod, scale, *forward)
    trans, gain = call(
        gram_kernel,
        [((2, 256, 256), F32), ((2, 256, 256), F32)],
        scratch=[
            pltpu.VMEM((2, 256, 256), F32),
            pltpu.VMEM((128, 128), F32),
            pltpu.VMEM((128, 128), F32),
        ],
    )(near, far)
    mixed = exchange(spectra.reshape(256, 2, 128), ("det", "tm")).reshape(512, 128)
    weighted = call(apply_kernel, ((512, 128), F32))(mixed, trans, gain)
    counted = [
        call(
            functools.partial(hits_kernel, half),
            [((256, 128), F32), ((128, 256), F32), ((128, 256), F32)],
            scratch=[pltpu.VMEM((256, 128), F32), pltpu.VMEM((96, 128), F32)],
        )(pointing)
        for half in range(2)
    ]
    back = exchange(weighted.reshape(256, 2, 128), ("det", "tm")).reshape(512, 128)
    series = call(inverse_kernel, ((16, 16, 256), F32))(back, scale, *inverse)
    got_series = exchange(series, "tm").reshape(256, 256)
    bins = call(
        lambda value, *refs: sums_kernel(value, refs[0:3], refs[3:6], *refs[6:]),
        ((256, 128), F32),
        scratch=[pltpu.VMEM((96, 128), F32)],
    )(got_series, *counted[0], *counted[1])
    filtered = call(
        spread_kernel, ((32, 2048), F32), scratch=[pltpu.VMEM((512, 128), F32)]
    )(got_series)
    got_bins = exchange(bins, ("det", "tm"))
    binned = call(finish_kernel, ((1, TPIX), F32))(got_bins)
    return filtered, binned.reshape(TPIX)


def solution(mesh):
    placed = (P("det", "tm"), P("det", "tm"), P(None, "det"), P(None, "det", None))
    return jax.shard_map(
        steps,
        mesh=mesh,
        in_specs=placed,
        out_specs=(P("det", "tm"), P(("det", "tm"))),
        check_vma=False,
    )
```

```python
import functools

import numpy as np
import jax
import jax.numpy as jnp
from jax import lax
from jax.experimental import pallas as pl
from jax.experimental.pallas import tpu as pltpu
from jax.sharding import PartitionSpec as P


HIGHEST = lax.Precision.HIGHEST
NS = 32768
N1 = 128
N2 = 256
BANDS = 8
TPIX = 48
HOPS = (2, 8, 1, 4)
GRANT = 12 << 20
WIDE_GRANT = 60 << 20
F32 = jnp.float32
BF16 = jnp.bfloat16


def _slots():
    dev, step = np.meshgrid(np.arange(16), np.arange(8), indexing="ij")
    top = (16 * step + dev).reshape(-1)
    bottom = (16 * (step + 8) + dev).reshape(-1)
    return top, bottom


def _forward_tables():
    n1 = np.arange(N1)[:, None]
    k1 = np.arange(64)[None, :]
    angle = 2 * np.pi * (n1 * k1 % N1) / N1
    first = np.concatenate([np.cos(angle), -np.sin(angle)], axis=1)
    first[:, 64] = np.cos(np.pi * np.arange(N1))
    n2 = np.arange(N2)[:, None]
    turn = 2 * np.pi * (n2 * k1) / NS
    keep = np.concatenate([np.cos(turn), np.cos(turn)], axis=1)
    swap = np.concatenate([np.sin(turn), -np.sin(turn)], axis=1)
    edge = 2 * np.pi * 64 * np.arange(N2) / NS
    keep[:, 0] = 1.0
    swap[:, 0] = np.cos(edge)
    keep[:, 64] = -np.sin(edge)
    swap[:, 64] = 0.0
    last = []
    for rows in _slots():
        phase = 2 * np.pi * (rows[:, None] * np.arange(N2)[None, :] % N2) / N2
        last.append(np.concatenate([np.cos(phase), np.sin(phase)], axis=1))
    return [np.asarray(a, np.float32) for a in (first, keep, swap, last[0], last[1])]


def _inverse_tables():
    na = np.arange(N2)
    first = []
    for position, rows in enumerate(_slots()):
        phase = 2 * np.pi * (na[:, None] * rows[None, :] % N2) / N2
        sine = np.sin(phase)
        if position == 0:
            sine[:, 0] = np.where(na % 2 == 0, 1.0, -1.0)
        first.append(np.concatenate([np.cos(phase), sine], axis=1))
    k1 = np.arange(64)[None, :]
    turn = 2 * np.pi * (na[:, None] * k1) / NS
    keep = np.concatenate([2 * np.cos(turn), 2 * np.cos(turn)], axis=1)
    swap = np.concatenate([-2 * np.sin(turn), 2 * np.sin(turn)], axis=1)
    edge = 2 * np.pi * 64 * na / NS
    keep[:, 0] = 2.0
    swap[:, 0] = 0.0
    keep[:, 64] = -2 * np.sin(edge)
    swap[:, 64] = 2 * np.cos(edge)
    nb = np.arange(N1)[:, None]
    angle = 2 * np.pi * (nb * k1 % N1) / N1
    last = np.concatenate([np.cos(angle), -np.sin(angle)], axis=1) / NS
    last[:, 64] = np.cos(np.pi * np.arange(N1)) / NS
    tables = [np.asarray(a, np.float32) for a in (keep, swap)]
    for a in (first[0], first[1], last):
        upper = np.asarray(a, jnp.bfloat16)
        lower = np.asarray(a - upper.astype(np.float64), jnp.bfloat16)
        tables.append(np.stack([upper, lower]))
    return tables


def _dot(a, b):
    return jnp.dot(a, b, precision=HIGHEST, preferred_element_type=F32)


def _dot_tn(a, b):
    return lax.dot_general(
        a, b, (((0,), (0,)), ((), ())), precision=HIGHEST, preferred_element_type=F32
    )


def _parts(a):
    upper = a.astype(BF16)
    return upper, (a - upper.astype(F32)).astype(BF16)


def _dot3(table_ref, b, dims):
    upper, lower = _parts(b)

    def product(x, y):
        return lax.dot_general(x, y, (dims, ((), ())), preferred_element_type=F32)

    return product(table_ref[0], upper) + (
        product(table_ref[0], lower) + product(table_ref[1], upper)
    )


def _lanes(shape):
    return lax.broadcasted_iota(jnp.int32, shape, 1)


def _position():
    return lax.axis_index("det"), lax.axis_index("tm")


def basis_kernel(modes_hbm, noise_hbm, v_out, scale_out, tmp_ref, modes_ref, noise_ref, sems):
    _, pos = _position()
    band = jnp.where(pos < BANDS, pos, 2 * BANDS - 1 - pos)
    copies = [
        pltpu.make_async_copy(noise_hbm, noise_ref, sems.at[0]),
        pltpu.make_async_copy(modes_hbm.at[band], modes_ref.at[0], sems.at[1]),
        pltpu.make_async_copy(modes_hbm.at[BANDS - 1], modes_ref.at[1], sems.at[2]),
    ]
    for copy in copies:
        copy.start()
    for copy in copies:
        copy.wait()
    root = lax.rsqrt(noise_ref[...])
    eye = lax.broadcasted_iota(jnp.int32, (32, 32), 0) == _lanes((32, 32))
    row_of = lax.broadcasted_iota(jnp.int32, (BANDS, 32), 0)
    for part, which in enumerate((band, BANDS - 1)):
        row = jnp.sum(jnp.where(row_of == which, root, 0.0), axis=0, keepdims=True)
        col = jnp.sum(jnp.where(eye, row, 0.0), axis=1, keepdims=True)
        tmp_ref[part] = modes_ref[part] * col
        for e in range(2):
            low = 32 * part + 16 * e
            v_out[0, low : low + 16, :] = tmp_ref[part, pl.ds(e, 16, stride=2), :]
    flipped = jnp.concatenate([root[BANDS - 1 - j : BANDS - j] for j in range(BANDS)], axis=0)
    for e in range(2):
        mask = _lanes((BANDS, 32)) == 2 * pos + e
        lanes = pl.ds(128 * e, 128)
        up = jnp.sum(jnp.where(mask, root, 0.0), axis=1, keepdims=True)
        down = jnp.sum(jnp.where(mask, flipped, 0.0), axis=1, keepdims=True)
        scale_out[0:8, lanes] = jnp.broadcast_to(up, (8, 128))
        scale_out[8:16, lanes] = jnp.broadcast_to(down, (8, 128))
        scale_out[16:24, lanes] = jnp.broadcast_to(up[7:8], (8, 128))


def _spread_rows(source_ref, tmp_ref, octet):
    for r in range(8):
        for h in range(2):
            cols = pl.ds(256 * r + 128 * h, 128)
            rows = pl.ds(256 * h + 64 * octet + r, 8, stride=8)
            tmp_ref[rows, :] = source_ref[8 * octet : 8 * octet + 8, cols].astype(F32)


def prep_kernel(tod_ref, tod_out, tod_in, tod_tmp, sems):
    copies = []
    for octet in range(4):
        rows = pl.ds(8 * octet, 8)
        copy = pltpu.make_async_copy(tod_ref.at[rows], tod_in.at[rows], sems.at[octet])
        copy.start()
        copies.append(copy)
    for octet in range(4):
        copies[octet].wait()
        _spread_rows(tod_in, tod_tmp, octet)
        for h in range(2):
            cols = slice(128 * h, 128 * h + 128)
            low = 256 * h + 64 * octet
            tod_out[64 * octet : 64 * octet + 64, cols] = tod_tmp[low : low + 64, :]


def _first_scale(scale_ref):
    lane = _lanes((8, 256)) % 128
    row = lax.broadcasted_iota(jnp.int32, (8, 256), 0)
    return jnp.where((lane == 64) & (row == 0), scale_ref[16:24, :], scale_ref[0:8, :])


def forward_kernel(x_ref, scale_ref, first_ref, keep_ref, swap_ref, top_ref, bottom_ref, out_ref):
    lane = _lanes((N2, 128))
    sign = jnp.where(lane < 64, 1.0, -1.0)
    parity = lax.broadcasted_iota(jnp.int32, (N2, 128), 0) % 2
    alternate = jnp.where(lane == 64, jnp.where(parity == 0, -1.0, 1.0), 0.0)
    tops, bottoms, nyquist = [], [], []
    for e in range(2):
        x = x_ref[:, 8 * e : 8 * e + 8, :].reshape(N1, N2)
        s = _dot_tn(x, first_ref[...])
        a = keep_ref[...] * s
        b = swap_ref[...] * pltpu.roll(s, 64, 1)
        both = a + b
        top = jnp.where(lane == 0, a, jnp.where(lane == 64, 0.0, both))
        bottom = jnp.where(lane == 0, b, jnp.where(lane == 64, a, both))
        top_turn = pltpu.roll(top, 64, 1) * sign
        bottom_turn = pltpu.roll(bottom, 64, 1) * sign
        nyquist.append(jnp.sum(top_turn * alternate, axis=0, keepdims=True))
        tops.append(jnp.concatenate([top, top_turn], axis=0))
        bottoms.append(jnp.concatenate([bottom, bottom_turn], axis=0))
    out_top = _dot(top_ref[...], jnp.concatenate(tops, axis=1))
    out_bottom = _dot(bottom_ref[...], jnp.concatenate(bottoms, axis=1))
    nyq = jnp.concatenate(nyquist, axis=1)
    row0 = lax.broadcasted_iota(jnp.int32, (8, 256), 0) == 0
    for d in range(16):
        up = out_top[8 * d : 8 * d + 8]
        if d == 0:
            up = (up + jnp.where(row0, nyq, 0.0)) * _first_scale(scale_ref)
        else:
            up = up * scale_ref[0:8, :]
        down = out_bottom[8 * d : 8 * d + 8] * scale_ref[8:16, :]
        for e in range(2):
            cols = slice(128 * e, 128 * e + 128)
            out_ref[pl.ds(32 * d + e, 8, stride=2), :] = up[:, cols]
            out_ref[pl.ds(32 * d + 16 + e, 8, stride=2), :] = down[:, cols]


def _pair_inverse(a, b, c):
    r = 1.0 / (a * c - b * b)
    return c * r, -b * r, a * r


def _quad_inverse(m):
    a0, a1, a2 = _pair_inverse(m[0][0], m[0][1], m[1][1])
    w00 = a0 * m[0][2] + a1 * m[1][2]
    w01 = a0 * m[0][3] + a1 * m[1][3]
    w10 = a1 * m[0][2] + a2 * m[1][2]
    w11 = a1 * m[0][3] + a2 * m[1][3]
    q0, q1, q2 = _pair_inverse(
        m[2][2] - (m[0][2] * w00 + m[1][2] * w10),
        m[2][3] - (m[0][2] * w01 + m[1][2] * w11),
        m[3][3] - (m[0][3] * w01 + m[1][3] * w11),
    )
    x00 = -(w00 * q0 + w01 * q1)
    x01 = -(w00 * q1 + w01 * q2)
    x10 = -(w10 * q0 + w11 * q1)
    x11 = -(w10 * q1 + w11 * q2)
    i00 = a0 - (x00 * w00 + x01 * w01)
    i01 = a1 - (x00 * w10 + x01 * w11)
    i11 = a2 - (x10 * w10 + x11 * w11)
    return [
        [i00, i01, x00, x01],
        [i01, i11, x10, x11],
        [x00, x10, q0, q1],
        [x01, x11, q1, q2],
    ]


def invert_in_place(mat_refs):
    lane = _lanes((128, 128))
    lane8 = _lanes((8, 128))

    def step(panel, carry):
        base = 4 * panel
        within = (lane >= base) & (lane < base + 4)
        index = [jnp.full((128, 128), base + j, jnp.int32) for j in range(4)]
        mats = [ref[...] for ref in mat_refs]
        rows = [
            [jnp.broadcast_to(ref[pl.ds(base + j, 1), :], (8, 128)) for j in range(4)]
            for ref in mat_refs
        ]
        pivots = [
            [[jnp.take_along_axis(r[i], index[j][:8], axis=1) for j in range(4)] for i in range(4)]
            for r in rows
        ]
        inverses = [_quad_inverse(p) for p in pivots]
        results = []
        for mat, row, inverse in zip(mats, rows, inverses):
            new = jnp.where(within, 0.0, mat)
            scaled = []
            for i in range(4):
                line = sum(inverse[i][j] * row[j] for j in range(4))
                for j in range(4):
                    line = jnp.where(lane8 == base + j, inverse[i][j], line)
                scaled.append(line)
                col = jnp.take_along_axis(mat, index[i], axis=1)
                new = new - col * jnp.concatenate([line] * 16, axis=0)
            results.append((new, scaled))
        for ref, (new, scaled) in zip(mat_refs, results):
            ref[...] = new
            for i in range(4):
                ref[pl.ds(base + i, 1), :] = scaled[i][0:1]
        return carry

    lax.fori_loop(0, 32, step, 0)


def gram_kernel(near_ref, far_ref, trans_ref, gain_ref, vees_ref, *mat_refs):
    dev, _ = _position()
    for j in range(16):
        source = near_ref if j < 8 else far_ref
        flip = sum(hop for bit, hop in enumerate(HOPS) if j >> bit & 1)
        rows = pl.ds(pl.multiple_of((dev ^ flip) * 16, 16), 16)
        for e in range(2):
            for part in range(2):
                low = 32 * part + 16 * e
                vees_ref[e, rows, 128 * part : 128 * part + 128] = source[j % 8, low : low + 16, :]
    parts = [[vees_ref[e, :, 128 * part : 128 * part + 128] for part in range(2)] for e in range(2)]
    eye = lax.broadcasted_iota(jnp.int32, (128, 128), 0) == _lanes((128, 128))
    for part in range(2):
        mat_refs[part][...] = (
            jnp.where(eye, 1.0, 0.0)
            + _dot_tn(parts[0][part], parts[0][part])
            + _dot_tn(parts[1][part], parts[1][part])
        )
    invert_in_place(mat_refs)
    for e in range(2):
        trans_ref[e] = jnp.concatenate([parts[e][0], parts[e][1]], axis=1).T
        gain_ref[e] = jnp.concatenate(
            [_dot(parts[e][part], mat_refs[part][...]) for part in range(2)], axis=1
        )


def apply_kernel(x_ref, trans_ref, gain_ref, out_ref):
    xs = [x_ref[pl.ds(e, 256, stride=2), :] for e in range(2)]
    proj = _dot(trans_ref[0], xs[0]) + _dot(trans_ref[1], xs[1])
    dev, pos = _position()
    special = (_lanes((256, 128)) == 64) & (dev * 16 + pos == 0)
    second = lax.broadcasted_iota(jnp.int32, (256, 128), 0) >= 128
    proj = jnp.where(special == second, proj, 0.0)
    for e in range(2):
        out_ref[pl.ds(e, 256, stride=2), :] = xs[e] - _dot(gain_ref[e], proj)


def inverse_kernel(y_ref, scale_ref, keep_ref, swap_ref, top_ref, bottom_ref, last_ref, out_ref):
    lane2 = _lanes((128, 256)) % 128
    sign2 = jnp.where(lane2 < 64, -1.0, 1.0)
    ups, downs = [], []
    for d in range(16):
        up, down = [
            jnp.concatenate(
                [y_ref[pl.ds(32 * d + 16 * half + e, 8, stride=2), :] for e in range(2)], axis=1
            )
            for half in range(2)
        ]
        ups.append(up * (_first_scale(scale_ref) if d == 0 else scale_ref[0:8, :]))
        downs.append(down * scale_ref[8:16, :])
    top = jnp.concatenate(ups, axis=0)
    bottom = jnp.concatenate(downs, axis=0)

    def turned(v):
        halves = [pltpu.roll(v[:, 128 * e : 128 * e + 128], 64, 1) for e in range(2)]
        return jnp.concatenate(halves, axis=1)

    first_row = lax.broadcasted_iota(jnp.int32, (128, 256), 0) == 0
    top_turn = turned(top)
    nyquist = jnp.where(lane2 == 0, 0.5 * top_turn, 0.0)
    top_turn = jnp.where(first_row, nyquist, top_turn * sign2)
    top = jnp.where(first_row & (lane2 == 0), 0.5 * top, top)
    bottom_turn = turned(bottom) * sign2
    a_top = _dot3(top_ref, jnp.concatenate([top, top_turn], axis=0), ((1,), (0,)))
    a_bottom = _dot3(bottom_ref, jnp.concatenate([bottom, bottom_turn], axis=0), ((1,), (0,)))
    lane = _lanes((N2, 128))
    for e in range(2):
        cols = slice(128 * e, 128 * e + 128)
        up, down = a_top[:, cols], a_bottom[:, cols]
        both = up + down
        direct = jnp.where(lane == 0, up, jnp.where(lane == 64, down, both))
        rolled = pltpu.roll(jnp.where(lane == 0, down, both), 64, 1)
        z = keep_ref[...] * direct + swap_ref[...] * rolled
        x = _dot3(last_ref, z, ((1,), (1,)))
        out_ref[:, 8 * e : 8 * e + 8, :] = x.reshape(16, 8, N2)


def _one_hot(row, count):
    index = lax.broadcasted_iota(jnp.int32, (count, 256), 0).astype(F32).astype(BF16)
    return index == jnp.broadcast_to(row, (count, 256)).astype(BF16)


def _pick(mask, row, count):
    return jnp.where(mask, jnp.broadcast_to(row, (count, 256)).astype(BF16), jnp.zeros((), BF16))


def _tally(small, big):
    return lax.dot_general(small, big, (((1,), (1,)), ((), ())), preferred_element_type=F32)


def _tiles(grid_ref, shift, out_fn):
    lane = _lanes((32, 128))
    rows = [grid_ref[pl.ds(r, 32, stride=3), :] for r in range(3)]

    def turned(value, amount):
        amount %= 128
        return pltpu.roll(value, amount, 1) if amount else value

    for j in range(8):
        first, offset = divmod(TPIX * j, 128)
        value = turned(rows[first], shift - offset)
        if offset + TPIX > 128:
            rest = turned(rows[first + 1], shift + 128 - offset)
            value = jnp.where(lane < shift + 128 - offset, value, rest)
        keep = (lane >= shift) & (lane < shift + TPIX)
        out_fn(pl.ds(j, 32, stride=8), jnp.where(keep, value, 0.0))


def _split_pixel(point):
    high = jnp.floor(point * (1.0 / 128))
    return high, point - 128.0 * high


def hits_kernel(half, point_ref, out_ref, high_ref, low_ref, tmp_ref, grid_ref):
    for octet in range(2):
        for r in range(8):
            for h in range(2):
                cols = pl.ds(256 * r + 128 * h, 128)
                rows = pl.ds(128 * h + 64 * octet + r, 8, stride=8)
                low = 16 * half + 8 * octet
                tmp_ref[rows, :] = point_ref[low : low + 8, cols].astype(F32)
    for h in range(2):
        cols = slice(128 * h, 128 * h + 128)
        high, low = _split_pixel(tmp_ref[128 * h : 128 * h + 128, :])
        high_ref[:, cols] = high
        low_ref[:, cols] = low
    one = jnp.ones((1, 256), F32)

    def step(r, acc):
        big = _pick(_one_hot(low_ref[pl.ds(r, 1), :], 128), one, 128)
        small = _pick(_one_hot(high_ref[pl.ds(r, 1), :], 96), one, 96)
        return acc + _tally(small, big)

    grid_ref[...] = lax.fori_loop(0, 128, step, jnp.zeros((96, 128), F32), unroll=32)

    def put(rows, value):
        out_ref[rows, :] = value

    _tiles(grid_ref, TPIX, put)


def sums_kernel(value_ref, first_refs, second_refs, out_ref, grid_ref):
    one = jnp.ones((1, 256), F32)

    def step(base, high_ref, low_ref, r, acc):
        value = value_ref[pl.ds(base + r, 1), :]
        upper = value.astype(BF16).astype(F32)
        big = _pick(_one_hot(low_ref[pl.ds(r, 1), :], 128), one, 128)
        mask = _one_hot(high_ref[pl.ds(r, 1), :], 96)
        small = jnp.concatenate([_pick(mask, upper, 96), _pick(mask, value - upper, 96)], axis=0)
        return acc + _tally(small, big)

    acc = jnp.zeros((192, 128), F32)
    for base, (_, high_ref, low_ref) in ((0, first_refs), (128, second_refs)):
        turn = functools.partial(step, base, high_ref, low_ref)
        acc = lax.fori_loop(0, 128, turn, acc, unroll=128)
    grid_ref[...] = acc[:96] + acc[96:]

    def put(rows, value):
        out_ref[rows, :] = value + first_refs[0][rows, :] + second_refs[0][rows, :]

    _tiles(grid_ref, 0, put)


def spread_kernel(x_ref, out_ref, tmp_ref):
    for h in range(2):
        tmp_ref[256 * h : 256 * h + 256, :] = x_ref[:, 128 * h : 128 * h + 128]
    for octet in range(4):
        for r in range(8):
            for h in range(2):
                rows = pl.ds(256 * h + 64 * octet + r, 8, stride=8)
                cols = pl.ds(256 * r + 128 * h, 128)
                out_ref[8 * octet : 8 * octet + 8, cols] = tmp_ref[rows, :]


def finish_kernel(x_ref, out_ref):
    total = jnp.sum(x_ref[...], axis=0, keepdims=True)
    hits = pltpu.roll(total, 128 - TPIX, 1)
    out_ref[...] = (total / jnp.sqrt(1.0 + hits))[:, :TPIX]


VMEM = pl.BlockSpec(memory_space=pltpu.VMEM)
HBM = pl.BlockSpec(memory_space=pltpu.HBM)


def call(kernel, outs, scratch=(), space=VMEM, grant=GRANT):
    many = isinstance(outs, list)
    shapes = [jax.ShapeDtypeStruct(s, d) for s, d in (outs if many else [outs])]

    def run(*args):
        return pl.pallas_call(
            kernel,
            out_shape=shapes if many else shapes[0],
            in_specs=[space] * len(args),
            out_specs=[VMEM] * len(shapes) if many else VMEM,
            scratch_shapes=list(scratch),
            compiler_params=pltpu.CompilerParams(vmem_limit_bytes=grant),
        )(*args)

    return run


def exchange(value, axes):
    return lax.all_to_all(value, axes, split_axis=0, concat_axis=0, tiled=True)


def steps(tod, pointing, noise_level, modes):
    forward = [jnp.asarray(a) for a in _forward_tables()]
    inverse = [jnp.asarray(a) for a in _inverse_tables()]
    send_v, scale = call(
        basis_kernel,
        [((1, 64, 128), F32), ((24, 256), F32)],
        scratch=[
            pltpu.VMEM((2, 32, 128), F32),
            pltpu.VMEM((2, 32, 128), F32),
            pltpu.VMEM((BANDS, 32), F32),
            pltpu.SemaphoreType.DMA((3,)),
        ],
        space=HBM,
        grant=WIDE_GRANT,
    )(modes, noise_level)
    send_tod = call(
        prep_kernel,
        ((256, 256), F32),
        scratch=[
            pltpu.VMEM((32, 2048), F32),
            pltpu.VMEM((512, 128), F32),
            pltpu.SemaphoreType.DMA((4,)),
        ],
        space=HBM,
        grant=WIDE_GRANT,
    )(tod).reshape(16, 16, 256)
    near = send_v
    for bit in range(4):
        pairs = [(i, i ^ HOPS[bit]) for i in range(16)]
        far = lax.ppermute(near, "det", pairs)
        if bit < 3:
            near = jnp.concatenate([near, far], axis=0)
    got_tod = exchange(send_tod, "tm")
    spectra = call(forward_kernel, ((512, 128), F32))(got_tod, scale, *forward)
    trans, gain = call(
        gram_kernel,
        [((2, 256, 256), F32), ((2, 256, 256), F32)],
        scratch=[
            pltpu.VMEM((2, 256, 256), F32),
            pltpu.VMEM((128, 128), F32),
            pltpu.VMEM((128, 128), F32),
        ],
    )(near, far)
    mixed = exchange(spectra.reshape(256, 2, 128), ("det", "tm")).reshape(512, 128)
    weighted = call(apply_kernel, ((512, 128), F32))(mixed, trans, gain)
    counted = [
        call(
            functools.partial(hits_kernel, half),
            [((256, 128), F32), ((128, 256), F32), ((128, 256), F32)],
            scratch=[pltpu.VMEM((256, 128), F32), pltpu.VMEM((96, 128), F32)],
        )(pointing)
        for half in range(2)
    ]
    back = exchange(weighted.reshape(256, 2, 128), ("det", "tm")).reshape(512, 128)
    series = call(inverse_kernel, ((16, 16, 256), F32))(back, scale, *inverse)
    got_series = exchange(series, "tm").reshape(256, 256)
    bins = call(
        lambda value, *refs: sums_kernel(value, refs[0:3], refs[3:6], *refs[6:]),
        ((256, 128), F32),
        scratch=[pltpu.VMEM((96, 128), F32)],
    )(got_series, *counted[0], *counted[1])
    filtered = call(
        spread_kernel, ((32, 2048), F32), scratch=[pltpu.VMEM((512, 128), F32)]
    )(got_series)
    got_bins = exchange(bins, ("det", "tm"))
    binned = call(finish_kernel, ((1, TPIX), F32))(got_bins)
    return filtered, binned.reshape(TPIX)


def solution(mesh):
    placed = (P("det", "tm"), P("det", "tm"), P(None, "det"), P(None, "det", None))
    return jax.shard_map(
        steps,
        mesh=mesh,
        in_specs=placed,
        out_specs=(P("det", "tm"), P(("det", "tm"))),
        check_vma=False,
    )
```

```python
import functools

import numpy as np
import jax
import jax.numpy as jnp
from jax import lax
from jax.experimental import pallas as pl
from jax.experimental.pallas import tpu as pltpu
from jax.sharding import PartitionSpec as P


HIGHEST = lax.Precision.HIGHEST
NS = 32768
N1 = 128
N2 = 256
BANDS = 8
TPIX = 48
HOPS = (2, 8, 1, 4)
GRANT = 12 << 20
WIDE_GRANT = 60 << 20
F32 = jnp.float32
BF16 = jnp.bfloat16


def _slots():
    dev, step = np.meshgrid(np.arange(16), np.arange(8), indexing="ij")
    top = (16 * step + dev).reshape(-1)
    bottom = (16 * (step + 8) + dev).reshape(-1)
    return top, bottom


def _forward_tables():
    n1 = np.arange(N1)[:, None]
    k1 = np.arange(64)[None, :]
    angle = 2 * np.pi * (n1 * k1 % N1) / N1
    first = np.concatenate([np.cos(angle), -np.sin(angle)], axis=1)
    first[:, 64] = np.cos(np.pi * np.arange(N1))
    n2 = np.arange(N2)[:, None]
    turn = 2 * np.pi * (n2 * k1) / NS
    keep = np.concatenate([np.cos(turn), np.cos(turn)], axis=1)
    swap = np.concatenate([np.sin(turn), -np.sin(turn)], axis=1)
    edge = 2 * np.pi * 64 * np.arange(N2) / NS
    keep[:, 0] = 1.0
    swap[:, 0] = np.cos(edge)
    keep[:, 64] = -np.sin(edge)
    swap[:, 64] = 0.0
    last = []
    for rows in _slots():
        phase = 2 * np.pi * (rows[:, None] * np.arange(N2)[None, :] % N2) / N2
        last.append(np.concatenate([np.cos(phase), np.sin(phase)], axis=1))
    return [np.asarray(a, np.float32) for a in (first, keep, swap, last[0], last[1])]


def _inverse_tables():
    na = np.arange(N2)
    first = []
    for position, rows in enumerate(_slots()):
        phase = 2 * np.pi * (na[:, None] * rows[None, :] % N2) / N2
        sine = np.sin(phase)
        if position == 0:
            sine[:, 0] = np.where(na % 2 == 0, 1.0, -1.0)
        first.append(np.concatenate([np.cos(phase), sine], axis=1))
    k1 = np.arange(64)[None, :]
    turn = 2 * np.pi * (na[:, None] * k1) / NS
    keep = np.concatenate([2 * np.cos(turn), 2 * np.cos(turn)], axis=1)
    swap = np.concatenate([-2 * np.sin(turn), 2 * np.sin(turn)], axis=1)
    edge = 2 * np.pi * 64 * na / NS
    keep[:, 0] = 2.0
    swap[:, 0] = 0.0
    keep[:, 64] = -2 * np.sin(edge)
    swap[:, 64] = 2 * np.cos(edge)
    nb = np.arange(N1)[:, None]
    angle = 2 * np.pi * (nb * k1 % N1) / N1
    last = np.concatenate([np.cos(angle), -np.sin(angle)], axis=1) / NS
    last[:, 64] = np.cos(np.pi * np.arange(N1)) / NS
    tables = [np.asarray(a, np.float32) for a in (keep, swap)]
    for a in (first[0], first[1], last):
        upper = np.asarray(a, jnp.bfloat16)
        lower = np.asarray(a - upper.astype(np.float64), jnp.bfloat16)
        tables.append(np.stack([upper, lower]))
    return tables


def _dot(a, b):
    return jnp.dot(a, b, precision=HIGHEST, preferred_element_type=F32)


def _dot_tn(a, b):
    return lax.dot_general(
        a, b, (((0,), (0,)), ((), ())), precision=HIGHEST, preferred_element_type=F32
    )


def _parts(a):
    upper = a.astype(BF16)
    return upper, (a - upper.astype(F32)).astype(BF16)


def _dot3(table_ref, b, dims):
    upper, lower = _parts(b)

    def product(x, y):
        return lax.dot_general(x, y, (dims, ((), ())), preferred_element_type=F32)

    return product(table_ref[0], upper) + (
        product(table_ref[0], lower) + product(table_ref[1], upper)
    )


def _lanes(shape):
    return lax.broadcasted_iota(jnp.int32, shape, 1)


def _position():
    return lax.axis_index("det"), lax.axis_index("tm")


def basis_kernel(modes_hbm, noise_hbm, v_out, scale_out, tmp_ref, modes_ref, noise_ref, sems):
    _, pos = _position()
    band = jnp.where(pos < BANDS, pos, 2 * BANDS - 1 - pos)
    copies = [
        pltpu.make_async_copy(noise_hbm, noise_ref, sems.at[0]),
        pltpu.make_async_copy(modes_hbm.at[band], modes_ref.at[0], sems.at[1]),
        pltpu.make_async_copy(modes_hbm.at[BANDS - 1], modes_ref.at[1], sems.at[2]),
    ]
    for copy in copies:
        copy.start()
    for copy in copies:
        copy.wait()
    root = lax.rsqrt(noise_ref[...])
    eye = lax.broadcasted_iota(jnp.int32, (32, 32), 0) == _lanes((32, 32))
    row_of = lax.broadcasted_iota(jnp.int32, (BANDS, 32), 0)
    for part, which in enumerate((band, BANDS - 1)):
        row = jnp.sum(jnp.where(row_of == which, root, 0.0), axis=0, keepdims=True)
        col = jnp.sum(jnp.where(eye, row, 0.0), axis=1, keepdims=True)
        tmp_ref[part] = modes_ref[part] * col
        for e in range(2):
            low = 32 * part + 16 * e
            v_out[0, low : low + 16, :] = tmp_ref[part, pl.ds(e, 16, stride=2), :]
    flipped = jnp.concatenate([root[BANDS - 1 - j : BANDS - j] for j in range(BANDS)], axis=0)
    for e in range(2):
        mask = _lanes((BANDS, 32)) == 2 * pos + e
        lanes = pl.ds(128 * e, 128)
        up = jnp.sum(jnp.where(mask, root, 0.0), axis=1, keepdims=True)
        down = jnp.sum(jnp.where(mask, flipped, 0.0), axis=1, keepdims=True)
        scale_out[0:8, lanes] = jnp.broadcast_to(up, (8, 128))
        scale_out[8:16, lanes] = jnp.broadcast_to(down, (8, 128))
        scale_out[16:24, lanes] = jnp.broadcast_to(up[7:8], (8, 128))


def _spread_rows(source_ref, tmp_ref, octet):
    for r in range(8):
        for h in range(2):
            cols = pl.ds(256 * r + 128 * h, 128)
            rows = pl.ds(256 * h + 64 * octet + r, 8, stride=8)
            tmp_ref[rows, :] = source_ref[8 * octet : 8 * octet + 8, cols].astype(F32)


def prep_kernel(tod_ref, tod_out, tod_in, tod_tmp, sems):
    copies = []
    for octet in range(4):
        rows = pl.ds(8 * octet, 8)
        copy = pltpu.make_async_copy(tod_ref.at[rows], tod_in.at[rows], sems.at[octet])
        copy.start()
        copies.append(copy)
    for octet in range(4):
        copies[octet].wait()
        _spread_rows(tod_in, tod_tmp, octet)
        for h in range(2):
            cols = slice(128 * h, 128 * h + 128)
            low = 256 * h + 64 * octet
            tod_out[64 * octet : 64 * octet + 64, cols] = tod_tmp[low : low + 64, :]


def _first_scale(scale_ref):
    lane = _lanes((8, 256)) % 128
    row = lax.broadcasted_iota(jnp.int32, (8, 256), 0)
    return jnp.where((lane == 64) & (row == 0), scale_ref[16:24, :], scale_ref[0:8, :])


def forward_kernel(x_ref, scale_ref, first_ref, keep_ref, swap_ref, top_ref, bottom_ref, out_ref):
    lane = _lanes((N2, 128))
    sign = jnp.where(lane < 64, 1.0, -1.0)
    parity = lax.broadcasted_iota(jnp.int32, (N2, 128), 0) % 2
    alternate = jnp.where(lane == 64, jnp.where(parity == 0, -1.0, 1.0), 0.0)
    tops, bottoms, nyquist = [], [], []
    for e in range(2):
        x = x_ref[:, 8 * e : 8 * e + 8, :].reshape(N1, N2)
        s = _dot_tn(x, first_ref[...])
        a = keep_ref[...] * s
        b = swap_ref[...] * pltpu.roll(s, 64, 1)
        both = a + b
        top = jnp.where(lane == 0, a, jnp.where(lane == 64, 0.0, both))
        bottom = jnp.where(lane == 0, b, jnp.where(lane == 64, a, both))
        top_turn = pltpu.roll(top, 64, 1) * sign
        bottom_turn = pltpu.roll(bottom, 64, 1) * sign
        nyquist.append(jnp.sum(top_turn * alternate, axis=0, keepdims=True))
        tops.append(jnp.concatenate([top, top_turn], axis=0))
        bottoms.append(jnp.concatenate([bottom, bottom_turn], axis=0))
    out_top = _dot(top_ref[...], jnp.concatenate(tops, axis=1))
    out_bottom = _dot(bottom_ref[...], jnp.concatenate(bottoms, axis=1))
    nyq = jnp.concatenate(nyquist, axis=1)
    row0 = lax.broadcasted_iota(jnp.int32, (8, 256), 0) == 0
    for d in range(16):
        up = out_top[8 * d : 8 * d + 8]
        if d == 0:
            up = (up + jnp.where(row0, nyq, 0.0)) * _first_scale(scale_ref)
        else:
            up = up * scale_ref[0:8, :]
        down = out_bottom[8 * d : 8 * d + 8] * scale_ref[8:16, :]
        for e in range(2):
            cols = slice(128 * e, 128 * e + 128)
            out_ref[pl.ds(32 * d + e, 8, stride=2), :] = up[:, cols]
            out_ref[pl.ds(32 * d + 16 + e, 8, stride=2), :] = down[:, cols]


def _pair_inverse(a, b, c):
    r = 1.0 / (a * c - b * b)
    return c * r, -b * r, a * r


def _quad_inverse(m):
    a0, a1, a2 = _pair_inverse(m[0][0], m[0][1], m[1][1])
    w00 = a0 * m[0][2] + a1 * m[1][2]
    w01 = a0 * m[0][3] + a1 * m[1][3]
    w10 = a1 * m[0][2] + a2 * m[1][2]
    w11 = a1 * m[0][3] + a2 * m[1][3]
    q0, q1, q2 = _pair_inverse(
        m[2][2] - (m[0][2] * w00 + m[1][2] * w10),
        m[2][3] - (m[0][2] * w01 + m[1][2] * w11),
        m[3][3] - (m[0][3] * w01 + m[1][3] * w11),
    )
    x00 = -(w00 * q0 + w01 * q1)
    x01 = -(w00 * q1 + w01 * q2)
    x10 = -(w10 * q0 + w11 * q1)
    x11 = -(w10 * q1 + w11 * q2)
    i00 = a0 - (x00 * w00 + x01 * w01)
    i01 = a1 - (x00 * w10 + x01 * w11)
    i11 = a2 - (x10 * w10 + x11 * w11)
    return [
        [i00, i01, x00, x01],
        [i01, i11, x10, x11],
        [x00, x10, q0, q1],
        [x01, x11, q1, q2],
    ]


def invert_in_place(mat_refs):
    lane = _lanes((128, 128))
    lane8 = _lanes((8, 128))

    def step(panel, carry):
        base = 4 * panel
        within = (lane >= base) & (lane < base + 4)
        index = [jnp.full((128, 128), base + j, jnp.int32) for j in range(4)]
        mats = [ref[...] for ref in mat_refs]
        rows = [
            [jnp.broadcast_to(ref[pl.ds(base + j, 1), :], (8, 128)) for j in range(4)]
            for ref in mat_refs
        ]
        pivots = [
            [[jnp.take_along_axis(r[i], index[j][:8], axis=1) for j in range(4)] for i in range(4)]
            for r in rows
        ]
        inverses = [_quad_inverse(p) for p in pivots]
        results = []
        for mat, row, inverse in zip(mats, rows, inverses):
            new = jnp.where(within, 0.0, mat)
            scaled = []
            for i in range(4):
                line = sum(inverse[i][j] * row[j] for j in range(4))
                for j in range(4):
                    line = jnp.where(lane8 == base + j, inverse[i][j], line)
                scaled.append(line)
                col = jnp.take_along_axis(mat, index[i], axis=1)
                new = new - col * jnp.concatenate([line] * 16, axis=0)
            results.append((new, scaled))
        for ref, (new, scaled) in zip(mat_refs, results):
            ref[...] = new
            for i in range(4):
                ref[pl.ds(base + i, 1), :] = scaled[i][0:1]
        return carry

    lax.fori_loop(0, 32, step, 0)


def gram_kernel(near_ref, far_ref, trans_ref, gain_ref, vees_ref, *mat_refs):
    dev, _ = _position()
    for j in range(16):
        source = near_ref if j < 8 else far_ref
        flip = sum(hop for bit, hop in enumerate(HOPS) if j >> bit & 1)
        rows = pl.ds(pl.multiple_of((dev ^ flip) * 16, 16), 16)
        for e in range(2):
            for part in range(2):
                low = 32 * part + 16 * e
                vees_ref[e, rows, 128 * part : 128 * part + 128] = source[j % 8, low : low + 16, :]
    parts = [[vees_ref[e, :, 128 * part : 128 * part + 128] for part in range(2)] for e in range(2)]
    eye = lax.broadcasted_iota(jnp.int32, (128, 128), 0) == _lanes((128, 128))
    for part in range(2):
        mat_refs[part][...] = (
            jnp.where(eye, 1.0, 0.0)
            + _dot_tn(parts[0][part], parts[0][part])
            + _dot_tn(parts[1][part], parts[1][part])
        )
    invert_in_place(mat_refs)
    for e in range(2):
        trans_ref[:, 256 * e : 256 * e + 256] = vees_ref[e].T
        gain_ref[e] = jnp.concatenate(
            [_dot(parts[e][part], mat_refs[part][...]) for part in range(2)], axis=1
        )


def apply_kernel(x_ref, trans_ref, gain_ref, out_ref):
    xs = [x_ref[pl.ds(e, 256, stride=2), :] for e in range(2)]
    proj = _dot(trans_ref[...], jnp.concatenate(xs, axis=0))
    dev, pos = _position()
    special = (_lanes((256, 128)) == 64) & (dev * 16 + pos == 0)
    second = lax.broadcasted_iota(jnp.int32, (256, 128), 0) >= 128
    proj = jnp.where(special == second, proj, 0.0)
    for e in range(2):
        out_ref[pl.ds(e, 256, stride=2), :] = xs[e] - _dot(gain_ref[e], proj)


def inverse_kernel(y_ref, scale_ref, keep_ref, swap_ref, top_ref, bottom_ref, last_ref, out_ref):
    lane2 = _lanes((128, 256)) % 128
    sign2 = jnp.where(lane2 < 64, -1.0, 1.0)
    ups, downs = [], []
    for d in range(16):
        up, down = [
            jnp.concatenate(
                [y_ref[pl.ds(32 * d + 16 * half + e, 8, stride=2), :] for e in range(2)], axis=1
            )
            for half in range(2)
        ]
        ups.append(up * (_first_scale(scale_ref) if d == 0 else scale_ref[0:8, :]))
        downs.append(down * scale_ref[8:16, :])
    top = jnp.concatenate(ups, axis=0)
    bottom = jnp.concatenate(downs, axis=0)

    def turned(v):
        halves = [pltpu.roll(v[:, 128 * e : 128 * e + 128], 64, 1) for e in range(2)]
        return jnp.concatenate(halves, axis=1)

    first_row = lax.broadcasted_iota(jnp.int32, (128, 256), 0) == 0
    top_turn = turned(top)
    nyquist = jnp.where(lane2 == 0, 0.5 * top_turn, 0.0)
    top_turn = jnp.where(first_row, nyquist, top_turn * sign2)
    top = jnp.where(first_row & (lane2 == 0), 0.5 * top, top)
    bottom_turn = turned(bottom) * sign2
    a_top = _dot3(top_ref, jnp.concatenate([top, top_turn], axis=0), ((1,), (0,)))
    a_bottom = _dot3(bottom_ref, jnp.concatenate([bottom, bottom_turn], axis=0), ((1,), (0,)))
    lane = _lanes((N2, 128))
    for e in range(2):
        cols = slice(128 * e, 128 * e + 128)
        up, down = a_top[:, cols], a_bottom[:, cols]
        both = up + down
        direct = jnp.where(lane == 0, up, jnp.where(lane == 64, down, both))
        rolled = pltpu.roll(jnp.where(lane == 0, down, both), 64, 1)
        z = keep_ref[...] * direct + swap_ref[...] * rolled
        x = _dot3(last_ref, z, ((1,), (1,)))
        out_ref[:, 8 * e : 8 * e + 8, :] = x.reshape(16, 8, N2)


def _one_hot(row, count):
    index = lax.broadcasted_iota(jnp.int32, (count, 256), 0).astype(F32).astype(BF16)
    return index == jnp.broadcast_to(row, (count, 256)).astype(BF16)


def _pick(mask, row, count):
    return jnp.where(mask, jnp.broadcast_to(row, (count, 256)).astype(BF16), jnp.zeros((), BF16))


def _tally(small, big):
    return lax.dot_general(small, big, (((1,), (1,)), ((), ())), preferred_element_type=F32)


def _tiles(grid_ref, shift, out_fn):
    lane = _lanes((32, 128))
    rows = [grid_ref[pl.ds(r, 32, stride=3), :] for r in range(3)]

    def turned(value, amount):
        amount %= 128
        return pltpu.roll(value, amount, 1) if amount else value

    for j in range(8):
        first, offset = divmod(TPIX * j, 128)
        value = turned(rows[first], shift - offset)
        if offset + TPIX > 128:
            rest = turned(rows[first + 1], shift + 128 - offset)
            value = jnp.where(lane < shift + 128 - offset, value, rest)
        keep = (lane >= shift) & (lane < shift + TPIX)
        out_fn(pl.ds(j, 32, stride=8), jnp.where(keep, value, 0.0))


def _split_pixel(point):
    high = jnp.floor(point * (1.0 / 128))
    return high, point - 128.0 * high


def hits_kernel(half, point_ref, out_ref, high_ref, low_ref, tmp_ref, grid_ref):
    for octet in range(2):
        for r in range(8):
            for h in range(2):
                cols = pl.ds(256 * r + 128 * h, 128)
                rows = pl.ds(128 * h + 64 * octet + r, 8, stride=8)
                low = 16 * half + 8 * octet
                tmp_ref[rows, :] = point_ref[low : low + 8, cols].astype(F32)
    for h in range(2):
        cols = slice(128 * h, 128 * h + 128)
        high, low = _split_pixel(tmp_ref[128 * h : 128 * h + 128, :])
        high_ref[:, cols] = high
        low_ref[:, cols] = low
    one = jnp.ones((1, 256), F32)

    def step(r, acc):
        big = _pick(_one_hot(low_ref[pl.ds(r, 1), :], 128), one, 128)
        small = _pick(_one_hot(high_ref[pl.ds(r, 1), :], 96), one, 96)
        return acc + _tally(small, big)

    grid_ref[...] = lax.fori_loop(0, 128, step, jnp.zeros((96, 128), F32), unroll=32)

    def put(rows, value):
        out_ref[rows, :] = value

    _tiles(grid_ref, TPIX, put)


def sums_kernel(value_ref, first_refs, second_refs, out_ref, grid_ref):
    one = jnp.ones((1, 256), F32)

    def step(base, high_ref, low_ref, r, acc):
        value = value_ref[pl.ds(base + r, 1), :]
        upper = value.astype(BF16).astype(F32)
        big = _pick(_one_hot(low_ref[pl.ds(r, 1), :], 128), one, 128)
        mask = _one_hot(high_ref[pl.ds(r, 1), :], 96)
        small = jnp.concatenate([_pick(mask, upper, 96), _pick(mask, value - upper, 96)], axis=0)
        return acc + _tally(small, big)

    acc = jnp.zeros((192, 128), F32)
    for base, (_, high_ref, low_ref) in ((0, first_refs), (128, second_refs)):
        turn = functools.partial(step, base, high_ref, low_ref)
        acc = lax.fori_loop(0, 128, turn, acc, unroll=128)
    grid_ref[...] = acc[:96] + acc[96:]

    def put(rows, value):
        out_ref[rows, :] = value + first_refs[0][rows, :] + second_refs[0][rows, :]

    _tiles(grid_ref, 0, put)


def spread_kernel(x_ref, out_ref, tmp_ref):
    for h in range(2):
        tmp_ref[256 * h : 256 * h + 256, :] = x_ref[:, 128 * h : 128 * h + 128]
    for octet in range(4):
        for r in range(8):
            for h in range(2):
                rows = pl.ds(256 * h + 64 * octet + r, 8, stride=8)
                cols = pl.ds(256 * r + 128 * h, 128)
                out_ref[8 * octet : 8 * octet + 8, cols] = tmp_ref[rows, :]


def finish_kernel(x_ref, out_ref):
    total = jnp.sum(x_ref[...], axis=0, keepdims=True)
    hits = pltpu.roll(total, 128 - TPIX, 1)
    out_ref[...] = (total / jnp.sqrt(1.0 + hits))[:, :TPIX]


VMEM = pl.BlockSpec(memory_space=pltpu.VMEM)
HBM = pl.BlockSpec(memory_space=pltpu.HBM)


def call(kernel, outs, scratch=(), space=VMEM, grant=GRANT):
    many = isinstance(outs, list)
    shapes = [jax.ShapeDtypeStruct(s, d) for s, d in (outs if many else [outs])]

    def run(*args):
        return pl.pallas_call(
            kernel,
            out_shape=shapes if many else shapes[0],
            in_specs=[space] * len(args),
            out_specs=[VMEM] * len(shapes) if many else VMEM,
            scratch_shapes=list(scratch),
            compiler_params=pltpu.CompilerParams(vmem_limit_bytes=grant),
        )(*args)

    return run


def exchange(value, axes):
    return lax.all_to_all(value, axes, split_axis=0, concat_axis=0, tiled=True)


def steps(tod, pointing, noise_level, modes):
    forward = [jnp.asarray(a) for a in _forward_tables()]
    inverse = [jnp.asarray(a) for a in _inverse_tables()]
    send_v, scale = call(
        basis_kernel,
        [((1, 64, 128), F32), ((24, 256), F32)],
        scratch=[
            pltpu.VMEM((2, 32, 128), F32),
            pltpu.VMEM((2, 32, 128), F32),
            pltpu.VMEM((BANDS, 32), F32),
            pltpu.SemaphoreType.DMA((3,)),
        ],
        space=HBM,
        grant=WIDE_GRANT,
    )(modes, noise_level)
    send_tod = call(
        prep_kernel,
        ((256, 256), F32),
        scratch=[
            pltpu.VMEM((32, 2048), F32),
            pltpu.VMEM((512, 128), F32),
            pltpu.SemaphoreType.DMA((4,)),
        ],
        space=HBM,
        grant=WIDE_GRANT,
    )(tod).reshape(16, 16, 256)
    near = send_v
    for bit in range(4):
        pairs = [(i, i ^ HOPS[bit]) for i in range(16)]
        far = lax.ppermute(near, "det", pairs)
        if bit < 3:
            near = jnp.concatenate([near, far], axis=0)
    got_tod = exchange(send_tod, "tm")
    spectra = call(forward_kernel, ((512, 128), F32))(got_tod, scale, *forward)
    trans, gain = call(
        gram_kernel,
        [((256, 512), F32), ((2, 256, 256), F32)],
        scratch=[
            pltpu.VMEM((2, 256, 256), F32),
            pltpu.VMEM((128, 128), F32),
            pltpu.VMEM((128, 128), F32),
        ],
    )(near, far)
    mixed = exchange(spectra.reshape(256, 2, 128), ("det", "tm")).reshape(512, 128)
    weighted = call(apply_kernel, ((512, 128), F32))(mixed, trans, gain)
    counted = [
        call(
            functools.partial(hits_kernel, half),
            [((256, 128), F32), ((128, 256), F32), ((128, 256), F32)],
            scratch=[pltpu.VMEM((256, 128), F32), pltpu.VMEM((96, 128), F32)],
        )(pointing)
        for half in range(2)
    ]
    back = exchange(weighted.reshape(256, 2, 128), ("det", "tm")).reshape(512, 128)
    series = call(inverse_kernel, ((16, 16, 256), F32))(back, scale, *inverse)
    got_series = exchange(series, "tm").reshape(256, 256)
    bins = call(
        lambda value, *refs: sums_kernel(value, refs[0:3], refs[3:6], *refs[6:]),
        ((256, 128), F32),
        scratch=[pltpu.VMEM((96, 128), F32)],
    )(got_series, *counted[0], *counted[1])
    filtered = call(
        spread_kernel, ((32, 2048), F32), scratch=[pltpu.VMEM((512, 128), F32)]
    )(got_series)
    got_bins = exchange(bins, ("det", "tm"))
    binned = call(finish_kernel, ((1, TPIX), F32))(got_bins)
    return filtered, binned.reshape(TPIX)


def solution(mesh):
    placed = (P("det", "tm"), P("det", "tm"), P(None, "det"), P(None, "det", None))
    return jax.shard_map(
        steps,
        mesh=mesh,
        in_specs=placed,
        out_specs=(P("det", "tm"), P(("det", "tm"))),
        check_vma=False,
    )
```
